32 devices in a mesh: seq: 8 (over z, x), head: 4 (over y, core).
Axes of the slice: x: 2, y: 2, z: 4, core: 2. Of those that a mesh axis runs over, the one named last changes fastest.
Arguments:
- tokens: bfloat16 [2, 4096, 2560], P(None, 'seq'), may hold values from -6 to 6
- gate_weight: bfloat16 [2560, 5120], P(None, 'head'), may hold values from -0.125 to 0.125
- value_weight: bfloat16 [2560, 5120], P(None, 'head'), may hold values from -0.125 to 0.125
- state_weight: bfloat16 [2560, 256], replicated, may hold values from -0.125 to 0.125
- step_weight: bfloat16 [2560, 80], P(None, 'head'), may hold values from -0.125 to 0.125
- value_kernel: float32 [4, 5120], P(None, 'head'), may hold values from -3 to 3
- value_offset: float32 [5120], P('head'), may hold values from -3 to 3
- state_kernel: float32 [4, 256], replicated, may hold values from -3 to 3
- state_offset: float32 [256], replicated, may hold values from -3 to 3
- step_offset: float32 [80], P('head'), may hold values from -2 to 0.5
- decay_rate: float32 [80], P('head'), may hold values from 0.00024414062 to 0.1
- skip_gain: float32 [80], P('head'), may hold values from 0.5 to 2
- norm_gain: float32 [5120], P('head'), may hold values from 0.5 to 1.5
Outputs:
- normed: bfloat16 [2, 4096, 5120], P(None, 'seq', 'head')
The draws below stay inside these ranges and needn't reach their ends.
All inputs are finite; a program needn't handle non-finite values.
Results may differ from the reference program's by a relative error of at most 0.0054.
Values may be sent and summed in bfloat16 or wider, within the bound.
No kernel may reach another device: no remote copies, remote signals or barrier semaphores. Data moves between devices by JAX's collectives and lax.ppermute only.
A program may use at most 128 MiB of HBM per device.

```python
import math
import jax
import jax.numpy as jnp
from jax import lax

D = 2560
HEADS = 80
HEAD_DIM = 64
STATE = 128
WIDTH = 4
GROUP = 256
BATCH = 2
SEQLEN = 4096
INNER = 5120


def steps_of(stream_key, shape, shards, least, top_value):
    loudness, own = 1.0, jax.random.fold_in(stream_key, 6)
    for position, parts in shards:
        heights = jnp.exp(jax.random.uniform(jax.random.fold_in(own, position), (parts,), jnp.float32, least / len(shards), top_value / len(shards)))
        loudness = loudness * jnp.repeat(heights, shape[position] // parts).reshape([-1 if axis == position else 1 for axis in range(len(shape))])
    return loudness


def scatter_about(stream_key, shape, scale, reach, pieces=(), kind=jnp.bfloat16):
    drawn = scale * jax.random.normal(stream_key, shape, jnp.float32)
    if pieces:
        drawn = drawn * steps_of(stream_key, shape, pieces, -0.22, 0.18)
    return jnp.clip(drawn, -reach, reach).astype(kind)


def setup_inputs(seed: int = 0) -> dict:
    arg_keys = jax.random.split(jax.random.key(seed), 14)
    tokens = scatter_about(arg_keys[0], (BATCH, SEQLEN, D), 1.0, 6.0, ((1, 8),))
    gate_weight = scatter_about(arg_keys[1], (D, INNER), D ** -0.5, 0.125, ((1, 4),))
    value_weight = scatter_about(arg_keys[2], (D, INNER), D ** -0.5, 0.125, ((1, 4),))
    state_weight = scatter_about(arg_keys[3], (D, 2 * STATE), D ** -0.5, 0.125)
    step_weight = scatter_about(arg_keys[4], (D, HEADS), D ** -0.5, 0.125, ((1, 4),))
    value_kernel = scatter_about(arg_keys[5], (WIDTH, INNER), WIDTH ** -0.5, 3.0, ((1, 4),), jnp.float32)
    value_offset = scatter_about(arg_keys[6], (INNER,), 0.5, 3.0, ((0, 4),), jnp.float32)
    state_kernel = scatter_about(arg_keys[7], (WIDTH, 2 * STATE), WIDTH ** -0.5, 3.0, (), jnp.float32)
    state_offset = scatter_about(arg_keys[8], (2 * STATE,), 0.5, 3.0, (), jnp.float32)
    step_offset = jnp.clip(-2.0 + 2.5 * jax.random.uniform(arg_keys[9], (HEADS,), jnp.float32) ** steps_of(arg_keys[9], (HEADS,), ((0, 4),), -0.2, 0.2), -2.0, 0.5)
    decay_rate = jnp.clip(jnp.exp(math.log(0.1) - 6.015181 * jax.random.uniform(arg_keys[10], (HEADS,), jnp.float32) ** steps_of(arg_keys[10], (HEADS,), ((0, 4),), -0.2, 0.2)), 0.00024414062, 0.1)
    skip_gain = jnp.clip(0.5 + 1.5 * jax.random.uniform(arg_keys[11], (HEADS,), jnp.float32) ** steps_of(arg_keys[11], (HEADS,), ((0, 4),), -0.2, 0.2), 0.5, 2.0)
    norm_gain = jnp.clip(1.0 + 0.1 * jax.random.normal(arg_keys[12], (INNER,), jnp.float32), 0.5, 1.5)
    return dict(tokens=tokens, gate_weight=gate_weight, value_weight=value_weight, state_weight=state_weight, step_weight=step_weight, value_kernel=value_kernel, value_offset=value_offset, state_kernel=state_kernel, state_offset=state_offset, step_offset=step_offset, decay_rate=decay_rate, skip_gain=skip_gain, norm_gain=norm_gain)


EPS = 1e-05

def conv_rows(previous, incoming, kernel, offset):
    joined = jnp.concatenate([previous, incoming], axis=-2).astype(jnp.float32)
    length = incoming.shape[-2]
    axis_pos = joined.ndim - 2
    summed = offset + kernel[0] * lax.slice_in_dim(joined, 0, length, axis=axis_pos)
    for tap_index in range(1, kernel.shape[0]):
        summed = summed + kernel[tap_index] * lax.slice_in_dim(joined, tap_index, tap_index + length, axis=axis_pos)
    return jax.nn.silu(summed).astype(jnp.bfloat16)

def group_core(values, b_rows, c_rows, step_sizes, decay_rate):
    log_decay = -step_sizes * decay_rate
    cumulative = jnp.cumsum(log_decay, axis=0)
    length = step_sizes.shape[0]
    causal = (jnp.arange(length)[:, None] >= jnp.arange(length)[None, :])[:, :, None]
    scores = jnp.dot(c_rows, b_rows.T, preferred_element_type=jnp.float32)
    spread = jnp.where(causal, cumulative[:, None, :] - cumulative[None, :, :], 0.0)
    mixing = jnp.where(causal, scores[:, :, None] * jnp.exp(spread) * step_sizes[None, :, :], 0.0).astype(jnp.bfloat16)
    within = jnp.einsum('tsh,shp->thp', mixing.astype(jnp.float32), values.astype(jnp.float32))
    closing = jnp.exp(cumulative[-1][None, :] - cumulative) * step_sizes
    weighted = (closing[:, :, None] * b_rows.astype(jnp.float32)[:, None, :]).astype(jnp.bfloat16)
    produced = jnp.einsum('shp,shn->hpn', values.astype(jnp.float32), weighted.astype(jnp.float32))
    return (within, produced, jnp.exp(cumulative[-1]), jnp.exp(cumulative))

def reference(tokens, gate_weight, value_weight, state_weight, step_weight, value_kernel, value_offset, state_kernel, state_offset, step_offset, decay_rate, skip_gain, norm_gain):
    rim_rows = WIDTH - 1

    def advance(carried_in, token_block):
        memory, value_tail, inout_tail = carried_in
        gate_part = jnp.dot(token_block, gate_weight, preferred_element_type=jnp.float32).astype(jnp.bfloat16)
        values = jnp.dot(token_block, value_weight, preferred_element_type=jnp.float32).astype(jnp.bfloat16)
        inout_rows = jnp.dot(token_block, state_weight, preferred_element_type=jnp.float32).astype(jnp.bfloat16)
        step_sizes = jax.nn.softplus(jnp.dot(token_block, step_weight, preferred_element_type=jnp.float32) + step_offset)
        value_conv = conv_rows(value_tail, values, value_kernel, value_offset)
        inout_conv = conv_rows(inout_tail, inout_rows, state_kernel, state_offset)
        b_rows = inout_conv[:, :STATE]
        c_rows = inout_conv[:, STATE:]
        heads_view = value_conv.reshape(GROUP, HEADS, HEAD_DIM)
        within, produced, through, inside = group_core(heads_view, b_rows, c_rows, step_sizes, decay_rate)
        carried = jnp.einsum('tn,hpn->thp', c_rows.astype(jnp.float32), memory, precision=lax.Precision.HIGHEST)
        mixture = within + inside[:, :, None] * carried + skip_gain[None, :, None] * heads_view.astype(jnp.float32)
        gated_rows = mixture.reshape(GROUP, INNER) * jax.nn.silu(gate_part.astype(jnp.float32))
        inverse = lax.rsqrt(lax.optimization_barrier(jnp.mean(gated_rows * gated_rows, axis=-1, keepdims=True)) + EPS)
        output = (gated_rows * inverse * norm_gain).astype(jnp.bfloat16)
        memory = through[:, None, None] * memory + produced
        return ((memory, values[GROUP - rim_rows:], inout_rows[GROUP - rim_rows:]), output)

    def one_sequence(sequence_rows):
        blocks = sequence_rows.reshape(SEQLEN // GROUP, GROUP, D)
        initial = (jnp.zeros((HEADS, HEAD_DIM, STATE), jnp.float32), jnp.zeros((rim_rows, INNER), jnp.bfloat16), jnp.zeros((rim_rows, 2 * STATE), jnp.bfloat16))
        final_state, outputs = lax.scan(advance, initial, blocks)
        return outputs.reshape(SEQLEN, INNER)
    return lax.map(one_sequence, tokens)
```

```python
import functools
import jax
import jax.numpy as jnp
from jax import lax
from jax.experimental import pallas as pl
from jax.experimental.pallas import tpu as pltpu
from jax.sharding import PartitionSpec as P

EPS = 1e-05
LOG2E = 1.4426950408889634
PAD = 16
CHUNK = 128
TILE = 256
F32 = jnp.float32
BF16 = jnp.bfloat16


def mm(a, b):
    return jnp.dot(a, b, preferred_element_type=F32)


def halves(x):
    hi = x.astype(BF16)
    return hi, (x - hi.astype(F32)).astype(BF16)


def silu(x):
    return x * (1.0 / (1.0 + jnp.exp(-x)))


def spread(x, select):
    hi, lo = halves(x)
    return mm(hi, select) + mm(lo, select)


def head_select(heads, width, head_width, first_head):
    row = lax.broadcasted_iota(jnp.int32, (heads, width), 0)
    col = lax.broadcasted_iota(jnp.int32, (heads, width), 1)
    start = (row - first_head) * head_width
    return jnp.where((col >= start) & (col < start + head_width), 1.0, 0.0).astype(BF16)


def conv_of(ref, rows, kernel, offset):
    taps = kernel.shape[0]
    total = offset
    for k in range(taps):
        total = total + kernel[k : k + 1, :] * ref[pl.ds(PAD - taps + 1 + k, rows), :]
    return silu(total).astype(BF16)


def front_kernel(tok, sw, tw, toff, rate, io_out, dt_out, cum_out, cumt_out, dtt_out):
    x = tok[0]
    rows = x.shape[0]
    io_out[0] = mm(x, sw[...]).astype(BF16)
    z = mm(x, tw[...]) + toff[...]
    dt = jnp.maximum(z, 0.0) + jnp.log1p(jnp.exp(-jnp.abs(z)))
    dt_out[0] = dt
    log_decay = dt * (rate[...] * (-LOG2E))
    r = lax.broadcasted_iota(jnp.int32, (CHUNK, CHUNK), 0)
    c = lax.broadcasted_iota(jnp.int32, (CHUNK, CHUNK), 1)
    tri = jnp.where(r >= c, 1.0, 0.0).astype(BF16)
    for q in range(rows // CHUNK):
        part = log_decay[q * CHUNK : (q + 1) * CHUNK]
        hi = part.astype(BF16)
        rest = part - hi.astype(F32)
        mid = rest.astype(BF16)
        low = (rest - mid.astype(F32)).astype(BF16)
        cum = mm(tri, hi) + (mm(tri, mid) + mm(tri, low))
        cum_out[0, pl.ds(q * CHUNK, CHUNK), :] = cum
        cumt_out[0, q] = cum.T
        dtt_out[0, q] = dt[q * CHUNK : (q + 1) * CHUNK].T


def front(tokens, state_weight, step_weight, step_offset, decay_rate):
    b, t, d = tokens.shape
    n2, h = state_weight.shape[1], step_weight.shape[1]
    rows = min(t, 256)
    nc = rows // CHUNK
    return pl.pallas_call(
        front_kernel,
        grid=(b, t // rows),
        in_specs=[
            pl.BlockSpec((1, rows, d), lambda i, j: (i, j, 0)),
            pl.BlockSpec((d, n2), lambda i, j: (0, 0)),
            pl.BlockSpec((d, h), lambda i, j: (0, 0)),
            pl.BlockSpec((1, h), lambda i, j: (0, 0)),
            pl.BlockSpec((1, h), lambda i, j: (0, 0)),
        ],
        out_specs=[
            pl.BlockSpec((1, rows, n2), lambda i, j: (i, j, 0)),
            pl.BlockSpec((1, rows, h), lambda i, j: (i, j, 0)),
            pl.BlockSpec((1, rows, h), lambda i, j: (i, j, 0)),
            pl.BlockSpec((1, nc, h, CHUNK), lambda i, j: (i, j, 0, 0)),
            pl.BlockSpec((1, nc, h, CHUNK), lambda i, j: (i, j, 0, 0)),
        ],
        out_shape=[
            jax.ShapeDtypeStruct((b, t, n2), BF16),
            jax.ShapeDtypeStruct((b, t, h), F32),
            jax.ShapeDtypeStruct((b, t, h), F32),
            jax.ShapeDtypeStruct((b, t // CHUNK, h, CHUNK), F32),
            jax.ShapeDtypeStruct((b, t // CHUNK, h, CHUNK), F32),
        ],
        name="front",
        cost_estimate=pl.CostEstimate(
            flops=2 * b * t * d * (n2 + h), transcendentals=0, bytes_accessed=2 * b * t * d
        ),
    )(tokens, state_weight, step_weight, step_offset, decay_rate)


def maps_kernel(io, halo, sw, kern, off, bt_out, b_out, c_out, buf):
    rows = io.shape[1]
    n = sw.shape[1] // 2
    buf[pl.ds(0, PAD), :] = mm(halo[0], sw[...]).astype(BF16).astype(F32)
    buf[pl.ds(PAD, rows), :] = io[0].astype(F32)
    y = conv_of(buf, rows, kern[...], off[...])
    b_out[0] = y[:, :n]
    c_out[0] = y[:, n:]
    bt_out[0] = y[:, :n].astype(F32).T.astype(BF16)


def maps(io, halo, state_weight, kernel, offset):
    b, t, n2 = io.shape
    d = halo.shape[2]
    n = n2 // 2
    return pl.pallas_call(
        maps_kernel,
        grid=(b,),
        in_specs=[
            pl.BlockSpec((1, t, n2), lambda i: (i, 0, 0)),
            pl.BlockSpec((1, PAD, d), lambda i: (i, 0, 0)),
            pl.BlockSpec((d, n2), lambda i: (0, 0)),
            pl.BlockSpec(kernel.shape, lambda i: (0, 0)),
            pl.BlockSpec((1, n2), lambda i: (0, 0)),
        ],
        out_specs=[
            pl.BlockSpec((1, n, t), lambda i: (i, 0, 0)),
            pl.BlockSpec((1, t, n), lambda i: (i, 0, 0)),
            pl.BlockSpec((1, t, n), lambda i: (i, 0, 0)),
        ],
        out_shape=[
            jax.ShapeDtypeStruct((b, n, t), BF16),
            jax.ShapeDtypeStruct((b, t, n), BF16),
            jax.ShapeDtypeStruct((b, t, n), BF16),
        ],
        scratch_shapes=[pltpu.VMEM((t + PAD, n2), F32)],
        name="maps",
    )(io, halo, state_weight, kernel, offset)


def values_kernel(
    share, first, head_width, tok, halo, w, kern, off, bt, dt, cum,
    vc_out, mid_out, end_out, ext, vbuf, sem,
):
    j = pl.program_id(0)
    b, t, h = dt.shape
    width = w.shape[1]
    n = bt.shape[1]
    chunks = t // CHUNK
    copies = []
    for i in range(b):
        copies.append(pltpu.make_async_copy(halo.at[i], ext.at[i, pl.ds(0, PAD)], sem.at[i, 0]))
        copies.append(pltpu.make_async_copy(tok.at[i], ext.at[i, pl.ds(PAD, t)], sem.at[i, 1]))

    @pl.when(j == 0)
    def _():
        for copy in copies:
            copy.start()
        for copy in copies:
            copy.wait()

    per = width // head_width
    select = head_select(h, width, head_width, (first + j) * per)
    for i in range(b):
        vbuf[i] = mm(ext[i], w[...]).astype(BF16).astype(F32)
        vc = conv_of(vbuf.at[i], t, kern[...], off[...])
        vc_out[i] = vc
        state = jnp.zeros((n, width), F32)
        sums = cum[i]
        last = jnp.concatenate(
            [sums[(q + 1) * CHUNK - 1 : (q + 1) * CHUNK] for q in range(chunks)], axis=0
        )
        through = spread(jnp.exp2(last), select)
        for q in range(chunks):
            span = slice(q * CHUNK, (q + 1) * CHUNK)
            closing = jnp.exp2(last[q : q + 1] - sums[span]) * dt[i, span]
            scaled = (vc[span].astype(F32) * spread(closing, select)).astype(BF16)
            made = mm(bt[i, :, span], scaled)
            if q == 0:
                state = made
            else:
                mid_out[i, q - 1] = state.astype(BF16)
                state = state * through[q : q + 1] + made
        at = i * (end_out.shape[1] // b)
        at = pl.multiple_of(at + j * width, 128)
        end_out[:, pl.ds(at, width)] = state.astype(BF16)


def values(tokens, halo, weight, kernel, offset, bt, dt, cum, share, head_width, first, count):
    b, t, d = tokens.shape
    inner, h, n = weight.shape[1], dt.shape[2], bt.shape[1]
    width = TILE
    chunks = t // CHUNK
    cols = count * width
    return pl.pallas_call(
        functools.partial(values_kernel, share, first, head_width),
        grid=(count,),
        in_specs=[
            pl.BlockSpec(memory_space=pl.ANY),
            pl.BlockSpec(memory_space=pl.ANY),
            pl.BlockSpec((d, width), lambda j: (0, j + first)),
            pl.BlockSpec((kernel.shape[0], width), lambda j: (0, j + first)),
            pl.BlockSpec((1, width), lambda j: (0, j + first)),
            pl.BlockSpec((b, n, t), lambda j: (0, 0, 0)),
            pl.BlockSpec((b, t, h), lambda j: (0, 0, 0)),
            pl.BlockSpec((b, t, h), lambda j: (0, 0, 0)),
        ],
        out_specs=[
            pl.BlockSpec((b, t, width), lambda j: (0, 0, j)),
            pl.BlockSpec((b, chunks - 1, n, width), lambda j: (0, 0, 0, j)),
            pl.BlockSpec((n, b * cols), lambda j: (0, 0)),
        ],
        out_shape=[
            jax.ShapeDtypeStruct((b, t, cols), BF16),
            jax.ShapeDtypeStruct((b, chunks - 1, n, cols), BF16),
            jax.ShapeDtypeStruct((n, b * cols), BF16),
        ],
        scratch_shapes=[
            pltpu.VMEM((b, t + PAD, d), BF16),
            pltpu.VMEM((b, t + PAD, width), F32),
            pltpu.SemaphoreType.DMA((b, 2)),
        ],
        name="values",
        cost_estimate=pl.CostEstimate(
            flops=2 * b * t * d * cols, transcendentals=0, bytes_accessed=2 * d * cols
        ),
    )(tokens, halo, weight, kernel, offset, bt, dt, cum)


def gate_kernel(tok, w, out):
    for i in range(tok.shape[0]):
        out[i] = mm(tok[i], w[...]).astype(BF16)


def gate(tokens, weight):
    b, t, d = tokens.shape
    inner = weight.shape[1]
    return pl.pallas_call(
        gate_kernel,
        grid=(inner // TILE,),
        in_specs=[
            pl.BlockSpec((b, t, d), lambda j: (0, 0, 0), pipeline_mode=pl.Buffered(1)),
            pl.BlockSpec((d, TILE), lambda j: (0, j)),
        ],
        out_specs=pl.BlockSpec((b, t, TILE), lambda j: (0, 0, j)),
        out_shape=jax.ShapeDtypeStruct((b, t, inner), BF16),
        name="gate",
        cost_estimate=pl.CostEstimate(
            flops=2 * b * t * d * inner, transcendentals=0, bytes_accessed=2 * d * inner
        ),
    )(tokens, weight)


def inside_kernel(
    head_width, b_rows, c_rows, vc, mid, dtt, cum, cumt, base, skip, gate_rows, part_out, grow_out
):
    q = pl.program_id(1)
    h = cum.shape[2]
    width = vc.shape[2]
    crow = c_rows[0]
    r = lax.broadcasted_iota(jnp.int32, (CHUNK, CHUNK), 0)
    s = lax.broadcasted_iota(jnp.int32, (CHUNK, CHUNK), 1)
    scores = lax.dot_general(
        crow, b_rows[0], (((1,), (1,)), ((), ())), preferred_element_type=F32
    )
    scores = jnp.where(r >= s, scores, 0.0)
    sums = cum[0]
    select = head_select(h, width, head_width, 0)
    rise = spread(jnp.exp2(sums), select)
    lane = lax.broadcasted_iota(jnp.int32, (CHUNK, 2 * head_width), 1)
    carried = mm(crow, mid[0, 0]) * jnp.where(q > 0, 1.0, 0.0)
    silu_gate = silu(gate_rows[0].astype(F32))
    grow_out[0] = (silu_gate * spread(jnp.exp2(sums + base[0, 0]), select)).astype(BF16)
    for pair in range(h // 2):
        at = slice(pair * 2 * head_width, (pair + 1) * 2 * head_width)
        rows = vc[0, :, at]
        mixes = []
        parts = []
        for k in range(2):
            head = 2 * pair + k
            gap = jnp.minimum(sums[:, head : head + 1] - cumt[0, 0, head : head + 1, :], 0.0)
            mixes.append((scores * jnp.exp2(gap) * dtt[0, 0, head : head + 1, :]).astype(BF16))
            parts.append(jnp.where((lane >= head_width) == (k == 1), rows, jnp.zeros_like(rows)))
        within = mm(jnp.concatenate(mixes, axis=1), jnp.concatenate(parts, axis=0))
        mixture = within + rise[:, at] * carried[:, at] + skip[:, at] * rows.astype(F32)
        part_out[0, :, at] = mixture * silu_gate[:, at]


def inside(b_rows, c_rows, vc, mid, dtt, cum, cumt, base, skip, gate_rows, head_width):
    b, t, n = b_rows.shape
    inner, h = vc.shape[2], cum.shape[2]
    return pl.pallas_call(
        functools.partial(inside_kernel, head_width),
        grid=(b, t // CHUNK),
        in_specs=[
            pl.BlockSpec((1, CHUNK, n), lambda i, q: (i, q, 0)),
            pl.BlockSpec((1, CHUNK, n), lambda i, q: (i, q, 0)),
            pl.BlockSpec((1, CHUNK, inner), lambda i, q: (i, q, 0)),
            pl.BlockSpec((1, 1, n, inner), lambda i, q: (i, jnp.maximum(q - 1, 0), 0, 0)),
            pl.BlockSpec((1, 1, h, CHUNK), lambda i, q: (i, q, 0, 0)),
            pl.BlockSpec((1, CHUNK, h), lambda i, q: (i, q, 0)),
            pl.BlockSpec((1, 1, h, CHUNK), lambda i, q: (i, q, 0, 0)),
            pl.BlockSpec((1, 1, 1, h), lambda i, q: (i, q, 0, 0)),
            pl.BlockSpec((1, inner), lambda i, q: (0, 0)),
            pl.BlockSpec((1, CHUNK, inner), lambda i, q: (i, q, 0)),
        ],
        out_specs=[
            pl.BlockSpec((1, CHUNK, inner), lambda i, q: (i, q, 0)),
            pl.BlockSpec((1, CHUNK, inner), lambda i, q: (i, q, 0)),
        ],
        out_shape=[
            jax.ShapeDtypeStruct((b, t, inner), F32),
            jax.ShapeDtypeStruct((b, t, inner), BF16),
        ],
        name="inside",
        cost_estimate=pl.CostEstimate(
            flops=12 * b * t * CHUNK * inner, transcendentals=b * t * CHUNK * h, bytes_accessed=12 * b * t * inner
        ),
    )(b_rows, c_rows, vc, mid, dtt, cum, cumt, base, skip, gate_rows)


def prefix_kernel(came, logs, out):
    peers = came.shape[0]
    through = jnp.exp2(logs[...])
    state = jnp.zeros(came.shape[1:], F32)
    for i in range(peers):
        out[i] = state.astype(BF16)
        if i + 1 < peers:
            state = state * through[i : i + 1] + came[i].astype(F32)


def prefix(came, logs):
    return pl.pallas_call(
        prefix_kernel,
        out_shape=jax.ShapeDtypeStruct(came.shape, BF16),
        name="prefix",
    )(came, logs)


def enter_kernel(part, grow, c_rows, state, out, sq_out):
    total = part[0] + grow[0].astype(F32) * mm(c_rows[0], state[...])
    out[0] = total
    sq = total * total
    acc = sq[:, :128]
    for k in range(1, sq.shape[1] // 128):
        acc = acc + sq[:, k * 128 : (k + 1) * 128]
    sq_out[...] = jnp.sum(acc.T, axis=0, keepdims=True)


def enter(part, grow, c_rows, state, rows=256):
    b, t, inner = part.shape
    n = c_rows.shape[2]
    per = t // rows
    return pl.pallas_call(
        enter_kernel,
        grid=(b, per),
        in_specs=[
            pl.BlockSpec((1, rows, inner), lambda i, q: (i, q, 0)),
            pl.BlockSpec((1, rows, inner), lambda i, q: (i, q, 0)),
            pl.BlockSpec((1, rows, n), lambda i, q: (i, q, 0)),
            pl.BlockSpec((n, inner), lambda i, q: (0, i)),
        ],
        out_specs=[
            pl.BlockSpec((1, rows, inner), lambda i, q: (i, q, 0)),
            pl.BlockSpec((1, rows), lambda i, q: (0, i * per + q)),
        ],
        out_shape=[
            jax.ShapeDtypeStruct((b, t, inner), F32),
            jax.ShapeDtypeStruct((1, b * t), F32),
        ],
        name="enter",
    )(part, grow, c_rows, state)


def norm_kernel(inner_all, count, *refs):
    squares = refs[:count]
    x, gain, out = refs[count:]
    total = squares[0][...]
    for ref in squares[1:]:
        total = total + ref[...]
    inverse = lax.rsqrt(total / inner_all + EPS)
    rows = x.shape[1]
    columns = jnp.broadcast_to(inverse, (128, rows)).T
    for k in range(x.shape[2] // 128):
        at = slice(k * 128, (k + 1) * 128)
        out[0, :, at] = (x[0, :, at] * columns * gain[:, at]).astype(BF16)


def norm(x, squares, gain, inner_all, rows=256):
    b, t, inner = x.shape
    per = t // rows
    return pl.pallas_call(
        functools.partial(norm_kernel, inner_all, len(squares)),
        grid=(b, per),
        in_specs=[pl.BlockSpec((1, rows), lambda i, q: (0, i * per + q)) for _ in squares]
        + [
            pl.BlockSpec((1, rows, inner), lambda i, q: (i, q, 0)),
            pl.BlockSpec((1, inner), lambda i, q: (0, 0)),
        ],
        out_specs=pl.BlockSpec((1, rows, inner), lambda i, q: (i, q, 0)),
        out_shape=jax.ShapeDtypeStruct((b, t, inner), BF16),
        name="norm",
    )(*squares, x, gain)


def local(
    tokens,
    gate_weight,
    value_weight,
    state_weight,
    step_weight,
    value_kernel,
    value_offset,
    state_kernel,
    state_offset,
    step_offset,
    decay_rate,
    skip_gain,
    norm_gain,
):
    b, t, d = tokens.shape
    inner = gate_weight.shape[1]
    h = step_weight.shape[1]
    head_width = inner // h
    peers = lax.axis_size("seq")
    ranks = lax.axis_size("head")
    chunks = t // CHUNK
    halo = lax.ppermute(tokens[:, t - PAD :], "seq", [(i, i + 1) for i in range(peers - 1)])
    io, dt, cum, cumt, dtt = front(
        tokens, state_weight, step_weight, step_offset[None], decay_rate[None]
    )
    last = cum[:, CHUNK - 1 :: CHUNK]
    running = jnp.cumsum(last, axis=1)
    base = (running - last)[:, :, None, :]
    log_total = jnp.repeat(running[:, -1], head_width, axis=1).reshape(1, b * inner)
    logs = lax.all_gather(log_total, "seq", axis=0, tiled=True)
    bt, b_rows, c_rows = maps(io, halo, state_weight, state_kernel, state_offset[None])
    vc, mid, end = values(
        tokens, halo, value_weight, value_kernel, value_offset[None], bt, dt, cum,
        None, head_width, 0, inner // TILE,
    )
    n = end.shape[0]
    came = lax.all_to_all(
        end.reshape(peers, n // peers, b * inner), "seq", split_axis=0, concat_axis=0, tiled=True
    )
    gate_rows = gate(tokens, gate_weight)
    back = lax.all_to_all(prefix(came, logs), "seq", split_axis=0, concat_axis=0, tiled=True)
    skip = jnp.repeat(skip_gain, head_width)[None]
    part, grow = inside(
        b_rows, c_rows, vc, mid, dtt, cum, cumt, base, skip, gate_rows, head_width
    )
    x, sq = enter(part, grow, c_rows, back.reshape(n, b * inner))
    squares = [sq] + [
        lax.ppermute(sq, "head", [(i, (i + k) % ranks) for i in range(ranks)])
        for k in range(1, ranks)
    ]
    return norm(x, squares, norm_gain[None], inner * ranks)


def solution(mesh):
    return jax.shard_map(
        local,
        mesh=mesh,
        in_specs=(
            P(None, "seq", None),
            P(None, "head"),
            P(None, "head"),
            P(),
            P(None, "head"),
            P(None, "head"),
            P("head"),
            P(),
            P(),
            P("head"),
            P("head"),
            P("head"),
            P("head"),
        ),
        out_specs=P(None, "seq", "head"),
        check_vma=False,
    )
```

```python
import functools
import jax
import jax.numpy as jnp
from jax import lax
from jax.experimental import pallas as pl
from jax.experimental.pallas import tpu as pltpu
from jax.sharding import PartitionSpec as P

EPS = 1e-05
LOG2E = 1.4426950408889634
PAD = 16
CHUNK = 128
TILE = 256
LANES = 128
SLOT = 32
F32 = jnp.float32
BF16 = jnp.bfloat16
WHOLE = pl.BlockSpec(memory_space=pltpu.VMEM)
SCALARS = pl.BlockSpec(memory_space=pltpu.SMEM)


def here(x):
    return pltpu.with_memory_space_constraint(x, pltpu.VMEM)


def params(mib):
    return pltpu.CompilerParams(vmem_limit_bytes=mib << 20)


def mm(a, b):
    return jnp.dot(a, b, preferred_element_type=F32)


def mm_t(a, b):
    return lax.dot_general(a, b, (((1,), (1,)), ((), ())), preferred_element_type=F32)


def silu(x):
    half = 0.5 * x
    return half + half * jnp.tanh(half)


def row(ref):
    return ref[...].reshape(1, ref.shape[0])


def head_select(width, head_width, first_head, group):
    lane = lax.broadcasted_iota(jnp.int32, (LANES, width), 0) - 2 * SLOT * group
    col = lax.broadcasted_iota(jnp.int32, (LANES, width), 1)
    head = lane & (SLOT - 1)
    start = (head - first_head) * head_width
    hit = (lane >= 0) & (lane < 2 * SLOT) & (col >= start) & (col < start + head_width)
    return jnp.where(hit, 1.0, 0.0).astype(BF16)


def conv_of(ref, rows, kernel, offset):
    taps = kernel.shape[0]
    total = offset
    for k in range(taps):
        total = total + kernel[k : k + 1, :] * ref[pl.ds(PAD - taps + 1 + k, rows), :]
    return silu(total).astype(BF16)


def front_kernel(tok, sw, twt, toff, rate, io_out, fac_out, thr_out, cum_out, cumt_out, dtt_out, tws, vec):
    batch, rows, _ = tok.shape
    heads = twt.shape[0]
    chunks = rows // CHUNK
    tws[...] = jnp.zeros_like(tws)
    vec[...] = jnp.zeros_like(vec)
    for g in range(LANES // SLOT):
        tws[pl.ds(g * SLOT, heads), :] = twt[...]
        vec[pl.ds(0, 1), pl.ds(g * SLOT, heads)] = row(toff)
        vec[pl.ds(1, 1), pl.ds(g * SLOT, heads)] = row(rate)
    offset = vec[pl.ds(0, 1), :]
    scale = vec[pl.ds(1, 1), :] * (-LOG2E)
    r = lax.broadcasted_iota(jnp.int32, (CHUNK, CHUNK), 0)
    c = lax.broadcasted_iota(jnp.int32, (CHUNK, CHUNK), 1)
    tri = jnp.where(r >= c, 1.0, 0.0).astype(BF16)
    group = lax.broadcasted_iota(jnp.int32, (1, LANES), 1) // SLOT
    low_lane = (group & 1) == 1

    def parts(x):
        hi = x.astype(BF16).astype(F32)
        return jnp.where(low_lane, x - hi, hi).astype(BF16)

    for i in range(batch):
        x = tok[i]
        io_out[i] = mm(x, sw[...]).astype(BF16)
        z = mm_t(x, tws[...]) + offset
        dt = jnp.maximum(z, 0.0) + jnp.log1p(jnp.exp(-jnp.abs(z)))
        log_decay = dt * scale
        base = jnp.zeros((1, LANES), F32)
        lasts, bases = [], []
        for q in range(chunks):
            span = slice(q * CHUNK, (q + 1) * CHUNK)
            part = log_decay[span]
            hi = part.astype(BF16)
            rest = part - hi.astype(F32)
            mid = rest.astype(BF16)
            low = (rest - mid.astype(F32)).astype(BF16)
            cum = mm(tri, hi) + (mm(tri, mid) + mm(tri, low))
            last = cum[CHUNK - 1 :]
            cum_out[i, pl.ds(q * CHUNK, CHUNK), :] = cum
            cumt_out[i, q] = cum.T[:SLOT]
            dtt_out[i, q] = dt[span].T[:SLOT]
            closing = jnp.exp2(last - cum) * dt[span]
            fac_out[i, pl.ds(q * CHUNK, CHUNK), :] = parts(
                jnp.where(group < 2, closing, jnp.exp2(cum))
            )
            lasts.append(last)
            bases.append(base)
            base = base + last
        blank = [jnp.zeros((1, LANES), F32)] * (4 - chunks % 4 if chunks % 4 else 0)
        table = jnp.concatenate(lasts + blank + bases + blank + [base], axis=0)
        thr_out[i] = jnp.concatenate(
            [parts(jnp.exp2(table)), jnp.zeros((thr_out.shape[1] - table.shape[0], LANES), BF16)], axis=0
        )


def values_kernel(
    owners, axis, head_width, tok, halo, w, sw, vkern, voff, skern, soff, io, fac, thr, *refs
):
    vc_out, mid_out, b_out, c_out = refs[:4]
    ends = refs[4 : 4 + owners]
    bt, mbuf, st0, st1 = refs[4 + owners : 8 + owners]
    vbufs = refs[8 + owners :]
    batch, rows, _ = tok.shape
    inner = w.shape[1]
    n = sw.shape[1] // 2
    chunks = rows // CHUNK
    tiles = inner // TILE
    per = TILE // head_width
    share = n // owners
    spot = lax.rem(lax.axis_index(axis), owners)
    offset = row(voff)

    def project(j, i, buf):
        x = jnp.concatenate([halo[i], tok[i]], axis=0)
        buf[...] = mm(x, w[:, j * TILE : (j + 1) * TILE]).astype(BF16).astype(F32)

    def maps(i, head_rows):
        mbuf[pl.ds(0, PAD), :] = head_rows[i * PAD : (i + 1) * PAD].astype(BF16).astype(F32)
        mbuf[pl.ds(PAD, rows), :] = io[i].astype(F32)
        y = conv_of(mbuf, rows, skern[...], row(soff))
        b_out[i] = y[:, :n]
        c_out[i] = y[:, n:]
        bt[i] = y[:, :n].astype(F32).T.astype(BF16)

    def finish(j, i, buf, hold):
        at = slice(j * TILE, (j + 1) * TILE)
        vc = conv_of(buf, rows, vkern[:, at], offset[:, at])
        vc_out[i, :, at] = vc
        select = head_select(TILE, head_width, j * per, 0)
        through = mm(thr[i], select)
        state = None
        for q in range(chunks):
            span = slice(q * CHUNK, (q + 1) * CHUNK)
            scaled = (vc[span].astype(F32) * mm(fac[i, span], select)).astype(BF16)
            made = mm(bt[i, :, span], scaled)
            if q == 0:
                state = made
            else:
                mid_out[i, q - 1, :, at] = state.astype(BF16)
                state = state * through[q : q + 1] + made
        hold[...] = state
        for k in range(owners):
            owner = jnp.bitwise_xor(spot, k)
            part = hold[pl.ds(pl.multiple_of(owner * share, share), share), :]
            ends[k][:, i * inner + j * TILE : i * inner + (j + 1) * TILE] = part.astype(BF16)

    head_rows = mm(
        jnp.concatenate([halo[i] for i in range(batch)], axis=0), sw[...]
    )
    lane = lax.broadcasted_iota(jnp.int32, (share, LANES), 1)
    line = lax.broadcasted_iota(jnp.int32, (share, LANES), 0)
    decays = jnp.zeros((share, LANES), F32)
    total_row = 2 * ((chunks + 3) // 4 * 4)
    for i in range(batch):
        mine = jnp.broadcast_to(thr[i].astype(F32)[total_row : total_row + 1], (share, LANES))
        decays = jnp.where((line == 0) & (lane // (2 * SLOT) == i), mine, decays)
    for k in range(owners):
        ends[k][:, batch * inner :] = decays.astype(BF16)
    stages = [(j, i) for j in range(tiles) for i in range(batch)]
    for s, (j, i) in enumerate(stages):
        project(j, i, vbufs[s % 4])
        if s < batch:
            maps(s, head_rows)
        else:
            jj, ii = stages[s - batch]
            finish(jj, ii, vbufs[(s - batch) % 4], st0 if s % 2 else st1)
    for s in range(len(stages), len(stages) + batch):
        jj, ii = stages[s - batch]
        finish(jj, ii, vbufs[(s - batch) % 4], st0 if s % 2 else st1)


def gate_kernel(tok, w, out):
    for j in range(w.shape[1] // TILE):
        at = slice(j * TILE, (j + 1) * TILE)
        for i in range(tok.shape[0]):
            out[i, :, at] = mm(tok[i], w[:, at]).astype(BF16)


def inside_kernel(
    head_width, b_rows, c_rows, vc, mid, dtt, cum, cumt, fac, thr, skip, gate_rows, part_out, grow_out
):
    i, q = pl.program_id(0), pl.program_id(1)
    heads = skip.shape[0]
    width = vc.shape[2]
    chunks = vc.shape[1] // CHUNK
    span = pl.ds(pl.multiple_of(q * CHUNK, CHUNK), CHUNK)
    crow = c_rows[i, span, :]
    r = lax.broadcasted_iota(jnp.int32, (CHUNK, CHUNK), 0)
    s = lax.broadcasted_iota(jnp.int32, (CHUNK, CHUNK), 1)
    scores = jnp.where(r >= s, mm_t(crow, b_rows[i, span, :]), 0.0)
    sums = cum[i, span, :]
    before = jnp.maximum(q - 1, 0)
    keep = jnp.where(q > 0, 1.0, 0.0)
    pad_chunks = (chunks + 3) // 4 * 4
    pick = lax.broadcasted_iota(jnp.int32, (thr.shape[1], TILE), 0) == pad_chunks + q
    lane = lax.broadcasted_iota(jnp.int32, (CHUNK, 2 * head_width), 1)
    flat = lane[:1]
    for j in range(width // TILE):
        tile = slice(j * TILE, (j + 1) * TILE)
        rise = mm(fac[i, span, :], head_select(TILE, head_width, j * TILE // head_width, 1))
        base = mm(thr[i], head_select(TILE, head_width, j * TILE // head_width, 0))
        base = jnp.sum(jnp.where(pick, base, 0.0), axis=0, keepdims=True)
        carried = mm(crow, mid[i, before, :, tile]) * (rise * keep)
        swish = silu(gate_rows[i, span, tile].astype(F32))
        grow_out[i, span, tile] = (swish * (rise * base)).astype(BF16)
        for pair in range(TILE // (2 * head_width)):
            inner_at = slice(pair * 2 * head_width, (pair + 1) * 2 * head_width)
            at = slice(j * TILE + inner_at.start, j * TILE + inner_at.stop)
            rows = vc[i, span, at]
            mixes, pieces = [], []
            for k in range(2):
                head = at.start // head_width + k
                gap = jnp.minimum(sums[:, head : head + 1] - cumt[i, q, head : head + 1, :], 0.0)
                mixes.append((scores * jnp.exp2(gap) * dtt[i, q, head : head + 1, :]).astype(BF16))
                pieces.append(jnp.where((lane >= head_width) == (k == 1), rows, jnp.zeros_like(rows)))
            within = mm(jnp.concatenate(mixes, axis=1), jnp.concatenate(pieces, axis=0))
            first = at.start // head_width
            gain = jnp.where(flat < head_width, skip[first], skip[first + 1])
            mixture = within + carried[:, inner_at] + gain * rows.astype(F32)
            part_out[i, span, at] = mixture * swish[:, inner_at]


def gather_owned(owners, axis, refs, held):
    spot = lax.rem(lax.axis_index(axis), owners)
    for k in range(owners):
        held[jnp.bitwise_xor(spot, k)] = refs[k][...]


def total_kernel(owners, axis, head_width, *refs):
    came = refs[:owners]
    total_out, decay_out, held, rows = refs[owners:]
    gather_owned(owners, axis, came, held)
    width = total_out.shape[1]
    batch = LANES // (2 * SLOT)
    for k in range(owners):
        rows[pl.ds(k, 1), :] = held[k, :, width:].astype(F32)[:1]
    lines = rows[...].astype(BF16)
    inner = width // batch
    decay_out[...] = jnp.concatenate(
        [mm(lines, head_select(inner, head_width, 0, i)) for i in range(batch)], axis=1
    )
    state = held[0, :, :width].astype(F32)
    for k in range(1, owners):
        state = state * decay_out[pl.ds(k, 1), :] + held[k, :, :width].astype(F32)
    total_out[...] = state.astype(BF16)


def prefix_kernel(owners, axis, *refs):
    came = refs[:owners]
    decay, first = refs[owners : owners + 2]
    outs = refs[owners + 2 : 2 * owners + 2]
    held, made = refs[2 * owners + 2 :]
    gather_owned(owners, axis, came, held)
    width = first.shape[1]
    state = first[...].astype(F32)
    for k in range(owners):
        made[k] = state.astype(BF16)
        if k + 1 < owners:
            state = state * decay[pl.ds(k, 1), :] + held[k, :, :width].astype(F32)
    spot = lax.rem(lax.axis_index(axis), owners)
    for k in range(owners):
        outs[k][...] = made[jnp.bitwise_xor(spot, k)]


def enter_kernel(owners, axis, part, grow, c_rows, *refs):
    came = refs[:owners]
    out, sq_out, state = refs[owners:]
    batch, rows, inner = part.shape
    share = came[0].shape[0]
    spot = lax.rem(lax.axis_index(axis), owners)
    for k in range(owners):
        at = pl.multiple_of(jnp.bitwise_xor(spot, k) * share, share)
        state[pl.ds(at, share), :] = came[k][...]
    for i in range(batch):
        for q in range(rows // CHUNK):
            span = slice(q * CHUNK, (q + 1) * CHUNK)
            acc = jnp.zeros((CHUNK, LANES), F32)
            for j in range(inner // TILE):
                at = slice(j * TILE, (j + 1) * TILE)
                extra = mm(c_rows[i, span, :], state[:, i * inner + j * TILE : i * inner + (j + 1) * TILE])
                total = part[i, span, at] + grow[i, span, at].astype(F32) * extra
                out[i, span, at] = total
                for k in range(TILE // LANES):
                    piece = total[:, k * LANES : (k + 1) * LANES]
                    acc = acc + piece * piece
            sq_out[:, i * rows + q * CHUNK : i * rows + (q + 1) * CHUNK] = jnp.sum(
                acc.T, axis=0, keepdims=True
            )


def norm_kernel(inner_all, count, *refs):
    squares = refs[:count]
    x, gain, out = refs[count:]
    i, q = pl.program_id(0), pl.program_id(1)
    rows = out.shape[1]
    at = pl.multiple_of((i * pl.num_programs(1) + q) * rows, rows)
    total = squares[0][:, pl.ds(at, rows)]
    for ref in squares[1:]:
        total = total + ref[:, pl.ds(at, rows)]
    inverse = lax.rsqrt(total / inner_all + EPS)
    columns = jnp.broadcast_to(inverse, (LANES, rows)).T
    gains = row(gain)
    span = pl.ds(pl.multiple_of(q * rows, rows), rows)
    for k in range(out.shape[2] // LANES):
        cut = slice(k * LANES, (k + 1) * LANES)
        out[0, :, cut] = (x[i, span, cut] * columns * gains[:, cut]).astype(BF16)


def local(
    tokens,
    gate_weight,
    value_weight,
    state_weight,
    step_weight,
    value_kernel,
    value_offset,
    state_kernel,
    state_offset,
    step_offset,
    decay_rate,
    skip_gain,
    norm_gain,
):
    b, t, d = tokens.shape
    inner = gate_weight.shape[1]
    h = step_weight.shape[1]
    n = state_weight.shape[1] // 2
    head_width = inner // h
    peers = lax.axis_size("seq")
    ranks = lax.axis_size("head")
    owners = peers // 2
    share = n // owners
    chunks = t // CHUNK
    table_rows = 16 * ((2 * ((chunks + 3) // 4 * 4) + 1 + 15) // 16)
    assert h <= SLOT and 2 * SLOT * b <= LANES and owners * 2 == peers

    def swap(arrays):
        return [arrays[0]] + [
            here(lax.ppermute(arrays[k], "seq", [(s, s ^ k) for s in range(peers)]))
            for k in range(1, owners)
        ]

    halo = here(
        lax.ppermute(tokens[:, t - PAD :], "seq", [(s, s + 1) for s in range(peers - 1)])
    )
    io, fac, thr, cum, cumt, dtt = pl.pallas_call(
        front_kernel,
        in_specs=[WHOLE] * 5,
        out_specs=[WHOLE] * 6,
        out_shape=[
            pltpu.VMEM((b, t, 2 * n), BF16),
            pltpu.VMEM((b, t, LANES), BF16),
            pltpu.VMEM((b, table_rows, LANES), BF16),
            pltpu.VMEM((b, t, LANES), F32),
            pltpu.VMEM((b, chunks, SLOT, CHUNK), F32),
            pltpu.VMEM((b, chunks, SLOT, CHUNK), F32),
        ],
        scratch_shapes=[pltpu.VMEM((LANES, d), BF16), pltpu.VMEM((8, LANES), F32)],
        compiler_params=params(16),
        name="front",
        cost_estimate=pl.CostEstimate(
            flops=2 * b * t * d * (2 * n + LANES), transcendentals=0, bytes_accessed=0
        ),
    )(tokens, state_weight, step_weight.T, step_offset, decay_rate)

    outs = pl.pallas_call(
        functools.partial(values_kernel, owners, "seq", head_width),
        in_specs=[WHOLE] * 11,
        out_specs=[WHOLE] * (4 + owners),
        out_shape=[
            pltpu.VMEM((b, t, inner), BF16),
            pltpu.VMEM((b, chunks - 1, n, inner), BF16),
            pltpu.VMEM((b, t, n), BF16),
            pltpu.VMEM((b, t, n), BF16),
        ]
        + [pltpu.VMEM((share, b * inner + LANES), BF16)] * owners,
        scratch_shapes=[
            pltpu.VMEM((b, n, t), BF16),
            pltpu.VMEM((t + PAD, 2 * n), F32),
            pltpu.VMEM((n, TILE), F32),
            pltpu.VMEM((n, TILE), F32),
        ]
        + [pltpu.VMEM((t + PAD, TILE), F32)] * 4,
        compiler_params=params(24),
        name="values",
        cost_estimate=pl.CostEstimate(
            flops=2 * b * t * d * inner, transcendentals=0, bytes_accessed=0
        ),
    )(
        tokens, halo, value_weight, state_weight, value_kernel, value_offset,
        state_kernel, state_offset, io, fac, thr,
    )
    vc, mid, b_rows, c_rows = outs[:4]
    came = swap(outs[4:])
    total, decay = pl.pallas_call(
        functools.partial(total_kernel, owners, "seq", head_width),
        in_specs=[WHOLE] * owners,
        out_specs=[WHOLE] * 2,
        out_shape=[
            pltpu.VMEM((share, b * inner), BF16),
            pltpu.VMEM((max(owners, 8), b * inner), F32),
        ],
        scratch_shapes=[
            pltpu.VMEM((owners, share, b * inner + LANES), BF16),
            pltpu.VMEM((max(owners, 8), LANES), F32),
        ],
        compiler_params=params(16),
        name="total",
    )(*came)
    first = here(lax.ppermute(total, "seq", [(s, s + owners) for s in range(owners)]))
    made = pl.pallas_call(
        functools.partial(prefix_kernel, owners, "seq"),
        in_specs=[WHOLE] * (owners + 2),
        out_specs=[WHOLE] * owners,
        out_shape=[pltpu.VMEM((share, b * inner), BF16)] * owners,
        scratch_shapes=[
            pltpu.VMEM((owners, share, b * inner + LANES), BF16),
            pltpu.VMEM((owners, share, b * inner), BF16),
        ],
        compiler_params=params(16),
        name="prefix",
    )(*came, decay, first)
    states = swap(made)

    gate_rows = pl.pallas_call(
        gate_kernel,
        in_specs=[WHOLE] * 2,
        out_specs=WHOLE,
        out_shape=pltpu.VMEM((b, t, inner), BF16),
        compiler_params=params(16),
        name="gate",
        cost_estimate=pl.CostEstimate(
            flops=2 * b * t * d * inner, transcendentals=0, bytes_accessed=0
        ),
    )(tokens, gate_weight)
    part, grow = pl.pallas_call(
        functools.partial(inside_kernel, head_width),
        grid=(b, chunks),
        in_specs=[WHOLE] * 9 + [SCALARS, WHOLE],
        out_specs=[WHOLE] * 2,
        out_shape=[pltpu.VMEM((b, t, inner), F32), pltpu.VMEM((b, t, inner), BF16)],
        compiler_params=params(16),
        name="inside",
        cost_estimate=pl.CostEstimate(
            flops=2 * b * t * d * inner, transcendentals=0, bytes_accessed=0
        ),
    )(b_rows, c_rows, vc, mid, dtt, cum, cumt, fac, thr, skip_gain, gate_rows)

    x, sq = pl.pallas_call(
        functools.partial(enter_kernel, owners, "seq"),
        in_specs=[WHOLE] * (3 + owners),
        out_specs=[WHOLE] * 2,
        out_shape=[pltpu.VMEM((b, t, inner), F32), pltpu.VMEM((1, b * t), F32)],
        scratch_shapes=[pltpu.VMEM((n, b * inner), BF16)],
        compiler_params=params(16),
        name="enter",
    )(part, grow, c_rows, *states)
    squares = [sq] + [
        here(lax.ppermute(sq, "head", [(s, (s + k) % ranks) for s in range(ranks)]))
        for k in range(1, ranks)
    ]
    rows = min(t, 256)
    return pl.pallas_call(
        functools.partial(norm_kernel, inner * ranks, ranks),
        grid=(b, t // rows),
        in_specs=[WHOLE] * (ranks + 2),
        out_specs=pl.BlockSpec((1, rows, inner), lambda i, q: (i, q, 0)),
        out_shape=jax.ShapeDtypeStruct((b, t, inner), BF16),
        compiler_params=params(16),
        name="norm",
    )(*squares, x, norm_gain)


def solution(mesh):
    return jax.shard_map(
        local,
        mesh=mesh,
        in_specs=(
            P(None, "seq", None),
            P(None, "head"),
            P(None, "head"),
            P(),
            P(None, "head"),
            P(None, "head"),
            P("head"),
            P(),
            P(),
            P("head"),
            P("head"),
            P("head"),
            P("head"),
        ),
        out_specs=P(None, "seq", "head"),
        check_vma=False,
    )
```

```python
import functools
import jax
import jax.numpy as jnp
from jax import lax
from jax.experimental import pallas as pl
from jax.experimental.pallas import tpu as pltpu
from jax.sharding import PartitionSpec as P

EPS = 1e-05
LOG2E = 1.4426950408889634
PAD = 16
CHUNK = 128
TILE = 256
LANES = 128
SLOT = 32
F32 = jnp.float32
BF16 = jnp.bfloat16
WHOLE = pl.BlockSpec(memory_space=pltpu.VMEM)
REMOTE = pl.BlockSpec(memory_space=pltpu.HBM)
SCALARS = pl.BlockSpec(memory_space=pltpu.SMEM)


def here(x):
    return pltpu.with_memory_space_constraint(x, pltpu.VMEM)


def far(x):
    return pltpu.with_memory_space_constraint(x, pltpu.HBM)


def params(mib):
    return pltpu.CompilerParams(vmem_limit_bytes=mib << 20)


def mm(a, b):
    return jnp.dot(a, b, preferred_element_type=F32)


def mm_t(a, b):
    return lax.dot_general(a, b, (((1,), (1,)), ((), ())), preferred_element_type=F32)


def silu(x):
    half = 0.5 * x
    return half + half * jnp.tanh(half)


def row(ref):
    return ref[...].reshape(1, ref.shape[0])


def head_select(width, head_width, first_head, group):
    lane = lax.broadcasted_iota(jnp.int32, (LANES, width), 0) - 2 * SLOT * group
    col = lax.broadcasted_iota(jnp.int32, (LANES, width), 1)
    head = lane & (SLOT - 1)
    start = (head - first_head) * head_width
    hit = (lane >= 0) & (lane < 2 * SLOT) & (col >= start) & (col < start + head_width)
    return jnp.where(hit, 1.0, 0.0).astype(BF16)


def conv_of(ref, rows, kernel, offset):
    taps = kernel.shape[0]
    total = offset
    for k in range(taps):
        total = total + kernel[k : k + 1, :] * ref[pl.ds(PAD - taps + 1 + k, rows), :]
    return silu(total).astype(BF16)


def front_kernel(
    tok_in, sw_in, twt_in, w_in, toff_in, rate_in,
    tok, sw, w, io_out, fac_out, thr_out, cum_out, cumt_out, dtt_out,
    twt, toff, rate, tws, vec, sem,
):
    batch, rows, _ = tok.shape
    heads = twt.shape[0]
    chunks = rows // CHUNK
    token_copies = [
        pltpu.make_async_copy(tok_in.at[i], tok.at[i], sem.at[i]) for i in range(batch)
    ]
    other = [
        pltpu.make_async_copy(twt_in, twt, sem.at[batch]),
        pltpu.make_async_copy(sw_in, sw, sem.at[batch + 1]),
        pltpu.make_async_copy(toff_in, toff, sem.at[batch + 3]),
        pltpu.make_async_copy(rate_in, rate, sem.at[batch + 4]),
    ]
    last_copy = pltpu.make_async_copy(w_in, w, sem.at[batch + 2])
    for copy in other[2:] + [other[0], token_copies[0], other[1]] + token_copies[1:] + [last_copy]:
        copy.start()
    for k in (0, 2, 3):
        other[k].wait()
    tws[...] = jnp.zeros_like(tws)
    vec[...] = jnp.zeros_like(vec)
    for g in range(LANES // SLOT):
        tws[pl.ds(g * SLOT, heads), :] = twt[...]
        vec[pl.ds(0, 1), pl.ds(g * SLOT, heads)] = row(toff)
        vec[pl.ds(1, 1), pl.ds(g * SLOT, heads)] = row(rate)
    offset = vec[pl.ds(0, 1), :]
    scale = vec[pl.ds(1, 1), :] * (-LOG2E)
    r = lax.broadcasted_iota(jnp.int32, (CHUNK, CHUNK), 0)
    c = lax.broadcasted_iota(jnp.int32, (CHUNK, CHUNK), 1)
    tri = jnp.where(r >= c, 1.0, 0.0).astype(BF16)
    group = lax.broadcasted_iota(jnp.int32, (1, LANES), 1) // SLOT
    low_lane = (group & 1) == 1

    def parts(x):
        hi = x.astype(BF16).astype(F32)
        return jnp.where(low_lane, x - hi, hi).astype(BF16)

    for i in range(batch):
        token_copies[i].wait()
        if i == 0:
            other[1].wait()
        x = tok[i]
        io_out[i] = mm(x, sw[...]).astype(BF16)
        z = mm_t(x, tws[...]) + offset
        dt = jnp.maximum(z, 0.0) + jnp.log1p(jnp.exp(-jnp.abs(z)))
        log_decay = dt * scale
        base = jnp.zeros((1, LANES), F32)
        lasts, bases = [], []
        for q in range(chunks):
            span = slice(q * CHUNK, (q + 1) * CHUNK)
            part = log_decay[span]
            hi = part.astype(BF16)
            rest = part - hi.astype(F32)
            mid = rest.astype(BF16)
            low = (rest - mid.astype(F32)).astype(BF16)
            cum = mm(tri, hi) + (mm(tri, mid) + mm(tri, low))
            last = cum[CHUNK - 1 :]
            cum_out[i, pl.ds(q * CHUNK, CHUNK), :] = cum
            cumt_out[i, q] = cum.T[:SLOT]
            dtt_out[i, q] = dt[span].T[:SLOT]
            closing = jnp.exp2(last - cum) * dt[span]
            fac_out[i, pl.ds(q * CHUNK, CHUNK), :] = parts(
                jnp.where(group < 2, closing, jnp.exp2(cum))
            )
            lasts.append(last)
            bases.append(base)
            base = base + last
        blank = [jnp.zeros((1, LANES), F32)] * (4 - chunks % 4 if chunks % 4 else 0)
        table = jnp.concatenate(lasts + blank + bases + blank + [base], axis=0)
        thr_out[i] = jnp.concatenate(
            [parts(jnp.exp2(table)), jnp.zeros((thr_out.shape[1] - table.shape[0], LANES), BF16)], axis=0
        )
    last_copy.wait()


def values_kernel(
    owners, axis, head_width, tok, halo, w, sw, vkern, voff, skern, soff, io, fac, thr, gw_in, *refs
):
    vc_out, mid_out, b_out, c_out, gw = refs[:5]
    ends = refs[5 : 5 + owners]
    bt, mbuf, st0, st1, sem = refs[5 + owners : 10 + owners]
    vbufs = refs[10 + owners :]
    copy = pltpu.make_async_copy(gw_in, gw, sem)
    copy.start()
    batch, rows, _ = tok.shape
    inner = w.shape[1]
    n = sw.shape[1] // 2
    chunks = rows // CHUNK
    tiles = inner // TILE
    per = TILE // head_width
    share = n // owners
    spot = lax.rem(lax.axis_index(axis), owners)
    offset = row(voff)

    def project(j, i, buf):
        x = jnp.concatenate([halo[i], tok[i]], axis=0)
        buf[...] = mm(x, w[:, j * TILE : (j + 1) * TILE]).astype(BF16).astype(F32)

    def maps(i, head_rows):
        mbuf[pl.ds(0, PAD), :] = head_rows[i * PAD : (i + 1) * PAD].astype(BF16).astype(F32)
        mbuf[pl.ds(PAD, rows), :] = io[i].astype(F32)
        y = conv_of(mbuf, rows, skern[...], row(soff))
        b_out[i] = y[:, :n]
        c_out[i] = y[:, n:]
        bt[i] = y[:, :n].astype(F32).T.astype(BF16)

    def finish(j, i, buf, hold):
        at = slice(j * TILE, (j + 1) * TILE)
        vc = conv_of(buf, rows, vkern[:, at], offset[:, at])
        vc_out[i, :, at] = vc
        select = head_select(TILE, head_width, j * per, 0)
        through = mm(thr[i], select)
        state = None
        for q in range(chunks):
            span = slice(q * CHUNK, (q + 1) * CHUNK)
            scaled = (vc[span].astype(F32) * mm(fac[i, span], select)).astype(BF16)
            made = mm(bt[i, :, span], scaled)
            if q == 0:
                state = made
            else:
                mid_out[i, q - 1, :, at] = state.astype(BF16)
                state = state * through[q : q + 1] + made
        hold[...] = state
        for k in range(owners):
            owner = jnp.bitwise_xor(spot, k)
            part = hold[pl.ds(pl.multiple_of(owner * share, share), share), :]
            ends[k][:, i * inner + j * TILE : i * inner + (j + 1) * TILE] = part.astype(BF16)

    head_rows = mm(
        jnp.concatenate([halo[i] for i in range(batch)], axis=0), sw[...]
    )
    lane = lax.broadcasted_iota(jnp.int32, (share, LANES), 1)
    line = lax.broadcasted_iota(jnp.int32, (share, LANES), 0)
    decays = jnp.zeros((share, LANES), F32)
    total_row = 2 * ((chunks + 3) // 4 * 4)
    for i in range(batch):
        mine = jnp.broadcast_to(thr[i].astype(F32)[total_row : total_row + 1], (share, LANES))
        decays = jnp.where((line == 0) & (lane // (2 * SLOT) == i), mine, decays)
    for k in range(owners):
        ends[k][:, batch * inner :] = decays.astype(BF16)
    stages = [(j, i) for j in range(tiles) for i in range(batch)]
    for s, (j, i) in enumerate(stages):
        project(j, i, vbufs[s % 4])
        if s < batch:
            maps(s, head_rows)
        else:
            jj, ii = stages[s - batch]
            finish(jj, ii, vbufs[(s - batch) % 4], st0 if s % 2 else st1)
    for s in range(len(stages), len(stages) + batch):
        jj, ii = stages[s - batch]
        finish(jj, ii, vbufs[(s - batch) % 4], st0 if s % 2 else st1)
    copy.wait()


def gate_kernel(tok, w, out):
    for j in range(w.shape[1] // TILE):
        at = slice(j * TILE, (j + 1) * TILE)
        for i in range(tok.shape[0]):
            out[i, :, at] = mm(tok[i], w[:, at]).astype(BF16)


def inside_kernel(
    head_width, b_rows, c_rows, vc, mid, dtt, cum, cumt, fac, thr, skip, gate_rows, part_out, grow_out
):
    i, q = pl.program_id(0), pl.program_id(1)
    heads = skip.shape[0]
    width = vc.shape[2]
    chunks = vc.shape[1] // CHUNK
    span = pl.ds(pl.multiple_of(q * CHUNK, CHUNK), CHUNK)
    crow = c_rows[i, span, :]
    r = lax.broadcasted_iota(jnp.int32, (CHUNK, CHUNK), 0)
    s = lax.broadcasted_iota(jnp.int32, (CHUNK, CHUNK), 1)
    scores = jnp.where(r >= s, mm_t(crow, b_rows[i, span, :]), 0.0)
    sums = cum[i, span, :]
    before = jnp.maximum(q - 1, 0)
    keep = jnp.where(q > 0, 1.0, 0.0)
    pad_chunks = (chunks + 3) // 4 * 4
    pick = lax.broadcasted_iota(jnp.int32, (thr.shape[1], TILE), 0) == pad_chunks + q
    lane = lax.broadcasted_iota(jnp.int32, (CHUNK, 2 * head_width), 1)
    flat = lane[:1]
    for j in range(width // TILE):
        tile = slice(j * TILE, (j + 1) * TILE)
        rise = mm(fac[i, span, :], head_select(TILE, head_width, j * TILE // head_width, 1))
        base = mm(thr[i], head_select(TILE, head_width, j * TILE // head_width, 0))
        base = jnp.sum(jnp.where(pick, base, 0.0), axis=0, keepdims=True)
        carried = mm(crow, mid[i, before, :, tile]) * (rise * keep)
        swish = silu(gate_rows[i, span, tile].astype(F32))
        grow_out[i, span, tile] = (swish * (rise * base)).astype(BF16)
        for pair in range(TILE // (2 * head_width)):
            inner_at = slice(pair * 2 * head_width, (pair + 1) * 2 * head_width)
            at = slice(j * TILE + inner_at.start, j * TILE + inner_at.stop)
            rows = vc[i, span, at]
            mixes, pieces = [], []
            for k in range(2):
                head = at.start // head_width + k
                gap = jnp.minimum(sums[:, head : head + 1] - cumt[i, q, head : head + 1, :], 0.0)
                mixes.append((scores * jnp.exp2(gap) * dtt[i, q, head : head + 1, :]).astype(BF16))
                pieces.append(jnp.where((lane >= head_width) == (k == 1), rows, jnp.zeros_like(rows)))
            within = mm(jnp.concatenate(mixes, axis=1), jnp.concatenate(pieces, axis=0))
            first = at.start // head_width
            gain = jnp.where(flat < head_width, skip[first], skip[first + 1])
            mixture = within + carried[:, inner_at] + gain * rows.astype(F32)
            part_out[i, span, at] = mixture * swish[:, inner_at]


def gather_owned(owners, axis, refs, held):
    spot = lax.rem(lax.axis_index(axis), owners)
    for k in range(owners):
        held[jnp.bitwise_xor(spot, k)] = refs[k][...]


def total_kernel(owners, axis, head_width, *refs):
    came = refs[:owners]
    total_out, decay_out, held, rows = refs[owners + 1 :]
    gather_owned(owners, axis, came, held)
    width = total_out.shape[1]
    batch = LANES // (2 * SLOT)
    for k in range(owners):
        rows[pl.ds(k, 1), :] = held[k, :, width:].astype(F32)[:1]
    lines = rows[...].astype(BF16)
    inner = width // batch
    decay_out[...] = jnp.concatenate(
        [mm(lines, head_select(inner, head_width, 0, i)) for i in range(batch)], axis=1
    )
    state = held[0, :, :width].astype(F32)
    for k in range(1, owners):
        state = state * decay_out[pl.ds(k, 1), :] + held[k, :, :width].astype(F32)
    total_out[...] = state.astype(BF16)


def prefix_kernel(owners, axis, *refs):
    came = refs[:owners]
    decay, first = refs[owners : owners + 2]
    outs = refs[owners + 3 : 2 * owners + 3]
    held, made = refs[2 * owners + 3 :]
    gather_owned(owners, axis, came, held)
    width = first.shape[1]
    state = first[...].astype(F32)
    for k in range(owners):
        made[k] = state.astype(BF16)
        if k + 1 < owners:
            state = state * decay[pl.ds(k, 1), :] + held[k, :, :width].astype(F32)
    spot = lax.rem(lax.axis_index(axis), owners)
    for k in range(owners):
        outs[k][...] = made[jnp.bitwise_xor(spot, k)]


def enter_kernel(owners, axis, part, grow, c_rows, *refs):
    came = refs[:owners]
    out, sq_out, state = refs[owners:]
    batch, rows, inner = part.shape
    share = came[0].shape[0]
    spot = lax.rem(lax.axis_index(axis), owners)
    for k in range(owners):
        at = pl.multiple_of(jnp.bitwise_xor(spot, k) * share, share)
        state[pl.ds(at, share), :] = came[k][...]
    for i in range(batch):
        for q in range(rows // CHUNK):
            span = slice(q * CHUNK, (q + 1) * CHUNK)
            acc = jnp.zeros((CHUNK, LANES), F32)
            for j in range(inner // TILE):
                at = slice(j * TILE, (j + 1) * TILE)
                extra = mm(c_rows[i, span, :], state[:, i * inner + j * TILE : i * inner + (j + 1) * TILE])
                total = part[i, span, at] + grow[i, span, at].astype(F32) * extra
                out[i, span, at] = total
                for k in range(TILE // LANES):
                    piece = total[:, k * LANES : (k + 1) * LANES]
                    acc = acc + piece * piece
            sq_out[:, i * rows + q * CHUNK : i * rows + (q + 1) * CHUNK] = jnp.sum(
                acc.T, axis=0, keepdims=True
            )


def norm_kernel(inner_all, count, *refs):
    squares = refs[:count]
    x, gain, out = refs[count:]
    i, q = pl.program_id(0), pl.program_id(1)
    rows = out.shape[1]
    at = pl.multiple_of((i * pl.num_programs(1) + q) * rows, rows)
    total = squares[0][:, pl.ds(at, rows)]
    for ref in squares[1:]:
        total = total + ref[:, pl.ds(at, rows)]
    inverse = lax.rsqrt(total / inner_all + EPS)
    columns = jnp.broadcast_to(inverse, (LANES, rows)).T
    gains = row(gain)
    span = pl.ds(pl.multiple_of(q * rows, rows), rows)
    for k in range(out.shape[2] // LANES):
        cut = slice(k * LANES, (k + 1) * LANES)
        out[0, :, cut] = (x[i, span, cut] * columns * gains[:, cut]).astype(BF16)


def local(
    tokens,
    gate_weight,
    value_weight,
    state_weight,
    step_weight,
    value_kernel,
    value_offset,
    state_kernel,
    state_offset,
    step_offset,
    decay_rate,
    skip_gain,
    norm_gain,
):
    b, t, d = tokens.shape
    inner = gate_weight.shape[1]
    h = step_weight.shape[1]
    n = state_weight.shape[1] // 2
    head_width = inner // h
    peers = lax.axis_size("seq")
    ranks = lax.axis_size("head")
    owners = peers // 2
    share = n // owners
    chunks = t // CHUNK
    table_rows = 16 * ((2 * ((chunks + 3) // 4 * 4) + 1 + 15) // 16)
    assert h <= SLOT and 2 * SLOT * b <= LANES and owners * 2 == peers

    def swap(arrays):
        return [arrays[0]] + [
            here(lax.ppermute(arrays[k], "seq", [(s, s ^ k) for s in range(peers)]))
            for k in range(1, owners)
        ]

    halo = here(
        lax.ppermute(tokens[:, t - PAD :], "seq", [(s, s + 1) for s in range(peers - 1)])
    )
    tok, sw, w, io, fac, thr, cum, cumt, dtt = pl.pallas_call(
        front_kernel,
        in_specs=[REMOTE] * 6,
        out_specs=[WHOLE] * 9,
        out_shape=[
            pltpu.VMEM(tokens.shape, BF16),
            pltpu.VMEM(state_weight.shape, BF16),
            pltpu.VMEM(value_weight.shape, BF16),
            pltpu.VMEM((b, t, 2 * n), BF16),
            pltpu.VMEM((b, t, LANES), BF16),
            pltpu.VMEM((b, table_rows, LANES), BF16),
            pltpu.VMEM((b, t, LANES), F32),
            pltpu.VMEM((b, chunks, SLOT, CHUNK), F32),
            pltpu.VMEM((b, chunks, SLOT, CHUNK), F32),
        ],
        scratch_shapes=[
            pltpu.VMEM((h, d), BF16),
            pltpu.VMEM((h,), F32),
            pltpu.VMEM((h,), F32),
            pltpu.VMEM((LANES, d), BF16),
            pltpu.VMEM((8, LANES), F32),
            pltpu.SemaphoreType.DMA((b + 5,)),
        ],
        compiler_params=params(16),
        name="front",
        cost_estimate=pl.CostEstimate(
            flops=2 * b * t * d * (2 * n + LANES), transcendentals=0, bytes_accessed=0
        ),
    )(*map(far, (tokens, state_weight, step_weight.T, value_weight, step_offset, decay_rate)))

    outs = pl.pallas_call(
        functools.partial(values_kernel, owners, "seq", head_width),
        in_specs=[WHOLE] * 11 + [REMOTE],
        out_specs=[WHOLE] * (5 + owners),
        out_shape=[
            pltpu.VMEM((b, t, inner), BF16),
            pltpu.VMEM((b, chunks - 1, n, inner), BF16),
            pltpu.VMEM((b, t, n), BF16),
            pltpu.VMEM((b, t, n), BF16),
            pltpu.VMEM(gate_weight.shape, BF16),
        ]
        + [pltpu.VMEM((share, b * inner + LANES), BF16)] * owners,
        scratch_shapes=[
            pltpu.VMEM((b, n, t), BF16),
            pltpu.VMEM((t + PAD, 2 * n), F32),
            pltpu.VMEM((n, TILE), F32),
            pltpu.VMEM((n, TILE), F32),
            pltpu.SemaphoreType.DMA,
        ]
        + [pltpu.VMEM((t + PAD, TILE), F32)] * 4,
        compiler_params=params(24),
        name="values",
        cost_estimate=pl.CostEstimate(
            flops=2 * b * t * d * inner, transcendentals=0, bytes_accessed=0
        ),
    )(
        tok, halo, w, sw, value_kernel, value_offset,
        state_kernel, state_offset, io, fac, thr, far(gate_weight),
    )
    vc, mid, b_rows, c_rows, gw = outs[:5]
    came = swap(outs[5:])
    gate_rows = pl.pallas_call(
        gate_kernel,
        in_specs=[WHOLE] * 2,
        out_specs=WHOLE,
        out_shape=pltpu.VMEM((b, t, inner), BF16),
        compiler_params=params(16),
        name="gate",
        cost_estimate=pl.CostEstimate(
            flops=2 * b * t * d * inner, transcendentals=0, bytes_accessed=0
        ),
    )(tok, gw)
    part, grow = pl.pallas_call(
        functools.partial(inside_kernel, head_width),
        grid=(b, chunks),
        in_specs=[WHOLE] * 9 + [SCALARS, WHOLE],
        out_specs=[WHOLE] * 2,
        out_shape=[pltpu.VMEM((b, t, inner), F32), pltpu.VMEM((b, t, inner), BF16)],
        compiler_params=params(16),
        name="inside",
        cost_estimate=pl.CostEstimate(
            flops=2 * b * t * d * inner, transcendentals=0, bytes_accessed=0
        ),
    )(b_rows, c_rows, vc, mid, dtt, cum, cumt, fac, thr, skip_gain, gate_rows)

    total, decay = pl.pallas_call(
        functools.partial(total_kernel, owners, "seq", head_width),
        in_specs=[WHOLE] * (owners + 1),
        out_specs=[WHOLE] * 2,
        out_shape=[
            pltpu.VMEM((share, b * inner), BF16),
            pltpu.VMEM((max(owners, 8), b * inner), F32),
        ],
        scratch_shapes=[
            pltpu.VMEM((owners, share, b * inner + LANES), BF16),
            pltpu.VMEM((max(owners, 8), LANES), F32),
        ],
        compiler_params=params(16),
        name="total",
    )(*came, gate_rows)
    first = here(lax.ppermute(total, "seq", [(s, s + owners) for s in range(owners)]))
    made = pl.pallas_call(
        functools.partial(prefix_kernel, owners, "seq"),
        in_specs=[WHOLE] * (owners + 3),
        out_specs=[WHOLE] * owners,
        out_shape=[pltpu.VMEM((share, b * inner), BF16)] * owners,
        scratch_shapes=[
            pltpu.VMEM((owners, share, b * inner + LANES), BF16),
            pltpu.VMEM((owners, share, b * inner), BF16),
        ],
        compiler_params=params(16),
        name="prefix",
    )(*came, decay, first, grow)
    states = swap(made)

    x, sq = pl.pallas_call(
        functools.partial(enter_kernel, owners, "seq"),
        in_specs=[WHOLE] * (3 + owners),
        out_specs=[WHOLE] * 2,
        out_shape=[pltpu.VMEM((b, t, inner), F32), pltpu.VMEM((1, b * t), F32)],
        scratch_shapes=[pltpu.VMEM((n, b * inner), BF16)],
        compiler_params=params(16),
        name="enter",
    )(part, grow, c_rows, *states)
    squares = [sq] + [
        here(lax.ppermute(sq, "head", [(s, (s + k) % ranks) for s in range(ranks)]))
        for k in range(1, ranks)
    ]
    rows = min(t, 256)
    return pl.pallas_call(
        functools.partial(norm_kernel, inner * ranks, ranks),
        grid=(b, t // rows),
        in_specs=[WHOLE] * (ranks + 2),
        out_specs=pl.BlockSpec((1, rows, inner), lambda i, q: (i, q, 0)),
        out_shape=jax.ShapeDtypeStruct((b, t, inner), BF16),
        compiler_params=params(16),
        name="norm",
    )(*squares, x, norm_gain)


def solution(mesh):
    return jax.shard_map(
        local,
        mesh=mesh,
        in_specs=(
            P(None, "seq", None),
            P(None, "head"),
            P(None, "head"),
            P(),
            P(None, "head"),
            P(None, "head"),
            P("head"),
            P(),
            P(),
            P("head"),
            P("head"),
            P("head"),
            P("head"),
        ),
        out_specs=P(None, "seq", "head"),
        check_vma=False,
    )
```

```python
import functools
import jax
import jax.numpy as jnp
from jax import lax
from jax.experimental import pallas as pl
from jax.experimental.pallas import tpu as pltpu
from jax.sharding import PartitionSpec as P

EPS = 1e-05
LOG2E = 1.4426950408889634
PAD = 16
CHUNK = 128
TILE = 256
LANES = 128
SLOT = 32
F32 = jnp.float32
BF16 = jnp.bfloat16
WHOLE = pl.BlockSpec(memory_space=pltpu.VMEM)
FAR = pl.BlockSpec(memory_space=pltpu.HBM)
SCALARS = pl.BlockSpec(memory_space=pltpu.SMEM)


def here(x):
    return pltpu.with_memory_space_constraint(x, pltpu.VMEM)


def far(x):
    return pltpu.with_memory_space_constraint(x, pltpu.HBM)


def params(mib):
    return pltpu.CompilerParams(vmem_limit_bytes=mib << 20)


def cost(flops):
    return pl.CostEstimate(flops=int(flops), transcendentals=0, bytes_accessed=0)


def mm(a, b):
    return jnp.dot(a, b, preferred_element_type=F32)


def mm_t(a, b):
    return lax.dot_general(a, b, (((1,), (1,)), ((), ())), preferred_element_type=F32)


def silu(x):
    half = 0.5 * x
    return half + half * jnp.tanh(half)


def row(ref):
    return ref[...].reshape(1, ref.shape[0])


def pieces(total, size=CHUNK):
    return [slice(k * size, (k + 1) * size) for k in range(total // size)]


def head_select(width, head_width, group):
    lane = lax.broadcasted_iota(jnp.int32, (LANES, width), 0) - 2 * SLOT * group
    col = lax.broadcasted_iota(jnp.int32, (LANES, width), 1)
    start = (lane & (SLOT - 1)) * head_width
    hit = (lane >= 0) & (lane < 2 * SLOT) & (col >= start) & (col < start + head_width)
    return jnp.where(hit, 1.0, 0.0).astype(BF16)


def conv_of(x, kernel, offset):
    back = pltpu.roll(x, 1, 0)
    near = offset + kernel[3:4] * x + kernel[2:3] * back
    deep = kernel[1:2] * x + kernel[0:1] * back
    return silu((near + pltpu.roll(deep, 2, 0))[PAD:]).astype(BF16)


def front_kernel(head_width, *refs):
    tok_in, sw_in, twt_in, w_in, toff_in, rate_in = refs[:6]
    batch = tok_in.shape[0]
    sw, w, sel_a, sel_b = refs[6:10]
    per_batch = [refs[10 + 8 * i : 18 + 8 * i] for i in range(batch)]
    twt, toff, rate, tws, vec, sem = refs[10 + 8 * batch :]
    rows = tok_in.shape[1]
    heads = twt.shape[0]
    token_copies = [
        pltpu.make_async_copy(tok_in.at[i], per_batch[i][0], sem.at[i]) for i in range(batch)
    ]
    copies = [
        pltpu.make_async_copy(twt_in, twt, sem.at[batch]),
        pltpu.make_async_copy(toff_in, toff, sem.at[batch + 1]),
        pltpu.make_async_copy(rate_in, rate, sem.at[batch + 2]),
        pltpu.make_async_copy(sw_in, sw, sem.at[batch + 3]),
        pltpu.make_async_copy(w_in.at[:, pl.ds(0, TILE)], w, sem.at[batch + 4]),
    ]
    for copy in copies[:3] + [token_copies[0], copies[3]] + token_copies[1:] + [copies[4]]:
        copy.start()
    sel_a[...] = head_select(sel_a.shape[1], head_width, 0)
    sel_b[...] = head_select(sel_b.shape[1], head_width, 1)
    for copy in copies[:3]:
        copy.wait()
    tws[...] = jnp.zeros_like(tws)
    vec[...] = jnp.zeros_like(vec)
    for g in range(LANES // SLOT):
        tws[pl.ds(g * SLOT, heads), :] = twt[...]
        vec[pl.ds(0, 1), pl.ds(g * SLOT, heads)] = row(toff)
        vec[pl.ds(1, 1), pl.ds(g * SLOT, heads)] = row(rate)
    offset = vec[pl.ds(0, 1), :]
    scale = vec[pl.ds(1, 1), :] * (-LOG2E)
    r = lax.broadcasted_iota(jnp.int32, (CHUNK, CHUNK), 0)
    c = lax.broadcasted_iota(jnp.int32, (CHUNK, CHUNK), 1)
    tri = jnp.where(r >= c, 1.0, 0.0).astype(BF16)
    group = lax.broadcasted_iota(jnp.int32, (1, LANES), 1) // SLOT
    low_lane = (group & 1) == 1

    def parts(x):
        hi = x.astype(BF16).astype(F32)
        return jnp.where(low_lane, x - hi, hi).astype(BF16)

    for i in range(batch):
        tok, io_out, close_out, rise_out, thr_out, cum_out, cumt_out, dtt_out = per_batch[i]
        token_copies[i].wait()
        if i == 0:
            copies[3].wait()
        x = tok[...]
        io_out[...] = mm(x, sw[...]).astype(BF16)
        z = mm_t(x, tws[...]) + offset
        dt = jnp.maximum(z, 0.0) + jnp.log1p(jnp.exp(-jnp.abs(z)))
        log_decay = dt * scale
        base = jnp.zeros((1, LANES), F32)
        lasts = []
        for q, span in enumerate(pieces(rows)):
            part = log_decay[span]
            hi = part.astype(BF16)
            rest = part - hi.astype(F32)
            mid = rest.astype(BF16)
            low = (rest - mid.astype(F32)).astype(BF16)
            cum = mm(tri, hi) + (mm(tri, mid) + mm(tri, low))
            last = cum[CHUNK - 1 :]
            cum_out[span, :] = cum
            cumt_out[q] = cum.T[:SLOT]
            dtt_out[q] = dt[span].T[:SLOT]
            close_out[span, :] = parts(jnp.exp2(last - cum) * dt[span])
            rise_out[span, :] = parts(jnp.exp2(jnp.where(group < 2, cum, cum + base)))
            lasts.append(last)
            base = base + last
        blank = [jnp.zeros((1, LANES), F32)] * (thr_out.shape[0] - len(lasts) - 1)
        thr_out[...] = parts(jnp.exp2(jnp.concatenate(lasts + [base] + blank, axis=0)))
    copies[4].wait()


def values_kernel(owners, axis, index, loads, *refs):
    tok, halo, w0, sw, vkern, voff, skern, soff, io, close, thr, sel = refs[:12]
    refs = refs[12:]
    if loads:
        w_in, refs = refs[0], refs[1:]
        vc_out, mid_out, b_out, c_out, wr = refs[:5]
        refs = refs[5:]
    else:
        wr, gate_in, refs = refs[0], refs[1], refs[2:]
        vc_out, mid_out, b_out, c_out, gw = refs[:5]
        refs = refs[5:]
    ends, (bt, mbuf, hold, vb0, vb1, sem) = refs[:owners], refs[owners:]
    rows = tok.shape[0]
    inner = vc_out.shape[1]
    n = b_out.shape[1]
    share = n // owners
    spot = lax.rem(lax.axis_index(axis), owners)
    tiles = pieces(inner, TILE)
    if loads:
        copies = [
            pltpu.make_async_copy(w_in.at[:, at], wr.at[:, to], sem.at[k])
            for k, (at, to) in enumerate(zip(tiles[1:], tiles))
        ]
    else:
        copies = [pltpu.make_async_copy(gate_in, gw, sem.at[0])]
    for copy in copies:
        copy.start()
    rim = halo[index]
    offset = row(voff)

    def project(j, buf):
        weight = w0[...] if j == 0 else wr[:, tiles[j - 1]]
        x = jnp.concatenate([rim, tok[...]], axis=0)
        buf[...] = mm(x, weight).astype(BF16).astype(F32)

    def maps():
        mbuf[pl.ds(0, PAD), :] = mm(rim, sw[...]).astype(BF16).astype(F32)
        mbuf[pl.ds(PAD, rows), :] = io[...].astype(F32)
        y = conv_of(mbuf[...], skern[...], row(soff))
        b_out[...] = y[:, :n]
        c_out[...] = y[:, n:]
        bt[...] = y[:, :n].astype(F32).T.astype(BF16)

    def finish(j, buf):
        at = tiles[j]
        vc = conv_of(buf[...], vkern[:, at], offset[:, at])
        vc_out[:, at] = vc
        select = sel[:, at]
        through = mm(thr[...], select)
        state = None
        for q, span in enumerate(pieces(rows)):
            scaled = (vc[span].astype(F32) * mm(close[span, :], select)).astype(BF16)
            made = mm(bt[:, span], scaled)
            if q == 0:
                state = made
            else:
                mid_out[q - 1, :, at] = state.astype(BF16)
                state = state * through[q : q + 1] + made
        hold[...] = state
        for k in range(owners):
            owner = jnp.bitwise_xor(spot, k)
            part = hold[pl.ds(pl.multiple_of(owner * share, share), share), :]
            ends[k][:, at] = part.astype(BF16)

    line = lax.broadcasted_iota(jnp.int32, (share, LANES), 0)
    count = rows // CHUNK
    mine = jnp.broadcast_to(thr[...].astype(F32)[count : count + 1], (share, LANES))
    decays = jnp.where(line == 0, mine, 0.0).astype(BF16)
    for k in range(owners):
        ends[k][:, inner:] = decays
    bufs = (vb0, vb1)
    for j in range(len(tiles)):
        if loads and j > 0:
            copies[j - 1].wait()
        project(j, bufs[j % 2])
        if j == 0:
            maps()
        else:
            finish(j - 1, bufs[(j - 1) % 2])
    finish(len(tiles) - 1, bufs[(len(tiles) - 1) % 2])
    if not loads:
        copies[0].wait()


def inside_kernel(
    head_width, tok, gw, b_rows, c_rows, vc, mid, dtt, cum, cumt, rise_in, sel_a, sel_b, skip,
    *refs,
):
    part_out, grow_out, scores, gb0, gb1 = refs[-5:]
    rows, inner = vc.shape
    tiles = pieces(inner, TILE)
    spans = pieces(rows)
    r = lax.broadcasted_iota(jnp.int32, (CHUNK, CHUNK), 0)
    s = lax.broadcasted_iota(jnp.int32, (CHUNK, CHUNK), 1)
    wide = 2 * head_width
    lane = lax.broadcasted_iota(jnp.int32, (CHUNK, wide), 1)
    flat = lane[:1]

    def project(j, buf):
        buf[...] = mm(tok[...], gw[:, tiles[j]]).astype(BF16)

    def score():
        for q, span in enumerate(spans):
            scores[q] = jnp.where(r >= s, mm_t(c_rows[span, :], b_rows[span, :]), 0.0)

    def finish(j, buf):
        tile = tiles[j]
        for q, span in enumerate(spans):
            rise = mm(rise_in[span, :], sel_a[:, tile])
            full = mm(rise_in[span, :], sel_b[:, tile])
            swish = silu(buf[span, :].astype(F32))
            grow_out[span, tile] = (swish * full).astype(BF16)
            if q > 0:
                carried = mm(c_rows[span, :], mid[q - 1, :, tile]) * rise
            for cut in pieces(TILE, wide):
                at = slice(tile.start + cut.start, tile.start + cut.stop)
                first = at.start // head_width
                block = vc[span, at]
                mixes, halves = [], []
                for k in range(2):
                    head = first + k
                    gap = jnp.minimum(
                        cum[span, head : head + 1] - cumt[q, head : head + 1, :], 0.0
                    )
                    mixes.append(
                        (scores[q] * jnp.exp2(gap) * dtt[q, head : head + 1, :]).astype(BF16)
                    )
                    halves.append(
                        jnp.where((lane >= head_width) == (k == 1), block, jnp.zeros_like(block))
                    )
                mixture = mm(jnp.concatenate(mixes, axis=1), jnp.concatenate(halves, axis=0))
                gain = jnp.where(flat < head_width, skip[first], skip[first + 1])
                mixture = mixture + gain * block.astype(F32)
                if q > 0:
                    mixture = mixture + carried[:, cut]
                part_out[span, at] = mixture * swish[:, cut]

    bufs = (gb0, gb1)
    for j in range(len(tiles)):
        project(j, bufs[j % 2])
        if j == 0:
            score()
        else:
            finish(j - 1, bufs[(j - 1) % 2])
    finish(len(tiles) - 1, bufs[(len(tiles) - 1) % 2])


def gather_owned(owners, axis, refs, held):
    spot = lax.rem(lax.axis_index(axis), owners)
    for k in range(owners):
        held[jnp.bitwise_xor(spot, k)] = refs[k][...]


def total_kernel(owners, axis, *refs):
    came, sel = refs[:owners], refs[owners]
    total_out, decay_out, held, lines = refs[-4:]
    gather_owned(owners, axis, came, held)
    width = total_out.shape[1]
    lines[...] = jnp.zeros_like(lines)
    for k in range(owners):
        lines[pl.ds(k, 1), :] = held[k, :, width:].astype(F32)[:1]
    decay_out[...] = mm(lines[...].astype(BF16), sel[...])
    state = held[0, :, :width].astype(F32)
    for k in range(1, owners):
        state = state * decay_out[pl.ds(k, 1), :] + held[k, :, :width].astype(F32)
    total_out[...] = state.astype(BF16)


def prefix_kernel(owners, axis, *refs):
    came = refs[:owners]
    decay, first = refs[owners : owners + 2]
    outs = refs[-owners - 2 : -2]
    held, made = refs[-2:]
    gather_owned(owners, axis, came, held)
    width = first.shape[1]
    state = first[...].astype(F32)
    for k in range(owners):
        made[k] = state.astype(BF16)
        if k + 1 < owners:
            state = state * decay[pl.ds(k, 1), :] + held[k, :, :width].astype(F32)
    spot = lax.rem(lax.axis_index(axis), owners)
    for k in range(owners):
        outs[k][...] = made[jnp.bitwise_xor(spot, k)]


def enter_kernel(owners, axis, part, grow, c_rows, *refs):
    came = refs[:owners]
    out, sq_out, state = refs[-3:]
    rows, inner = part.shape
    share = came[0].shape[0]
    spot = lax.rem(lax.axis_index(axis), owners)
    for k in range(owners):
        at = pl.multiple_of(jnp.bitwise_xor(spot, k) * share, share)
        state[pl.ds(at, share), :] = came[k][...]
    for span in pieces(rows):
        acc = jnp.zeros((CHUNK, LANES), F32)
        for at in pieces(inner, TILE):
            extra = mm(c_rows[span, :], state[:, at])
            total = part[span, at] + grow[span, at].astype(F32) * extra
            out[span, at] = total
            for cut in pieces(TILE, LANES):
                acc = acc + total[:, cut] * total[:, cut]
        sq_out[:, span] = jnp.sum(acc.T, axis=0, keepdims=True)


def norm_kernel(inner_all, count, *refs):
    squares = refs[:count]
    x, gain = refs[count : count + 2]
    out = refs[-1]
    rows = out.shape[1]
    q = pl.program_id(0)
    span = pl.ds(pl.multiple_of(q * rows, rows), rows)
    total = squares[0][:, span]
    for ref in squares[1:]:
        total = total + ref[:, span]
    inverse = lax.rsqrt(total / inner_all + EPS)
    columns = jnp.broadcast_to(inverse, (LANES, rows)).T
    gains = row(gain)
    for cut in pieces(out.shape[2], LANES):
        out[0, :, cut] = (x[span, cut] * columns * gains[:, cut]).astype(BF16)


def local(
    tokens,
    gate_weight,
    value_weight,
    state_weight,
    step_weight,
    value_kernel,
    value_offset,
    state_kernel,
    state_offset,
    step_offset,
    decay_rate,
    skip_gain,
    norm_gain,
):
    b, t, d = tokens.shape
    inner = gate_weight.shape[1]
    h = step_weight.shape[1]
    n = state_weight.shape[1] // 2
    head_width = inner // h
    peers = lax.axis_size("seq")
    ranks = lax.axis_size("head")
    owners = peers // 2
    share = n // owners
    chunks = t // CHUNK
    assert h <= SLOT and owners * 2 == peers and owners & (owners - 1) == 0
    assert chunks < 16 and value_kernel.shape[0] == 4
    lines = max(owners, 8)

    def swap(arrays):
        return [arrays[0]] + [
            here(lax.ppermute(arrays[k], "seq", [(s, s ^ k) for s in range(peers)]))
            for k in range(1, owners)
        ]

    halo = here(
        lax.ppermute(tokens[:, t - PAD :], "seq", [(s, s + 1) for s in range(peers - 1)])
    )
    outs = pl.pallas_call(
        functools.partial(front_kernel, head_width),
        in_specs=[FAR] * 6,
        out_specs=[WHOLE] * (4 + 8 * b),
        out_shape=[
            pltpu.VMEM(state_weight.shape, BF16),
            pltpu.VMEM((d, TILE), BF16),
            pltpu.VMEM((LANES, inner), BF16),
            pltpu.VMEM((LANES, inner), BF16),
        ]
        + [
            pltpu.VMEM((t, d), BF16),
            pltpu.VMEM((t, 2 * n), BF16),
            pltpu.VMEM((t, LANES), BF16),
            pltpu.VMEM((t, LANES), BF16),
            pltpu.VMEM((16, LANES), BF16),
            pltpu.VMEM((t, LANES), F32),
            pltpu.VMEM((chunks, SLOT, CHUNK), F32),
            pltpu.VMEM((chunks, SLOT, CHUNK), F32),
        ]
        * b,
        scratch_shapes=[
            pltpu.VMEM((h, d), BF16),
            pltpu.VMEM((h,), F32),
            pltpu.VMEM((h,), F32),
            pltpu.VMEM((LANES, d), BF16),
            pltpu.VMEM((8, LANES), F32),
            pltpu.SemaphoreType.DMA((b + 5,)),
        ],
        compiler_params=params(16),
        name="front",
        cost_estimate=cost(2 * b * t * d * (2 * n + LANES)),
    )(*map(far, (tokens, state_weight, step_weight.T, value_weight, step_offset, decay_rate)))
    sw, w0, sel_a, sel_b = outs[:4]
    fronts = [outs[4 + 8 * i : 12 + 8 * i] for i in range(b)]

    def values(i, rest):
        tok, io, close, _, thr, _, _, _ = fronts[i]
        extra = [(d, inner - TILE)] if i == 0 else [(d, inner)] if i == 1 else []
        assert i < 2
        args = (far(value_weight),) if i == 0 else (rest, far(gate_weight))
        return pl.pallas_call(
            functools.partial(values_kernel, owners, "seq", i, i == 0),
            in_specs=[WHOLE] * 12 + ([FAR] if i == 0 else [WHOLE, FAR]),
            out_specs=[WHOLE] * (5 + owners),
            out_shape=[
                pltpu.VMEM((t, inner), BF16),
                pltpu.VMEM((chunks - 1, n, inner), BF16),
                pltpu.VMEM((t, n), BF16),
                pltpu.VMEM((t, n), BF16),
                pltpu.VMEM(extra[0], BF16),
            ]
            + [pltpu.VMEM((share, inner + LANES), BF16)] * owners,
            scratch_shapes=[
                pltpu.VMEM((n, t), BF16),
                pltpu.VMEM((t + PAD, 2 * n), F32),
                pltpu.VMEM((n, TILE), F32),
                pltpu.VMEM((t + PAD, TILE), F32),
                pltpu.VMEM((t + PAD, TILE), F32),
                pltpu.SemaphoreType.DMA((inner // TILE,)),
            ],
            compiler_params=params(16),
            name=f"values{i}",
            cost_estimate=cost(2 * t * d * inner),
        )(
            tok, halo, w0, sw, value_kernel, value_offset, state_kernel, state_offset,
            io, close, thr, sel_a, *args,
        )

    def inside(i, gw, made, after):
        tok, _, _, rise, _, cum, cumt, dtt = fronts[i]
        vc, mid, b_rows, c_rows = made[:4]
        return pl.pallas_call(
            functools.partial(inside_kernel, head_width),
            in_specs=[WHOLE] * 12 + [SCALARS] + [WHOLE] * len(after),
            out_specs=[WHOLE] * 2,
            out_shape=[pltpu.VMEM((t, inner), F32), pltpu.VMEM((t, inner), BF16)],
            scratch_shapes=[
                pltpu.VMEM((chunks, CHUNK, CHUNK), F32),
                pltpu.VMEM((t, TILE), BF16),
                pltpu.VMEM((t, TILE), BF16),
            ],
            compiler_params=params(16),
            name=f"inside{i}",
            cost_estimate=cost(2.5 * t * d * inner),
        )(tok, gw, b_rows, c_rows, vc, mid, dtt, cum, cumt, rise, sel_a, sel_b, skip_gain, *after)

    def total(i, came, after):
        return pl.pallas_call(
            functools.partial(total_kernel, owners, "seq"),
            in_specs=[WHOLE] * (owners + 1 + len(after)),
            out_specs=[WHOLE] * 2,
            out_shape=[pltpu.VMEM((share, inner), BF16), pltpu.VMEM((lines, inner), F32)],
            scratch_shapes=[
                pltpu.VMEM((owners, share, inner + LANES), BF16),
                pltpu.VMEM((lines, LANES), F32),
            ],
            compiler_params=params(16),
            name=f"total{i}",
        )(*came, sel_a, *after)

    def prefix(i, came, decay, first, after):
        return pl.pallas_call(
            functools.partial(prefix_kernel, owners, "seq"),
            in_specs=[WHOLE] * (owners + 2 + len(after)),
            out_specs=[WHOLE] * owners,
            out_shape=[pltpu.VMEM((share, inner), BF16)] * owners,
            scratch_shapes=[
                pltpu.VMEM((owners, share, inner + LANES), BF16),
                pltpu.VMEM((owners, share, inner), BF16),
            ],
            compiler_params=params(16),
            name=f"prefix{i}",
        )(*came, decay, first, *after)

    def across(x):
        return here(lax.ppermute(x, "seq", [(s, s + owners) for s in range(owners)]))

    def enter(i, part, grow, c_rows, states, after):
        x, sq = pl.pallas_call(
            functools.partial(enter_kernel, owners, "seq"),
            in_specs=[WHOLE] * (3 + owners) + [FAR] * len(after),
            out_specs=[WHOLE] * 2,
            out_shape=[pltpu.VMEM((t, inner), F32), pltpu.VMEM((1, t), F32)],
            scratch_shapes=[pltpu.VMEM((n, inner), BF16)],
            compiler_params=params(16),
            name=f"enter{i}",
        )(part, grow, c_rows, *states, *after)
        return x, [sq] + [
            here(lax.ppermute(sq, "head", [(s, (s + k) % ranks) for s in range(ranks)]))
            for k in range(1, ranks)
        ]

    def norm(i, x, squares, into):
        rows = min(t, 256)
        return pl.pallas_call(
            functools.partial(norm_kernel, inner * ranks, ranks),
            grid=(t // rows,),
            in_specs=[WHOLE] * (ranks + 2) + [FAR] * len(into),
            out_specs=pl.BlockSpec((1, rows, inner), lambda q: (i, q, 0)),
            out_shape=jax.ShapeDtypeStruct((b, t, inner), BF16),
            input_output_aliases={ranks + 2: 0} if into else {},
            compiler_params=params(16),
            name=f"norm{i}",
        )(*squares, x, norm_gain, *into)

    made0 = values(0, None)
    came0 = swap(made0[5:])
    made1 = values(1, made0[4])
    gw = made1[4]
    came1 = swap(made1[5:])
    total0, decay0 = total(0, came0, (made1[2],))
    first0 = across(total0)
    part0, grow0 = inside(0, gw, made0, (total0,))
    total1, decay1 = total(1, came1, (grow0,))
    first1 = across(total1)
    enter0 = prefix(0, came0, decay0, first0, (grow0,))
    back0 = swap(enter0)
    part1, grow1 = inside(1, gw, made1, (enter0[1],))
    back1 = swap(prefix(1, came1, decay1, first1, (grow1,)))
    x0, squares0 = enter(0, part0, grow0, made0[3], back0, ())
    out = norm(0, x0, squares0, ())
    x1, squares1 = enter(1, part1, grow1, made1[3], back1, (out,))
    return norm(1, x1, squares1, (out,))


def solution(mesh):
    return jax.shard_map(
        local,
        mesh=mesh,
        in_specs=(
            P(None, "seq", None),
            P(None, "head"),
            P(None, "head"),
            P(),
            P(None, "head"),
            P(None, "head"),
            P("head"),
            P(),
            P(),
            P("head"),
            P("head"),
            P("head"),
            P("head"),
        ),
        out_specs=P(None, "seq", "head"),
        check_vma=False,
    )
```

```python
import functools
import jax
import jax.numpy as jnp
from jax import lax
from jax.experimental import pallas as pl
from jax.experimental.pallas import tpu as pltpu
from jax.sharding import PartitionSpec as P

EPS = 1e-05
LOG2E = 1.4426950408889634
PAD = 16
CHUNK = 128
TILE = 256
LANES = 128
SLOT = 32
F32 = jnp.float32
BF16 = jnp.bfloat16
WHOLE = pl.BlockSpec(memory_space=pltpu.VMEM)
FAR = pl.BlockSpec(memory_space=pltpu.HBM)
SCALARS = pl.BlockSpec(memory_space=pltpu.SMEM)


def here(x):
    return pltpu.with_memory_space_constraint(x, pltpu.VMEM)


def far(x):
    return pltpu.with_memory_space_constraint(x, pltpu.HBM)


def params(mib):
    return pltpu.CompilerParams(vmem_limit_bytes=mib << 20)


def cost(flops):
    return pl.CostEstimate(flops=int(flops), transcendentals=0, bytes_accessed=0)


def mm(a, b):
    return jnp.dot(a, b, preferred_element_type=F32)


def mm_t(a, b):
    return lax.dot_general(a, b, (((1,), (1,)), ((), ())), preferred_element_type=F32)


def silu(x):
    half = 0.5 * x
    return half + half * jnp.tanh(half)


def row(ref):
    return ref[...].reshape(1, ref.shape[0])


def pieces(total, size=CHUNK):
    return [slice(k * size, (k + 1) * size) for k in range(total // size)]


def head_select(width, head_width, group):
    lane = lax.broadcasted_iota(jnp.int32, (LANES, width), 0) - 2 * SLOT * group
    col = lax.broadcasted_iota(jnp.int32, (LANES, width), 1)
    start = (lane & (SLOT - 1)) * head_width
    hit = (lane >= 0) & (lane < 2 * SLOT) & (col >= start) & (col < start + head_width)
    return jnp.where(hit, 1.0, 0.0).astype(BF16)


def conv_of(x, kernel, offset):
    back = pltpu.roll(x, 1, 0)
    near = offset + kernel[3:4] * x + kernel[2:3] * back
    deep = kernel[1:2] * x + kernel[0:1] * back
    return silu((near + pltpu.roll(deep, 2, 0))[PAD:]).astype(BF16)


def front_kernel(head_width, *refs):
    tok_in, sw_in, twt_in, w_in, toff_in, rate_in = refs[:6]
    batch = tok_in.shape[0]
    sw, w, sel = refs[6:9]
    per_batch = [refs[9 + 7 * i : 16 + 7 * i] for i in range(batch)]
    twt, toff, rate, tws, vec, sem = refs[9 + 7 * batch :]
    rows = tok_in.shape[1]
    heads = twt.shape[0]
    token_copies = [
        pltpu.make_async_copy(tok_in.at[i], per_batch[i][0], sem.at[i]) for i in range(batch)
    ]
    copies = [
        pltpu.make_async_copy(twt_in, twt, sem.at[batch]),
        pltpu.make_async_copy(toff_in, toff, sem.at[batch + 1]),
        pltpu.make_async_copy(rate_in, rate, sem.at[batch + 2]),
        pltpu.make_async_copy(sw_in, sw, sem.at[batch + 3]),
        pltpu.make_async_copy(w_in, w, sem.at[batch + 4]),
    ]
    for copy in copies[:3] + [token_copies[0], copies[3]] + token_copies[1:] + [copies[4]]:
        copy.start()
    sel[...] = head_select(sel.shape[1], head_width, 0)
    for copy in copies[:3]:
        copy.wait()
    tws[...] = jnp.zeros_like(tws)
    vec[...] = jnp.zeros_like(vec)
    for g in range(LANES // SLOT):
        tws[pl.ds(g * SLOT, heads), :] = twt[...]
        vec[pl.ds(0, 1), pl.ds(g * SLOT, heads)] = row(toff)
        vec[pl.ds(1, 1), pl.ds(g * SLOT, heads)] = row(rate)
    offset = vec[pl.ds(0, 1), :]
    scale = vec[pl.ds(1, 1), :] * (-LOG2E)
    r = lax.broadcasted_iota(jnp.int32, (CHUNK, CHUNK), 0)
    c = lax.broadcasted_iota(jnp.int32, (CHUNK, CHUNK), 1)
    tri = jnp.where(r >= c, 1.0, 0.0).astype(BF16)
    group = lax.broadcasted_iota(jnp.int32, (1, LANES), 1) // SLOT
    low_lane = (group & 1) == 1

    def parts(x):
        hi = x.astype(BF16).astype(F32)
        return jnp.where(low_lane, x - hi, hi).astype(BF16)

    for i in range(batch):
        tok, io_out, close_out, thr_out, cum_out, cumt_out, dtt_out = per_batch[i]
        token_copies[i].wait()
        if i == 0:
            copies[3].wait()
        x = tok[...]
        io_out[...] = mm(x, sw[...]).astype(BF16)
        z = mm_t(x, tws[...]) + offset
        dt = jnp.maximum(z, 0.0) + jnp.log1p(jnp.exp(-jnp.abs(z)))
        log_decay = dt * scale
        base = jnp.zeros((1, LANES), F32)
        lasts, bases = [], []
        for q, span in enumerate(pieces(rows)):
            part = log_decay[span]
            hi = part.astype(BF16)
            rest = part - hi.astype(F32)
            mid = rest.astype(BF16)
            low = (rest - mid.astype(F32)).astype(BF16)
            cum = mm(tri, hi) + (mm(tri, mid) + mm(tri, low))
            last = cum[CHUNK - 1 :]
            cum_out[span, :] = cum
            cumt_out[q] = cum.T[:SLOT]
            dtt_out[q] = dt[span].T[:SLOT]
            close_out[span, :] = parts(jnp.exp2(last - cum) * dt[span])
            lasts.append(last)
            bases.append(base)
            base = base + last
        zero = [jnp.zeros((1, LANES), F32)]
        table = lasts + [base] + zero * (7 - len(lasts)) + bases + zero * (8 - len(bases))
        thr_out[...] = parts(jnp.exp2(jnp.concatenate(table, axis=0)))
    copies[4].wait()


def values_kernel(owners, axis, index, loads, *refs):
    tok, halo, w, sw, vkern, voff, skern, soff, io, close, thr, sel = refs[:12]
    refs = refs[12:]
    if loads:
        gate_in, gw = refs[0], refs[5]
        refs = refs[:5] + refs[6:]
        refs = refs[1:]
    vc_out, mid_out, b_out, c_out = refs[:4]
    refs = refs[4:]
    ends, (bt, mbuf, hold, vb0, vb1, sem) = refs[:owners], refs[owners:]
    rows = tok.shape[0]
    inner = vc_out.shape[1]
    n = b_out.shape[1]
    share = n // owners
    spot = lax.rem(lax.axis_index(axis), owners)
    tiles = pieces(inner, TILE)
    if loads:
        copy = pltpu.make_async_copy(gate_in, gw, sem)
        copy.start()
    rim = halo[index]
    offset = row(voff)

    def project(j, buf):
        x = jnp.concatenate([rim, tok[...]], axis=0)
        buf[...] = mm(x, w[:, tiles[j]]).astype(BF16).astype(F32)

    def maps():
        mbuf[pl.ds(0, PAD), :] = mm(rim, sw[...]).astype(BF16).astype(F32)
        mbuf[pl.ds(PAD, rows), :] = io[...].astype(F32)
        y = conv_of(mbuf[...], skern[...], row(soff))
        b_out[...] = y[:, :n]
        c_out[...] = y[:, n:]
        bt[...] = y[:, :n].astype(F32).T.astype(BF16)

    def finish(j, buf):
        at = tiles[j]
        vc = conv_of(buf[...], vkern[:, at], offset[:, at])
        vc_out[:, at] = vc
        select = sel[:, at]
        through = mm(thr[...], select)
        state = None
        for q, span in enumerate(pieces(rows)):
            scaled = (vc[span].astype(F32) * mm(close[span, :], select)).astype(BF16)
            made = mm(bt[:, span], scaled)
            if q == 0:
                state = made
            else:
                mid_out[q - 1, :, at] = state.astype(BF16)
                state = state * through[q : q + 1] + made
        hold[...] = state
        for k in range(owners):
            owner = jnp.bitwise_xor(spot, k)
            part = hold[pl.ds(pl.multiple_of(owner * share, share), share), :]
            ends[k][:, at] = part.astype(BF16)

    line = lax.broadcasted_iota(jnp.int32, (share, LANES), 0)
    count = rows // CHUNK
    mine = jnp.broadcast_to(thr[...].astype(F32)[count : count + 1], (share, LANES))
    decays = jnp.where(line == 0, mine, 0.0).astype(BF16)
    for k in range(owners):
        ends[k][:, inner:] = decays
    bufs = (vb0, vb1)
    for j in range(len(tiles)):
        project(j, bufs[j % 2])
        if j == 0:
            maps()
        else:
            finish(j - 1, bufs[(j - 1) % 2])
    finish(len(tiles) - 1, bufs[(len(tiles) - 1) % 2])
    if loads:
        copy.wait()


def inside_kernel(
    head_width, tok, gw, b_rows, c_rows, vc, mid, dtt, cum, cumt, thr, sel, skip,
    *refs,
):
    part_out, grow_out, scores, gb0, gb1 = refs[-5:]
    rows, inner = vc.shape
    tiles = pieces(inner, TILE)
    spans = pieces(rows)
    r = lax.broadcasted_iota(jnp.int32, (CHUNK, CHUNK), 0)
    s = lax.broadcasted_iota(jnp.int32, (CHUNK, CHUNK), 1)
    wide = 2 * head_width
    assert wide == CHUNK
    lane = lax.broadcasted_iota(jnp.int32, (CHUNK, wide), 1)
    flat = lane[:1]

    def project(j, buf):
        buf[...] = mm(tok[...], gw[:, tiles[j]]).astype(BF16)

    def score():
        for q, span in enumerate(spans):
            scores[q] = jnp.where(r >= s, mm_t(c_rows[span, :], b_rows[span, :]), 0.0)

    def finish(j, buf):
        tile = tiles[j]
        base = mm(thr[...], sel[:, tile])
        for q, span in enumerate(spans):
            swish = silu(buf[span, :].astype(F32))
            if q > 0:
                carried = mm(c_rows[span, :], mid[q - 1, :, tile])
            for cut in pieces(TILE, wide):
                at = slice(tile.start + cut.start, tile.start + cut.stop)
                first = at.start // head_width
                block = vc[span, at]
                mixes, halves, columns = [], [], []
                for k in range(2):
                    head = first + k
                    column = jnp.broadcast_to(cum[span, head : head + 1], (CHUNK, CHUNK))
                    columns.append(column)
                    gap = jnp.minimum(column - cumt[q, head : head + 1, :], 0.0)
                    mixes.append(
                        (scores[q] * jnp.exp2(gap) * dtt[q, head : head + 1, :]).astype(BF16)
                    )
                    halves.append(
                        jnp.where((lane >= head_width) == (k == 1), block, jnp.zeros_like(block))
                    )
                mixture = mm(jnp.concatenate(mixes, axis=1), jnp.concatenate(halves, axis=0))
                gain = jnp.where(flat < head_width, skip[first], skip[first + 1])
                mixture = mixture + gain * block.astype(F32)
                rise = jnp.exp2(jnp.where(lane < head_width, columns[0], columns[1]))
                gated = swish[:, cut] * rise
                if q > 0:
                    mixture = mixture + carried[:, cut] * rise
                    gated = gated * base[8 + q : 9 + q, cut]
                grow_out[span, at] = gated.astype(BF16)
                part_out[span, at] = mixture * swish[:, cut]

    bufs = (gb0, gb1)
    for j in range(len(tiles)):
        project(j, bufs[j % 2])
        if j == 0:
            score()
        else:
            finish(j - 1, bufs[(j - 1) % 2])
    finish(len(tiles) - 1, bufs[(len(tiles) - 1) % 2])


def gather_owned(owners, axis, refs, held):
    spot = lax.rem(lax.axis_index(axis), owners)
    for k in range(owners):
        held[jnp.bitwise_xor(spot, k)] = refs[k][...]


def total_kernel(owners, axis, *refs):
    came, sel = refs[:owners], refs[owners]
    total_out, decay_out, held, lines = refs[-4:]
    gather_owned(owners, axis, came, held)
    width = total_out.shape[1]
    lines[...] = jnp.zeros_like(lines)
    for k in range(owners):
        lines[pl.ds(k, 1), :] = held[k, :, width:].astype(F32)[:1]
    decay_out[...] = mm(lines[...].astype(BF16), sel[...])
    state = held[0, :, :width].astype(F32)
    for k in range(1, owners):
        state = state * decay_out[pl.ds(k, 1), :] + held[k, :, :width].astype(F32)
    total_out[...] = state.astype(BF16)


def prefix_kernel(owners, axis, *refs):
    came = refs[:owners]
    decay, first = refs[owners : owners + 2]
    outs = refs[-owners - 2 : -2]
    held, made = refs[-2:]
    gather_owned(owners, axis, came, held)
    width = first.shape[1]
    state = first[...].astype(F32)
    for k in range(owners):
        made[k] = state.astype(BF16)
        if k + 1 < owners:
            state = state * decay[pl.ds(k, 1), :] + held[k, :, :width].astype(F32)
    spot = lax.rem(lax.axis_index(axis), owners)
    for k in range(owners):
        outs[k][...] = made[jnp.bitwise_xor(spot, k)]


def enter_kernel(owners, axis, index, part, grow, c_rows, *refs):
    came = refs[:owners]
    out, sq_out, state = refs[-3:]
    rows, inner = part.shape
    share = came[0].shape[0]
    if index:
        sq_out[:, : index * rows] = refs[owners][...]
    spot = lax.rem(lax.axis_index(axis), owners)
    for k in range(owners):
        at = pl.multiple_of(jnp.bitwise_xor(spot, k) * share, share)
        state[pl.ds(at, share), :] = came[k][...]
    for span in pieces(rows):
        acc = jnp.zeros((CHUNK, LANES), F32)
        for at in pieces(inner, TILE):
            extra = mm(c_rows[span, :], state[:, at])
            total = part[span, at] + grow[span, at].astype(F32) * extra
            out[span, at] = total
            for cut in pieces(TILE, LANES):
                acc = acc + total[:, cut] * total[:, cut]
        at = slice(index * rows + span.start, index * rows + span.stop)
        sq_out[:, at] = jnp.sum(acc.T, axis=0, keepdims=True)


def norm_kernel(inner_all, count, *refs):
    squares, xs = refs[:count], refs[count:-2]
    gain, out = refs[-2:]
    rows = out.shape[1]
    i, q = pl.program_id(0), pl.program_id(1)
    span = pl.ds(pl.multiple_of(q * rows, rows), rows)
    at = pl.ds(pl.multiple_of((i * pl.num_programs(1) + q) * rows, rows), rows)
    total = squares[0][:, at]
    for ref in squares[1:]:
        total = total + ref[:, at]
    inverse = lax.rsqrt(total / inner_all + EPS)
    columns = jnp.broadcast_to(inverse, (LANES, rows)).T
    gains = row(gain)
    for k, x in enumerate(xs):

        @pl.when(i == k)
        def _():
            for cut in pieces(out.shape[2], LANES):
                out[0, :, cut] = (x[span, cut] * columns * gains[:, cut]).astype(BF16)


def local(
    tokens,
    gate_weight,
    value_weight,
    state_weight,
    step_weight,
    value_kernel,
    value_offset,
    state_kernel,
    state_offset,
    step_offset,
    decay_rate,
    skip_gain,
    norm_gain,
):
    b, t, d = tokens.shape
    inner = gate_weight.shape[1]
    h = step_weight.shape[1]
    n = state_weight.shape[1] // 2
    head_width = inner // h
    peers = lax.axis_size("seq")
    ranks = lax.axis_size("head")
    owners = peers // 2
    share = n // owners
    chunks = t // CHUNK
    assert h <= SLOT and owners * 2 == peers and owners & (owners - 1) == 0
    assert b == 2 and chunks < 8 and value_kernel.shape[0] == 4
    lines = max(owners, 8)

    def swap(arrays):
        return [arrays[0]] + [
            here(lax.ppermute(arrays[k], "seq", [(s, s ^ k) for s in range(peers)]))
            for k in range(1, owners)
        ]

    halo = here(
        lax.ppermute(tokens[:, t - PAD :], "seq", [(s, s + 1) for s in range(peers - 1)])
    )
    outs = pl.pallas_call(
        functools.partial(front_kernel, head_width),
        in_specs=[FAR] * 6,
        out_specs=[WHOLE] * (3 + 7 * b),
        out_shape=[
            pltpu.VMEM(state_weight.shape, BF16),
            pltpu.VMEM(value_weight.shape, BF16),
            pltpu.VMEM((LANES, inner), BF16),
        ]
        + [
            pltpu.VMEM((t, d), BF16),
            pltpu.VMEM((t, 2 * n), BF16),
            pltpu.VMEM((t, LANES), BF16),
            pltpu.VMEM((16, LANES), BF16),
            pltpu.VMEM((t, LANES), F32),
            pltpu.VMEM((chunks, SLOT, CHUNK), F32),
            pltpu.VMEM((chunks, SLOT, CHUNK), F32),
        ]
        * b,
        scratch_shapes=[
            pltpu.VMEM((h, d), BF16),
            pltpu.VMEM((h,), F32),
            pltpu.VMEM((h,), F32),
            pltpu.VMEM((LANES, d), BF16),
            pltpu.VMEM((8, LANES), F32),
            pltpu.SemaphoreType.DMA((b + 5,)),
        ],
        compiler_params=params(16),
        name="front",
        cost_estimate=cost(2 * b * t * d * (2 * n + LANES)),
    )(*map(far, (tokens, state_weight, step_weight.T, value_weight, step_offset, decay_rate)))
    sw, w, sel = outs[:3]
    fronts = [outs[3 + 7 * i : 10 + 7 * i] for i in range(b)]

    def values(i):
        tok, io, close, thr, _, _, _ = fronts[i]
        loads = i == b - 1
        return pl.pallas_call(
            functools.partial(values_kernel, owners, "seq", i, loads),
            in_specs=[WHOLE] * 12 + [FAR] * loads,
            out_specs=[WHOLE] * (4 + loads + owners),
            out_shape=[
                pltpu.VMEM((t, inner), BF16),
                pltpu.VMEM((chunks - 1, n, inner), BF16),
                pltpu.VMEM((t, n), BF16),
                pltpu.VMEM((t, n), BF16),
            ]
            + [pltpu.VMEM(gate_weight.shape, BF16)] * loads
            + [pltpu.VMEM((share, inner + LANES), BF16)] * owners,
            scratch_shapes=[
                pltpu.VMEM((n, t), BF16),
                pltpu.VMEM((t + PAD, 2 * n), F32),
                pltpu.VMEM((n, TILE), F32),
                pltpu.VMEM((t + PAD, TILE), F32),
                pltpu.VMEM((t + PAD, TILE), F32),
                pltpu.SemaphoreType.DMA,
            ],
            compiler_params=params(16),
            name=f"values{i}",
            cost_estimate=cost(2 * t * d * inner),
        )(
            tok, halo, w, sw, value_kernel, value_offset, state_kernel, state_offset,
            io, close, thr, sel, *[far(gate_weight)] * loads,
        )

    def inside(i, gw, made, after):
        tok, _, _, thr, cum, cumt, dtt = fronts[i]
        vc, mid, b_rows, c_rows = made[:4]
        return pl.pallas_call(
            functools.partial(inside_kernel, head_width),
            in_specs=[WHOLE] * 11 + [SCALARS] + [WHOLE] * len(after),
            out_specs=[WHOLE] * 2,
            out_shape=[pltpu.VMEM((t, inner), F32), pltpu.VMEM((t, inner), BF16)],
            scratch_shapes=[
                pltpu.VMEM((chunks, CHUNK, CHUNK), F32),
                pltpu.VMEM((t, TILE), BF16),
                pltpu.VMEM((t, TILE), BF16),
            ],
            compiler_params=params(16),
            name=f"inside{i}",
            cost_estimate=cost(2.5 * t * d * inner),
        )(tok, gw, b_rows, c_rows, vc, mid, dtt, cum, cumt, thr, sel, skip_gain, *after)

    def total(i, came, after):
        return pl.pallas_call(
            functools.partial(total_kernel, owners, "seq"),
            in_specs=[WHOLE] * (owners + 1 + len(after)),
            out_specs=[WHOLE] * 2,
            out_shape=[pltpu.VMEM((share, inner), BF16), pltpu.VMEM((lines, inner), F32)],
            scratch_shapes=[
                pltpu.VMEM((owners, share, inner + LANES), BF16),
                pltpu.VMEM((lines, LANES), F32),
            ],
            compiler_params=params(16),
            name=f"total{i}",
        )(*came, sel, *after)

    def prefix(i, came, decay, first, after):
        return pl.pallas_call(
            functools.partial(prefix_kernel, owners, "seq"),
            in_specs=[WHOLE] * (owners + 2 + len(after)),
            out_specs=[WHOLE] * owners,
            out_shape=[pltpu.VMEM((share, inner), BF16)] * owners,
            scratch_shapes=[
                pltpu.VMEM((owners, share, inner + LANES), BF16),
                pltpu.VMEM((owners, share, inner), BF16),
            ],
            compiler_params=params(16),
            name=f"prefix{i}",
        )(*came, decay, first, *after)

    def across(x):
        return here(lax.ppermute(x, "seq", [(s, s + owners) for s in range(owners)]))

    def enter(i, part, grow, c_rows, states, before):
        return pl.pallas_call(
            functools.partial(enter_kernel, owners, "seq", i),
            in_specs=[WHOLE] * (3 + owners + len(before)),
            out_specs=[WHOLE] * 2,
            out_shape=[pltpu.VMEM((t, inner), F32), pltpu.VMEM((1, (i + 1) * t), F32)],
            scratch_shapes=[pltpu.VMEM((n, inner), BF16)],
            compiler_params=params(16),
            name=f"enter{i}",
        )(part, grow, c_rows, *states, *before)

    def norm(xs, squares):
        rows = min(t, 256)
        return pl.pallas_call(
            functools.partial(norm_kernel, inner * ranks, ranks),
            grid=(b, t // rows),
            in_specs=[WHOLE] * (ranks + b + 1),
            out_specs=pl.BlockSpec((1, rows, inner), lambda i, q: (i, q, 0)),
            out_shape=jax.ShapeDtypeStruct((b, t, inner), BF16),
            compiler_params=params(16),
            name="norm",
        )(*squares, *xs, norm_gain)

    made0 = values(0)
    came0 = swap(made0[4:])
    made1 = values(1)
    gw = made1[4]
    came1 = swap(made1[5:])
    total0, decay0 = total(0, came0, (made1[2],))
    first0 = across(total0)
    part0, grow0 = inside(0, gw, made0, (total0,))
    total1, decay1 = total(1, came1, (grow0,))
    first1 = across(total1)
    sent0 = prefix(0, came0, decay0, first0, (grow0,))
    back0 = swap(sent0)
    part1, grow1 = inside(1, gw, made1, (sent0[1],))
    back1 = swap(prefix(1, came1, decay1, first1, (grow1,)))
    x0, sq0 = enter(0, part0, grow0, made0[3], back0, ())
    x1, sq1 = enter(1, part1, grow1, made1[3], back1, (sq0,))
    squares = [sq1] + [
        here(lax.ppermute(sq1, "head", [(s, (s + k) % ranks) for s in range(ranks)]))
        for k in range(1, ranks)
    ]
    return norm((x0, x1), squares)


def solution(mesh):
    return jax.shard_map(
        local,
        mesh=mesh,
        in_specs=(
            P(None, "seq", None),
            P(None, "head"),
            P(None, "head"),
            P(),
            P(None, "head"),
            P(None, "head"),
            P("head"),
            P(),
            P(),
            P("head"),
            P("head"),
            P("head"),
            P("head"),
        ),
        out_specs=P(None, "seq", "head"),
        check_vma=False,
    )
```

```python
import functools
import jax
import jax.numpy as jnp
from jax import lax
from jax.experimental import pallas as pl
from jax.experimental.pallas import tpu as pltpu
from jax.sharding import PartitionSpec as P

EPS = 1e-05
LOG2E = 1.4426950408889634
PAD = 16
CHUNK = 128
TILE = 256
LANES = 128
SLOT = 32
F32 = jnp.float32
BF16 = jnp.bfloat16
WHOLE = pl.BlockSpec(memory_space=pltpu.VMEM)
FAR = pl.BlockSpec(memory_space=pltpu.HBM)
SCALARS = pl.BlockSpec(memory_space=pltpu.SMEM)


def here(x):
    return pltpu.with_memory_space_constraint(x, pltpu.VMEM)


def far(x):
    return pltpu.with_memory_space_constraint(x, pltpu.HBM)


def params(mib):
    return pltpu.CompilerParams(vmem_limit_bytes=mib << 20)


def cost(flops):
    return pl.CostEstimate(flops=int(flops), transcendentals=0, bytes_accessed=0)


def mm(a, b):
    return jnp.dot(a, b, preferred_element_type=F32)


def mm_t(a, b):
    return lax.dot_general(a, b, (((1,), (1,)), ((), ())), preferred_element_type=F32)


def silu(x):
    half = 0.5 * x
    return half + half * jnp.tanh(half)


def row(ref):
    return ref[...].reshape(1, ref.shape[0])


def pieces(total, size=CHUNK):
    return [slice(k * size, (k + 1) * size) for k in range(total // size)]


def head_select(width, head_width, group):
    lane = lax.broadcasted_iota(jnp.int32, (LANES, width), 0) - 2 * SLOT * group
    col = lax.broadcasted_iota(jnp.int32, (LANES, width), 1)
    start = (lane & (SLOT - 1)) * head_width
    hit = (lane >= 0) & (lane < 2 * SLOT) & (col >= start) & (col < start + head_width)
    return jnp.where(hit, 1.0, 0.0).astype(BF16)


def conv_of(x, kernel, offset):
    back = pltpu.roll(x, 1, 0)
    near = offset + kernel[3:4] * x + kernel[2:3] * back
    deep = kernel[1:2] * x + kernel[0:1] * back
    return silu((near + pltpu.roll(deep, 2, 0))[PAD:]).astype(BF16)


def front_kernel(head_width, *refs):
    tok_in, sw_in, twt_in, w_in, toff_in, rate_in = refs[:6]
    batch = tok_in.shape[0]
    sw, w, sel = refs[6:9]
    per_batch = [refs[9 + 7 * i : 16 + 7 * i] for i in range(batch)]
    twt, toff, rate, tws, vec, sem = refs[9 + 7 * batch :]
    rows = tok_in.shape[1]
    heads = twt.shape[0]
    token_copies = [
        pltpu.make_async_copy(tok_in.at[i], per_batch[i][0], sem.at[i]) for i in range(batch)
    ]
    copies = [
        pltpu.make_async_copy(twt_in, twt, sem.at[batch]),
        pltpu.make_async_copy(toff_in, toff, sem.at[batch + 1]),
        pltpu.make_async_copy(rate_in, rate, sem.at[batch + 2]),
        pltpu.make_async_copy(sw_in, sw, sem.at[batch + 3]),
        pltpu.make_async_copy(w_in, w, sem.at[batch + 4]),
    ]
    for copy in copies[:3] + [token_copies[0], copies[3]] + token_copies[1:] + [copies[4]]:
        copy.start()
    sel[...] = head_select(sel.shape[1], head_width, 0)
    for copy in copies[:3]:
        copy.wait()
    tws[...] = jnp.zeros_like(tws)
    vec[...] = jnp.zeros_like(vec)
    for g in range(LANES // SLOT):
        tws[pl.ds(g * SLOT, heads), :] = twt[...]
        vec[pl.ds(0, 1), pl.ds(g * SLOT, heads)] = row(toff)
        vec[pl.ds(1, 1), pl.ds(g * SLOT, heads)] = row(rate)
    offset = vec[pl.ds(0, 1), :]
    scale = vec[pl.ds(1, 1), :] * (-LOG2E)
    r = lax.broadcasted_iota(jnp.int32, (CHUNK, CHUNK), 0)
    c = lax.broadcasted_iota(jnp.int32, (CHUNK, CHUNK), 1)
    tri = jnp.where(r >= c, 1.0, 0.0).astype(BF16)
    group = lax.broadcasted_iota(jnp.int32, (1, LANES), 1) // SLOT
    low_lane = (group & 1) == 1

    def parts(x):
        hi = x.astype(BF16).astype(F32)
        return jnp.where(low_lane, x - hi, hi).astype(BF16)

    for i in range(batch):
        tok, io_out, close_out, thr_out, cum_out, cumt_out, dtt_out = per_batch[i]
        token_copies[i].wait()
        if i == 0:
            copies[3].wait()
        x = tok[...]
        io_out[...] = mm(x, sw[...]).astype(BF16)
        z = mm_t(x, tws[...]) + offset
        dt = jnp.maximum(z, 0.0) + jnp.log1p(jnp.exp(-jnp.abs(z)))
        log_decay = dt * scale
        base = jnp.zeros((1, LANES), F32)
        lasts, bases = [], []
        for q, span in enumerate(pieces(rows)):
            part = log_decay[span]
            hi = part.astype(BF16)
            rest = part - hi.astype(F32)
            mid = rest.astype(BF16)
            low = (rest - mid.astype(F32)).astype(BF16)
            cum = mm(tri, hi) + (mm(tri, mid) + mm(tri, low))
            last = cum[CHUNK - 1 :]
            cum_out[span, :] = cum
            cumt_out[q] = cum.T[:SLOT]
            dtt_out[q] = dt[span].T[:SLOT]
            close_out[span, :] = parts(jnp.exp2(last - cum) * dt[span])
            lasts.append(last)
            bases.append(base)
            base = base + last
        zero = [jnp.zeros((1, LANES), F32)]
        table = lasts + [base] + zero * (7 - len(lasts)) + bases + zero * (8 - len(bases))
        thr_out[...] = parts(jnp.exp2(jnp.concatenate(table, axis=0)))
    copies[4].wait()


def values_kernel(owners, axis, batch, *refs):
    toks, refs = refs[:batch], refs[batch:]
    ios, refs = refs[:batch], refs[batch:]
    closes, refs = refs[:batch], refs[batch:]
    thrs, refs = refs[:batch], refs[batch:]
    halo, w, sw, vkern, voff, skern, soff, sel, gate_in = refs[:9]
    refs = refs[9:]
    gw, refs = refs[0], refs[1:]
    made_refs = [refs[4 * i : 4 * i + 4] for i in range(batch)]
    refs = refs[4 * batch :]
    ends, refs = refs[:owners], refs[owners:]
    bt, mbuf, hold0, hold1, sem = refs[:5]
    bufs = refs[5:]
    holds = (hold0, hold1)
    rows = toks[0].shape[0]
    inner = w.shape[1]
    n = sw.shape[1] // 2
    share = n // owners
    spot = lax.rem(lax.axis_index(axis), owners)
    tiles = pieces(inner, TILE)
    copy = pltpu.make_async_copy(gate_in, gw, sem)
    copy.start()
    offset = row(voff)

    def project(j, i, buf):
        x = jnp.concatenate([halo[i], toks[i][...]], axis=0)
        buf[...] = mm(x, w[:, tiles[j]]).astype(BF16).astype(F32)

    rims = mm(jnp.concatenate([halo[i] for i in range(batch)], axis=0), sw[...])

    def maps(i):
        b_out, c_out = made_refs[i][2:]
        mbuf[pl.ds(0, PAD), :] = rims[i * PAD : (i + 1) * PAD].astype(BF16).astype(F32)
        mbuf[pl.ds(PAD, rows), :] = ios[i][...].astype(F32)
        y = conv_of(mbuf[...], skern[...], row(soff))
        b_out[...] = y[:, :n]
        c_out[...] = y[:, n:]
        bt[i] = y[:, :n].astype(F32).T.astype(BF16)

    def finish(j, i, buf, hold):
        vc_out, mid_out = made_refs[i][:2]
        at = tiles[j]
        vc = conv_of(buf[...], vkern[:, at], offset[:, at])
        vc_out[:, at] = vc
        select = sel[:, at]
        through = mm(thrs[i][...], select)
        state = None
        for q, span in enumerate(pieces(rows)):
            scaled = (vc[span].astype(F32) * mm(closes[i][span, :], select)).astype(BF16)
            made = mm(bt[i, :, span], scaled)
            if q == 0:
                state = made
            else:
                mid_out[q - 1, :, at] = state.astype(BF16)
                state = state * through[q : q + 1] + made
        hold[...] = state
        for k in range(owners):
            owner = jnp.bitwise_xor(spot, k)
            part = hold[pl.ds(pl.multiple_of(owner * share, share), share), :]
            ends[k][:, i * inner + at.start : i * inner + at.stop] = part.astype(BF16)

    line = lax.broadcasted_iota(jnp.int32, (share, LANES), 0)
    count = rows // CHUNK
    decays = jnp.zeros((share, LANES), F32)
    for i in range(batch):
        mine = thrs[i][...].astype(F32)[count : count + 1]
        decays = jnp.where(line == i, jnp.broadcast_to(mine, (share, LANES)), decays)
    for k in range(owners):
        ends[k][:, batch * inner :] = decays.astype(BF16)
    stages = [(j, i) for j in range(len(tiles)) for i in range(batch)]
    for s, (j, i) in enumerate(stages):
        project(j, i, bufs[s % len(bufs)])
        if s < batch:
            maps(s)
        if s > 0:
            finish(*stages[s - 1], bufs[(s - 1) % len(bufs)], holds[s % 2])
    last = len(stages)
    finish(*stages[last - 1], bufs[(last - 1) % len(bufs)], holds[last % 2])
    copy.wait()


def inside_kernel(
    head_width, tok, gw, b_rows, c_rows, vc, mid, dtt, cum, cumt, thr, sel, skip,
    *refs,
):
    part_out, grow_out, scores, gb0, gb1 = refs[-5:]
    rows, inner = vc.shape
    tiles = pieces(inner, TILE)
    spans = pieces(rows)
    r = lax.broadcasted_iota(jnp.int32, (CHUNK, CHUNK), 0)
    s = lax.broadcasted_iota(jnp.int32, (CHUNK, CHUNK), 1)
    wide = 2 * head_width
    assert wide == CHUNK
    lane = lax.broadcasted_iota(jnp.int32, (CHUNK, wide), 1)
    flat = lane[:1]

    def project(j, buf):
        buf[...] = mm(tok[...], gw[:, tiles[j]]).astype(BF16)

    def score():
        for q, span in enumerate(spans):
            scores[q] = jnp.where(r >= s, mm_t(c_rows[span, :], b_rows[span, :]), 0.0)

    def finish(j, buf):
        tile = tiles[j]
        base = mm(thr[...], sel[:, tile])
        for q, span in enumerate(spans):
            swish = silu(buf[span, :].astype(F32))
            if q > 0:
                carried = mm(c_rows[span, :], mid[q - 1, :, tile])
            for cut in pieces(TILE, wide):
                at = slice(tile.start + cut.start, tile.start + cut.stop)
                first = at.start // head_width
                block = vc[span, at]
                mixes, halves, columns = [], [], []
                for k in range(2):
                    head = first + k
                    column = jnp.broadcast_to(cum[span, head : head + 1], (CHUNK, CHUNK))
                    columns.append(column)
                    gap = jnp.minimum(column - cumt[q, head : head + 1, :], 0.0)
                    mixes.append(
                        (scores[q] * jnp.exp2(gap) * dtt[q, head : head + 1, :]).astype(BF16)
                    )
                    halves.append(
                        jnp.where((lane >= head_width) == (k == 1), block, jnp.zeros_like(block))
                    )
                mixture = mm(jnp.concatenate(mixes, axis=1), jnp.concatenate(halves, axis=0))
                gain = jnp.where(flat < head_width, skip[first], skip[first + 1])
                mixture = mixture + gain * block.astype(F32)
                rise = jnp.exp2(jnp.where(lane < head_width, columns[0], columns[1]))
                gated = swish[:, cut] * rise
                if q > 0:
                    mixture = mixture + carried[:, cut] * rise
                    gated = gated * base[8 + q : 9 + q, cut]
                grow_out[span, at] = gated.astype(BF16)
                part_out[span, at] = mixture * swish[:, cut]

    bufs = (gb0, gb1)
    for j in range(len(tiles)):
        project(j, bufs[j % 2])
        if j == 0:
            score()
        else:
            finish(j - 1, bufs[(j - 1) % 2])
    finish(len(tiles) - 1, bufs[(len(tiles) - 1) % 2])


def gather_owned(owners, axis, refs, held):
    spot = lax.rem(lax.axis_index(axis), owners)
    for k in range(owners):
        held[jnp.bitwise_xor(spot, k)] = refs[k][...]


def total_kernel(owners, axis, batch, *refs):
    came, sel = refs[:owners], refs[owners]
    total_out, decay_out, held, lines = refs[-4:]
    gather_owned(owners, axis, came, held)
    inner = sel.shape[1]
    depth = lines.shape[0] // batch
    lines[...] = jnp.zeros_like(lines)
    for k in range(owners):
        tail = held[k, :, batch * inner :].astype(F32)
        for i in range(batch):
            lines[pl.ds(i * depth + k, 1), :] = tail[i : i + 1]
    decay_out[...] = mm(lines[...].astype(BF16), sel[...])
    for i in range(batch):
        at = slice(i * inner, (i + 1) * inner)
        state = held[0, :, at].astype(F32)
        for k in range(1, owners):
            state = state * decay_out[pl.ds(i * depth + k, 1), :] + held[k, :, at].astype(F32)
        total_out[:, at] = state.astype(BF16)


def prefix_kernel(owners, axis, batch, *refs):
    came = refs[:owners]
    decay, first = refs[owners : owners + 2]
    outs = refs[-owners - 2 : -2]
    held, made = refs[-2:]
    gather_owned(owners, axis, came, held)
    inner = decay.shape[1]
    depth = decay.shape[0] // batch
    for i in range(batch):
        at = slice(i * inner, (i + 1) * inner)
        state = first[:, at].astype(F32)
        for k in range(owners):
            made[k, :, at] = state.astype(BF16)
            if k + 1 < owners:
                state = state * decay[pl.ds(i * depth + k, 1), :] + held[k, :, at].astype(F32)
    spot = lax.rem(lax.axis_index(axis), owners)
    for k in range(owners):
        outs[k][...] = made[jnp.bitwise_xor(spot, k)]


def enter_kernel(owners, axis, index, part, grow, c_rows, *refs):
    came = refs[:owners]
    out, sq_out, state = refs[-3:]
    rows, inner = part.shape
    share = came[0].shape[0]
    spot = lax.rem(lax.axis_index(axis), owners)
    for k in range(owners):
        at = pl.multiple_of(jnp.bitwise_xor(spot, k) * share, share)
        state[pl.ds(at, share), :] = came[k][:, index * inner : (index + 1) * inner]
    for span in pieces(rows):
        acc = jnp.zeros((CHUNK, LANES), F32)
        for at in pieces(inner, TILE):
            extra = mm(c_rows[span, :], state[:, at])
            total = part[span, at] + grow[span, at].astype(F32) * extra
            out[span, at] = total
            for cut in pieces(TILE, LANES):
                acc = acc + total[:, cut] * total[:, cut]
        sq_out[:, span] = jnp.sum(acc.T, axis=0, keepdims=True)


def norm_kernel(inner_all, count, *refs):
    squares = refs[:count]
    x, gain = refs[count : count + 2]
    out = refs[-1]
    rows = out.shape[1]
    span = pl.ds(pl.multiple_of(pl.program_id(0) * rows, rows), rows)
    total = squares[0][:, span]
    for ref in squares[1:]:
        total = total + ref[:, span]
    inverse = lax.rsqrt(total / inner_all + EPS)
    columns = jnp.broadcast_to(inverse, (LANES, rows)).T
    gains = row(gain)
    for cut in pieces(out.shape[2], LANES):
        out[0, :, cut] = (x[span, cut] * columns * gains[:, cut]).astype(BF16)


def local(
    tokens,
    gate_weight,
    value_weight,
    state_weight,
    step_weight,
    value_kernel,
    value_offset,
    state_kernel,
    state_offset,
    step_offset,
    decay_rate,
    skip_gain,
    norm_gain,
):
    b, t, d = tokens.shape
    inner = gate_weight.shape[1]
    h = step_weight.shape[1]
    n = state_weight.shape[1] // 2
    head_width = inner // h
    peers = lax.axis_size("seq")
    ranks = lax.axis_size("head")
    owners = peers // 2
    share = n // owners
    chunks = t // CHUNK
    assert h <= SLOT and owners * 2 == peers and owners & (owners - 1) == 0
    assert b == 2 and chunks < 8 and value_kernel.shape[0] == 4
    lines = max(owners, 8)

    def swap(arrays):
        return [arrays[0]] + [
            here(lax.ppermute(arrays[k], "seq", [(s, s ^ k) for s in range(peers)]))
            for k in range(1, owners)
        ]

    halo = here(
        lax.ppermute(tokens[:, t - PAD :], "seq", [(s, s + 1) for s in range(peers - 1)])
    )
    outs = pl.pallas_call(
        functools.partial(front_kernel, head_width),
        in_specs=[FAR] * 6,
        out_specs=[WHOLE] * (3 + 7 * b),
        out_shape=[
            pltpu.VMEM(state_weight.shape, BF16),
            pltpu.VMEM(value_weight.shape, BF16),
            pltpu.VMEM((LANES, inner), BF16),
        ]
        + [
            pltpu.VMEM((t, d), BF16),
            pltpu.VMEM((t, 2 * n), BF16),
            pltpu.VMEM((t, LANES), BF16),
            pltpu.VMEM((16, LANES), BF16),
            pltpu.VMEM((t, LANES), F32),
            pltpu.VMEM((chunks, SLOT, CHUNK), F32),
            pltpu.VMEM((chunks, SLOT, CHUNK), F32),
        ]
        * b,
        scratch_shapes=[
            pltpu.VMEM((h, d), BF16),
            pltpu.VMEM((h,), F32),
            pltpu.VMEM((h,), F32),
            pltpu.VMEM((LANES, d), BF16),
            pltpu.VMEM((8, LANES), F32),
            pltpu.SemaphoreType.DMA((b + 5,)),
        ],
        compiler_params=params(16),
        name="front",
        cost_estimate=cost(2 * b * t * d * (2 * n + LANES)),
    )(*map(far, (tokens, state_weight, step_weight.T, value_weight, step_offset, decay_rate)))
    sw, w, sel = outs[:3]
    fronts = [outs[3 + 7 * i : 10 + 7 * i] for i in range(b)]

    toks, ios, closes, thrs = [[fronts[i][k] for i in range(b)] for k in range(4)]
    outs = pl.pallas_call(
        functools.partial(values_kernel, owners, "seq", b),
        in_specs=[WHOLE] * (4 * b + 8) + [FAR],
        out_specs=[WHOLE] * (1 + 4 * b + owners),
        out_shape=[pltpu.VMEM(gate_weight.shape, BF16)]
        + [
            pltpu.VMEM((t, inner), BF16),
            pltpu.VMEM((chunks - 1, n, inner), BF16),
            pltpu.VMEM((t, n), BF16),
            pltpu.VMEM((t, n), BF16),
        ]
        * b
        + [pltpu.VMEM((share, b * inner + LANES), BF16)] * owners,
        scratch_shapes=[
            pltpu.VMEM((b, n, t), BF16),
            pltpu.VMEM((t + PAD, 2 * n), F32),
            pltpu.VMEM((n, TILE), F32),
            pltpu.VMEM((n, TILE), F32),
            pltpu.SemaphoreType.DMA,
        ]
        + [pltpu.VMEM((t + PAD, TILE), F32)] * 3,
        compiler_params=params(20),
        name="values",
        cost_estimate=cost(2 * b * t * d * inner),
    )(
        *toks, *ios, *closes, *thrs, halo, w, sw, value_kernel, value_offset,
        state_kernel, state_offset, sel, far(gate_weight),
    )
    gw = outs[0]
    made = [outs[1 + 4 * i : 5 + 4 * i] for i in range(b)]
    ends = outs[1 + 4 * b :]

    def inside(i, gw, made, after):
        tok, _, _, thr, cum, cumt, dtt = fronts[i]
        vc, mid, b_rows, c_rows = made[:4]
        return pl.pallas_call(
            functools.partial(inside_kernel, head_width),
            in_specs=[WHOLE] * 11 + [SCALARS] + [WHOLE] * len(after),
            out_specs=[WHOLE] * 2,
            out_shape=[pltpu.VMEM((t, inner), F32), pltpu.VMEM((t, inner), BF16)],
            scratch_shapes=[
                pltpu.VMEM((chunks, CHUNK, CHUNK), F32),
                pltpu.VMEM((t, TILE), BF16),
                pltpu.VMEM((t, TILE), BF16),
            ],
            compiler_params=params(16),
            name=f"inside{i}",
            cost_estimate=cost(2.5 * t * d * inner),
        )(tok, gw, b_rows, c_rows, vc, mid, dtt, cum, cumt, thr, sel, skip_gain, *after)

    def total(came, after):
        return pl.pallas_call(
            functools.partial(total_kernel, owners, "seq", b),
            in_specs=[WHOLE] * (owners + 1 + len(after)),
            out_specs=[WHOLE] * 2,
            out_shape=[
                pltpu.VMEM((share, b * inner), BF16),
                pltpu.VMEM((b * lines, inner), F32),
            ],
            scratch_shapes=[
                pltpu.VMEM((owners, share, b * inner + LANES), BF16),
                pltpu.VMEM((b * lines, LANES), F32),
            ],
            compiler_params=params(16),
            name="total",
        )(*came, sel, *after)

    def prefix(came, decay, first, after):
        return pl.pallas_call(
            functools.partial(prefix_kernel, owners, "seq", b),
            in_specs=[WHOLE] * (owners + 2 + len(after)),
            out_specs=[WHOLE] * owners,
            out_shape=[pltpu.VMEM((share, b * inner), BF16)] * owners,
            scratch_shapes=[
                pltpu.VMEM((owners, share, b * inner + LANES), BF16),
                pltpu.VMEM((owners, share, b * inner), BF16),
            ],
            compiler_params=params(16),
            name="prefix",
        )(*came, decay, first, *after)

    def across(x):
        return here(lax.ppermute(x, "seq", [(s, s + owners) for s in range(owners)]))

    def enter(i, part, grow, c_rows, states, after):
        x, sq = pl.pallas_call(
            functools.partial(enter_kernel, owners, "seq", i),
            in_specs=[WHOLE] * (3 + owners + len(after)),
            out_specs=[WHOLE] * 2,
            out_shape=[pltpu.VMEM((t, inner), F32), pltpu.VMEM((1, t), F32)],
            scratch_shapes=[pltpu.VMEM((n, inner), BF16)],
            compiler_params=params(16),
            name=f"enter{i}",
        )(part, grow, c_rows, *states, *after)
        return x, [sq] + [
            here(lax.ppermute(sq, "head", [(s, (s + k) % ranks) for s in range(ranks)]))
            for k in range(1, ranks)
        ]

    def norm(i, x, squares, into):
        rows = min(t, 256)
        return pl.pallas_call(
            functools.partial(norm_kernel, inner * ranks, ranks),
            grid=(t // rows,),
            in_specs=[WHOLE] * (ranks + 2) + [FAR] * len(into),
            out_specs=pl.BlockSpec((1, rows, inner), lambda q: (i, q, 0)),
            out_shape=jax.ShapeDtypeStruct((b, t, inner), BF16),
            input_output_aliases={ranks + 2: 0} if into else {},
            compiler_params=params(16),
            name=f"norm{i}",
        )(*squares, x, norm_gain, *into)

    came = swap(ends)
    part0, grow0 = inside(0, gw, made[0], ())
    whole, decay = total(came, (grow0,))
    first = across(whole)
    sent = prefix(came, decay, first, ())
    back = swap(sent)
    part1, grow1 = inside(1, gw, made[1], (sent[1],))
    x0, squares0 = enter(0, part0, grow0, made[0][3], back, (grow1,))
    x1, squares1 = enter(1, part1, grow1, made[1][3], back, (squares0[0],))
    out = norm(0, x0, squares0, ())
    return norm(1, x1, squares1, (out,))


def solution(mesh):
    return jax.shard_map(
        local,
        mesh=mesh,
        in_specs=(
            P(None, "seq", None),
            P(None, "head"),
            P(None, "head"),
            P(),
            P(None, "head"),
            P(None, "head"),
            P("head"),
            P(),
            P(),
            P("head"),
            P("head"),
            P("head"),
            P("head"),
        ),
        out_specs=P(None, "seq", "head"),
        check_vma=False,
    )
```

```python
import functools
import jax
import jax.numpy as jnp
from jax import lax
from jax.experimental import pallas as pl
from jax.experimental.pallas import tpu as pltpu
from jax.sharding import PartitionSpec as P

EPS = 1e-05
LOG2E = 1.4426950408889634
PAD = 16
CHUNK = 128
TILE = 256
LANES = 128
SLOT = 32
F32 = jnp.float32
BF16 = jnp.bfloat16
WHOLE = pl.BlockSpec(memory_space=pltpu.VMEM)
FAR = pl.BlockSpec(memory_space=pltpu.HBM)
SCALARS = pl.BlockSpec(memory_space=pltpu.SMEM)


def here(x):
    return pltpu.with_memory_space_constraint(x, pltpu.VMEM)


def far(x):
    return pltpu.with_memory_space_constraint(x, pltpu.HBM)


def params(mib):
    return pltpu.CompilerParams(vmem_limit_bytes=mib << 20)


def cost(flops):
    return pl.CostEstimate(flops=int(flops), transcendentals=0, bytes_accessed=0)


def mm(a, b):
    return jnp.dot(a, b, preferred_element_type=F32)


def mm_t(a, b):
    return lax.dot_general(a, b, (((1,), (1,)), ((), ())), preferred_element_type=F32)


def silu(x):
    half = 0.5 * x
    return half + half * jnp.tanh(half)


def row(ref):
    return ref[...].reshape(1, ref.shape[0])


def pieces(total, size=CHUNK):
    return [slice(k * size, (k + 1) * size) for k in range(total // size)]


def head_select(width, head_width, group):
    lane = lax.broadcasted_iota(jnp.int32, (LANES, width), 0) - 2 * SLOT * group
    col = lax.broadcasted_iota(jnp.int32, (LANES, width), 1)
    start = (lane & (SLOT - 1)) * head_width
    hit = (lane >= 0) & (lane < 2 * SLOT) & (col >= start) & (col < start + head_width)
    return jnp.where(hit, 1.0, 0.0).astype(BF16)


def conv_of(x, kernel, offset):
    back = pltpu.roll(x, 1, 0)
    near = offset + kernel[3:4] * x + kernel[2:3] * back
    deep = kernel[1:2] * x + kernel[0:1] * back
    return silu((near + pltpu.roll(deep, 2, 0))[PAD:]).astype(BF16)


def front_kernel(head_width, *refs):
    tok_in, sw_in, twt_in, w_in, toff_in, rate_in = refs[:6]
    batch = tok_in.shape[0]
    sw, w, sel = refs[6:9]
    per_batch = [refs[9 + 7 * i : 16 + 7 * i] for i in range(batch)]
    twt, toff, rate, tws, vec, sem = refs[9 + 7 * batch :]
    rows = tok_in.shape[1]
    heads = twt.shape[0]
    token_copies = [
        pltpu.make_async_copy(tok_in.at[i], per_batch[i][0], sem.at[i]) for i in range(batch)
    ]
    copies = [
        pltpu.make_async_copy(twt_in, twt, sem.at[batch]),
        pltpu.make_async_copy(toff_in, toff, sem.at[batch + 1]),
        pltpu.make_async_copy(rate_in, rate, sem.at[batch + 2]),
        pltpu.make_async_copy(sw_in, sw, sem.at[batch + 3]),
        pltpu.make_async_copy(w_in, w, sem.at[batch + 4]),
    ]
    for copy in copies[:3] + [token_copies[0], copies[3]] + token_copies[1:] + [copies[4]]:
        copy.start()
    sel[...] = head_select(sel.shape[1], head_width, 0)
    for copy in copies[:3]:
        copy.wait()
    tws[...] = jnp.zeros_like(tws)
    vec[...] = jnp.zeros_like(vec)
    for g in range(LANES // SLOT):
        tws[pl.ds(g * SLOT, heads), :] = twt[...]
        vec[pl.ds(0, 1), pl.ds(g * SLOT, heads)] = row(toff)
        vec[pl.ds(1, 1), pl.ds(g * SLOT, heads)] = row(rate)
    offset = vec[pl.ds(0, 1), :]
    scale = vec[pl.ds(1, 1), :] * (-LOG2E)
    r = lax.broadcasted_iota(jnp.int32, (CHUNK, CHUNK), 0)
    c = lax.broadcasted_iota(jnp.int32, (CHUNK, CHUNK), 1)
    tri = jnp.where(r >= c, 1.0, 0.0).astype(BF16)
    group = lax.broadcasted_iota(jnp.int32, (1, LANES), 1) // SLOT
    low_lane = (group & 1) == 1

    def parts(x):
        hi = x.astype(BF16).astype(F32)
        return jnp.where(low_lane, x - hi, hi).astype(BF16)

    for i in range(batch):
        tok, io_out, close_out, thr_out, cum_out, cumt_out, dtt_out = per_batch[i]
        token_copies[i].wait()
        if i == 0:
            copies[3].wait()
        x = tok[...]
        io_out[...] = mm(x, sw[...]).astype(BF16)
        z = mm_t(x, tws[...]) + offset
        dt = jnp.maximum(z, 0.0) + jnp.log1p(jnp.exp(-jnp.abs(z)))
        log_decay = dt * scale
        base = jnp.zeros((1, LANES), F32)
        lasts, bases = [], []
        for q, span in enumerate(pieces(rows)):
            part = log_decay[span]
            hi = part.astype(BF16)
            rest = part - hi.astype(F32)
            mid = rest.astype(BF16)
            low = (rest - mid.astype(F32)).astype(BF16)
            cum = mm(tri, hi) + (mm(tri, mid) + mm(tri, low))
            last = cum[CHUNK - 1 :]
            cum_out[span, :] = cum
            cumt_out[q] = cum.T[:SLOT]
            dtt_out[q] = dt[span].T[:SLOT]
            close_out[span, :] = parts(jnp.exp2(last - cum) * dt[span])
            lasts.append(last)
            bases.append(base)
            base = base + last
        zero = [jnp.zeros((1, LANES), F32)]
        table = lasts + [base] + zero * (7 - len(lasts)) + bases + zero * (8 - len(bases))
        thr_out[...] = parts(jnp.exp2(jnp.concatenate(table, axis=0)))
    copies[4].wait()


def values_kernel(owners, axis, index, batch, *refs):
    tok, io, close, thr, halo, w, sw, vkern, voff, skern, soff, sel = refs[:12]
    loads = index == batch - 1
    sem = refs[-6]
    bt, mbuf, hold, vb0, vb1 = refs[-5:]
    ends = refs[-6 - owners : -6]
    if loads:
        gate_in, gw = refs[12], refs[-7 - owners]
        copy = pltpu.make_async_copy(gate_in, gw, sem)
        copy.start()
    first = -6 - owners - loads - 4
    vc_out, mid_out, b_out, c_out = refs[first : first + 4]
    rows = tok.shape[0]
    inner = w.shape[1]
    n = sw.shape[1] // 2
    share = n // owners
    spot = lax.rem(lax.axis_index(axis), owners)
    tiles = pieces(inner, TILE)
    rim = halo[index]
    offset = row(voff)

    def project(j, buf):
        x = jnp.concatenate([rim, tok[...]], axis=0)
        buf[...] = mm(x, w[:, tiles[j]]).astype(BF16).astype(F32)

    def maps():
        mbuf[pl.ds(0, PAD), :] = mm(rim, sw[...]).astype(BF16).astype(F32)
        mbuf[pl.ds(PAD, rows), :] = io[...].astype(F32)
        y = conv_of(mbuf[...], skern[...], row(soff))
        b_out[...] = y[:, :n]
        c_out[...] = y[:, n:]
        bt[...] = y[:, :n].astype(F32).T.astype(BF16)

    def finish(j, buf):
        at = tiles[j]
        vc = conv_of(buf[...], vkern[:, at], offset[:, at])
        vc_out[:, at] = vc
        select = sel[:, at]
        through = mm(thr[...], select)
        state = None
        for q, span in enumerate(pieces(rows)):
            scaled = (vc[span].astype(F32) * mm(close[span, :], select)).astype(BF16)
            made = mm(bt[:, span], scaled)
            if q == 0:
                state = made
            else:
                mid_out[q - 1, :, at] = state.astype(BF16)
                state = state * through[q : q + 1] + made
        hold[...] = state
        for k in range(owners):
            owner = jnp.bitwise_xor(spot, k)
            part = hold[pl.ds(pl.multiple_of(owner * share, share), share), :]
            ends[k][:, index * inner + at.start : index * inner + at.stop] = part.astype(BF16)

    line = lax.broadcasted_iota(jnp.int32, (share, LANES), 0)
    count = rows // CHUNK
    mine = jnp.broadcast_to(thr[...].astype(F32)[count : count + 1], (share, LANES))
    decays = jnp.where(line == 0, mine, 0.0).astype(BF16)
    tail = batch * inner + index * LANES
    for k in range(owners):
        ends[k][:, tail : tail + LANES] = decays
    bufs = (vb0, vb1)
    for j in range(len(tiles)):
        project(j, bufs[j % 2])
        if j == 0:
            maps()
        else:
            finish(j - 1, bufs[(j - 1) % 2])
    finish(len(tiles) - 1, bufs[(len(tiles) - 1) % 2])
    if loads:
        copy.wait()


def inside_kernel(
    head_width, tok, gw, b_rows, c_rows, vc, mid, dtt, cum, cumt, thr, sel, skip,
    *refs,
):
    part_out, grow_out, scores, gb0, gb1 = refs[-5:]
    rows, inner = vc.shape
    tiles = pieces(inner, TILE)
    spans = pieces(rows)
    r = lax.broadcasted_iota(jnp.int32, (CHUNK, CHUNK), 0)
    s = lax.broadcasted_iota(jnp.int32, (CHUNK, CHUNK), 1)
    wide = 2 * head_width
    assert wide == CHUNK
    lane = lax.broadcasted_iota(jnp.int32, (CHUNK, wide), 1)
    flat = lane[:1]

    def project(j, buf):
        buf[...] = mm(tok[...], gw[:, tiles[j]]).astype(BF16)

    def score():
        for q, span in enumerate(spans):
            scores[q] = jnp.where(r >= s, mm_t(c_rows[span, :], b_rows[span, :]), 0.0)

    def finish(j, buf):
        tile = tiles[j]
        base = mm(thr[...], sel[:, tile])
        for q, span in enumerate(spans):
            swish = silu(buf[span, :].astype(F32))
            if q > 0:
                carried = mm(c_rows[span, :], mid[q - 1, :, tile])
            for cut in pieces(TILE, wide):
                at = slice(tile.start + cut.start, tile.start + cut.stop)
                first = at.start // head_width
                block = vc[span, at]
                mixes, halves, columns = [], [], []
                for k in range(2):
                    head = first + k
                    column = jnp.broadcast_to(cum[span, head : head + 1], (CHUNK, CHUNK))
                    columns.append(column)
                    gap = jnp.minimum(column - cumt[q, head : head + 1, :], 0.0)
                    mixes.append(
                        (scores[q] * jnp.exp2(gap) * dtt[q, head : head + 1, :]).astype(BF16)
                    )
                    halves.append(
                        jnp.where((lane >= head_width) == (k == 1), block, jnp.zeros_like(block))
                    )
                mixture = mm(jnp.concatenate(mixes, axis=1), jnp.concatenate(halves, axis=0))
                gain = jnp.where(flat < head_width, skip[first], skip[first + 1])
                mixture = mixture + gain * block.astype(F32)
                rise = jnp.exp2(jnp.where(lane < head_width, columns[0], columns[1]))
                gated = swish[:, cut] * rise
                if q > 0:
                    mixture = mixture + carried[:, cut] * rise
                    gated = gated * base[8 + q : 9 + q, cut]
                grow_out[span, at] = gated.astype(BF16)
                part_out[span, at] = mixture * swish[:, cut]

    bufs = (gb0, gb1)
    for j in range(len(tiles)):
        project(j, bufs[j % 2])
        if j == 0:
            score()
        else:
            finish(j - 1, bufs[(j - 1) % 2])
    finish(len(tiles) - 1, bufs[(len(tiles) - 1) % 2])


def total_kernel(owners, axis, index, batch, *refs):
    came, sel = refs[:owners], refs[owners]
    total_out, decay_out, held, lines = refs[-4:]
    inner = sel.shape[1]
    at = slice(index * inner, (index + 1) * inner)
    tail = slice(batch * inner + index * LANES, batch * inner + (index + 1) * LANES)
    spot = lax.rem(lax.axis_index(axis), owners)
    lines[...] = jnp.zeros_like(lines)
    for k in range(owners):
        owner = jnp.bitwise_xor(spot, k)
        held[owner] = came[k][:, at]
        lines[pl.ds(owner, 1), :] = came[k][:, tail].astype(F32)[:1]
    decay_out[...] = mm(lines[...].astype(BF16), sel[...])
    state = held[0].astype(F32)
    for k in range(1, owners):
        state = state * decay_out[pl.ds(k, 1), :] + held[k].astype(F32)
    total_out[...] = state.astype(BF16)


def prefix_kernel(owners, axis, index, *refs):
    came = refs[:owners]
    decay, first = refs[owners : owners + 2]
    outs = refs[-owners - 2 : -2]
    held, made = refs[-2:]
    inner = decay.shape[1]
    at = slice(index * inner, (index + 1) * inner)
    spot = lax.rem(lax.axis_index(axis), owners)
    for k in range(owners):
        held[jnp.bitwise_xor(spot, k)] = came[k][:, at]
    state = first[...].astype(F32)
    for k in range(owners):
        made[k] = state.astype(BF16)
        if k + 1 < owners:
            state = state * decay[pl.ds(k, 1), :] + held[k].astype(F32)
    for k in range(owners):
        outs[k][...] = made[jnp.bitwise_xor(spot, k)]


def enter_kernel(owners, axis, part, grow, c_rows, *refs):
    came = refs[:owners]
    out, sq_out, state = refs[-3:]
    rows, inner = part.shape
    share = came[0].shape[0]
    spot = lax.rem(lax.axis_index(axis), owners)
    for k in range(owners):
        at = pl.multiple_of(jnp.bitwise_xor(spot, k) * share, share)
        state[pl.ds(at, share), :] = came[k][...]
    for span in pieces(rows):
        acc = jnp.zeros((CHUNK, LANES), F32)
        for at in pieces(inner, TILE):
            extra = mm(c_rows[span, :], state[:, at])
            total = part[span, at] + grow[span, at].astype(F32) * extra
            out[span, at] = total
            for cut in pieces(TILE, LANES):
                acc = acc + total[:, cut] * total[:, cut]
        sq_out[:, span] = jnp.sum(acc.T, axis=0, keepdims=True)


def norm_kernel(inner_all, count, *refs):
    squares = refs[:count]
    x, gain = refs[count : count + 2]
    out = refs[-1]
    rows = out.shape[1]
    span = pl.ds(pl.multiple_of(pl.program_id(0) * rows, rows), rows)
    total = squares[0][:, span]
    for ref in squares[1:]:
        total = total + ref[:, span]
    inverse = lax.rsqrt(total / inner_all + EPS)
    columns = jnp.broadcast_to(inverse, (LANES, rows)).T
    gains = row(gain)
    for cut in pieces(out.shape[2], LANES):
        out[0, :, cut] = (x[span, cut] * columns * gains[:, cut]).astype(BF16)


def local(
    tokens,
    gate_weight,
    value_weight,
    state_weight,
    step_weight,
    value_kernel,
    value_offset,
    state_kernel,
    state_offset,
    step_offset,
    decay_rate,
    skip_gain,
    norm_gain,
):
    b, t, d = tokens.shape
    inner = gate_weight.shape[1]
    h = step_weight.shape[1]
    n = state_weight.shape[1] // 2
    head_width = inner // h
    peers = lax.axis_size("seq")
    ranks = lax.axis_size("head")
    owners = peers // 2
    share = n // owners
    chunks = t // CHUNK
    assert h <= SLOT and owners * 2 == peers and owners & (owners - 1) == 0
    assert b == 2 and chunks < 8 and value_kernel.shape[0] == 4
    lines = max(owners, 8)

    def swap(arrays):
        return [arrays[0]] + [
            here(lax.ppermute(arrays[k], "seq", [(s, s ^ k) for s in range(peers)]))
            for k in range(1, owners)
        ]

    halo = here(
        lax.ppermute(tokens[:, t - PAD :], "seq", [(s, s + 1) for s in range(peers - 1)])
    )
    outs = pl.pallas_call(
        functools.partial(front_kernel, head_width),
        in_specs=[FAR] * 6,
        out_specs=[WHOLE] * (3 + 7 * b),
        out_shape=[
            pltpu.VMEM(state_weight.shape, BF16),
            pltpu.VMEM(value_weight.shape, BF16),
            pltpu.VMEM((LANES, inner), BF16),
        ]
        + [
            pltpu.VMEM((t, d), BF16),
            pltpu.VMEM((t, 2 * n), BF16),
            pltpu.VMEM((t, LANES), BF16),
            pltpu.VMEM((16, LANES), BF16),
            pltpu.VMEM((t, LANES), F32),
            pltpu.VMEM((chunks, SLOT, CHUNK), F32),
            pltpu.VMEM((chunks, SLOT, CHUNK), F32),
        ]
        * b,
        scratch_shapes=[
            pltpu.VMEM((h, d), BF16),
            pltpu.VMEM((h,), F32),
            pltpu.VMEM((h,), F32),
            pltpu.VMEM((LANES, d), BF16),
            pltpu.VMEM((8, LANES), F32),
            pltpu.SemaphoreType.DMA((b + 5,)),
        ],
        compiler_params=params(16),
        name="front",
        cost_estimate=cost(2 * b * t * d * (2 * n + LANES)),
    )(*map(far, (tokens, state_weight, step_weight.T, value_weight, step_offset, decay_rate)))
    sw, w, sel = outs[:3]
    fronts = [outs[3 + 7 * i : 10 + 7 * i] for i in range(b)]

    wide = b * (inner + LANES)

    def values(i, ends):
        tok, io, close, thr, _, _, _ = fronts[i]
        loads = i == b - 1
        inputs = 12 + loads
        return pl.pallas_call(
            functools.partial(values_kernel, owners, "seq", i, b),
            in_specs=[WHOLE] * 12 + [FAR] * loads + [WHOLE] * len(ends),
            out_specs=[WHOLE] * (4 + loads + owners),
            out_shape=[
                pltpu.VMEM((t, inner), BF16),
                pltpu.VMEM((chunks - 1, n, inner), BF16),
                pltpu.VMEM((t, n), BF16),
                pltpu.VMEM((t, n), BF16),
            ]
            + [pltpu.VMEM(gate_weight.shape, BF16)] * loads
            + [pltpu.VMEM((share, wide), BF16)] * owners,
            scratch_shapes=[
                pltpu.SemaphoreType.DMA,
                pltpu.VMEM((n, t), BF16),
                pltpu.VMEM((t + PAD, 2 * n), F32),
                pltpu.VMEM((n, TILE), F32),
                pltpu.VMEM((t + PAD, TILE), F32),
                pltpu.VMEM((t + PAD, TILE), F32),
            ],
            input_output_aliases={inputs + k: 4 + loads + k for k in range(len(ends))},
            compiler_params=params(16),
            name=f"values{i}",
            cost_estimate=cost(2 * t * d * inner),
        )(
            tok, io, close, thr, halo, w, sw, value_kernel, value_offset,
            state_kernel, state_offset, sel, *[far(gate_weight)] * loads, *ends,
        )

    made, ends = [], ()
    for i in range(b):
        outs = values(i, ends)
        made.append(outs[:4])
        ends = outs[-owners:]
    gw = outs[4]

    def inside(i, gw, made, after):
        tok, _, _, thr, cum, cumt, dtt = fronts[i]
        vc, mid, b_rows, c_rows = made[:4]
        return pl.pallas_call(
            functools.partial(inside_kernel, head_width),
            in_specs=[WHOLE] * 11 + [SCALARS] + [WHOLE] * len(after),
            out_specs=[WHOLE] * 2,
            out_shape=[pltpu.VMEM((t, inner), F32), pltpu.VMEM((t, inner), BF16)],
            scratch_shapes=[
                pltpu.VMEM((chunks, CHUNK, CHUNK), F32),
                pltpu.VMEM((t, TILE), BF16),
                pltpu.VMEM((t, TILE), BF16),
            ],
            compiler_params=params(16),
            name=f"inside{i}",
            cost_estimate=cost(2.5 * t * d * inner),
        )(tok, gw, b_rows, c_rows, vc, mid, dtt, cum, cumt, thr, sel, skip_gain, *after)

    def total(i, came, after):
        return pl.pallas_call(
            functools.partial(total_kernel, owners, "seq", i, b),
            in_specs=[WHOLE] * (owners + 1 + len(after)),
            out_specs=[WHOLE] * 2,
            out_shape=[pltpu.VMEM((share, inner), BF16), pltpu.VMEM((lines, inner), F32)],
            scratch_shapes=[
                pltpu.VMEM((owners, share, inner), BF16),
                pltpu.VMEM((lines, LANES), F32),
            ],
            compiler_params=params(16),
            name=f"total{i}",
        )(*came, sel, *after)

    def prefix(i, came, decay, first, after):
        return pl.pallas_call(
            functools.partial(prefix_kernel, owners, "seq", i),
            in_specs=[WHOLE] * (owners + 2 + len(after)),
            out_specs=[WHOLE] * owners,
            out_shape=[pltpu.VMEM((share, inner), BF16)] * owners,
            scratch_shapes=[
                pltpu.VMEM((owners, share, inner), BF16),
                pltpu.VMEM((owners, share, inner), BF16),
            ],
            compiler_params=params(16),
            name=f"prefix{i}",
        )(*came, decay, first, *after)

    def across(x):
        return here(lax.ppermute(x, "seq", [(s, s + owners) for s in range(owners)]))

    def enter(i, part, grow, c_rows, states, after):
        x, sq = pl.pallas_call(
            functools.partial(enter_kernel, owners, "seq"),
            in_specs=[WHOLE] * (3 + owners + len(after)),
            out_specs=[WHOLE] * 2,
            out_shape=[pltpu.VMEM((t, inner), F32), pltpu.VMEM((1, t), F32)],
            scratch_shapes=[pltpu.VMEM((n, inner), BF16)],
            compiler_params=params(16),
            name=f"enter{i}",
        )(part, grow, c_rows, *states, *after)
        return x, [sq] + [
            here(lax.ppermute(sq, "head", [(s, (s + k) % ranks) for s in range(ranks)]))
            for k in range(1, ranks)
        ]

    def norm(i, x, squares, into):
        rows = min(t, 256)
        return pl.pallas_call(
            functools.partial(norm_kernel, inner * ranks, ranks),
            grid=(t // rows,),
            in_specs=[WHOLE] * (ranks + 2) + [FAR] * len(into),
            out_specs=pl.BlockSpec((1, rows, inner), lambda q: (i, q, 0)),
            out_shape=jax.ShapeDtypeStruct((b, t, inner), BF16),
            input_output_aliases={ranks + 2: 0} if into else {},
            compiler_params=params(16),
            name=f"norm{i}",
        )(*squares, x, norm_gain, *into)

    came = swap(ends)
    part0, grow0 = inside(0, gw, made[0], ())
    whole0, decay0 = total(0, came, (grow0,))
    first0 = across(whole0)
    whole1, decay1 = total(1, came, (whole0,))
    first1 = across(whole1)
    part1, grow1 = inside(1, gw, made[1], (whole1,))
    sent0 = prefix(0, came, decay0, first0, (grow1,))
    back0 = swap(sent0)
    sent1 = prefix(1, came, decay1, first1, (sent0[1],))
    back1 = swap(sent1)
    x0, squares0 = enter(0, part0, grow0, made[0][3], back0, (sent1[1],))
    x1, squares1 = enter(1, part1, grow1, made[1][3], back1, (squares0[0],))
    out = norm(0, x0, squares0, ())
    return norm(1, x1, squares1, (out,))


def solution(mesh):
    return jax.shard_map(
        local,
        mesh=mesh,
        in_specs=(
            P(None, "seq", None),
            P(None, "head"),
            P(None, "head"),
            P(),
            P(None, "head"),
            P(None, "head"),
            P("head"),
            P(),
            P(),
            P("head"),
            P("head"),
            P("head"),
            P("head"),
        ),
        out_specs=P(None, "seq", "head"),
        check_vma=False,
    )
```

```python
import functools
import jax
import jax.numpy as jnp
from jax import lax
from jax.experimental import pallas as pl
from jax.experimental.pallas import tpu as pltpu
from jax.sharding import PartitionSpec as P

EPS = 1e-05
LOG2E = 1.4426950408889634
PAD = 16
CHUNK = 128
TILE = 256
LANES = 128
SLOT = 32
F32 = jnp.float32
BF16 = jnp.bfloat16
WHOLE = pl.BlockSpec(memory_space=pltpu.VMEM)
FAR = pl.BlockSpec(memory_space=pltpu.HBM)
SCALARS = pl.BlockSpec(memory_space=pltpu.SMEM)


def here(x):
    return pltpu.with_memory_space_constraint(x, pltpu.VMEM)


def far(x):
    return pltpu.with_memory_space_constraint(x, pltpu.HBM)


def params(mib):
    return pltpu.CompilerParams(vmem_limit_bytes=mib << 20)


def cost(flops):
    return pl.CostEstimate(flops=int(flops), transcendentals=0, bytes_accessed=0)


def mm(a, b):
    return jnp.dot(a, b, preferred_element_type=F32)


def mm_t(a, b):
    return lax.dot_general(a, b, (((1,), (1,)), ((), ())), preferred_element_type=F32)


def silu(x):
    half = 0.5 * x
    return half + half * jnp.tanh(half)


def row(ref):
    return ref[...].reshape(1, ref.shape[0])


def pieces(total, size=CHUNK):
    return [slice(k * size, (k + 1) * size) for k in range(total // size)]


def head_select(width, head_width, group):
    lane = lax.broadcasted_iota(jnp.int32, (LANES, width), 0) - 2 * SLOT * group
    col = lax.broadcasted_iota(jnp.int32, (LANES, width), 1)
    start = (lane & (SLOT - 1)) * head_width
    hit = (lane >= 0) & (lane < 2 * SLOT) & (col >= start) & (col < start + head_width)
    return jnp.where(hit, 1.0, 0.0).astype(BF16)


def conv_of(x, kernel, offset):
    back = pltpu.roll(x, 1, 0)
    near = offset + kernel[3:4] * x + kernel[2:3] * back
    deep = kernel[1:2] * x + kernel[0:1] * back
    return silu((near + pltpu.roll(deep, 2, 0))[PAD:]).astype(BF16)


def front_kernel(head_width, *refs):
    tok_in, sw_in, twt_in, w_in, toff_in, rate_in = refs[:6]
    batch = tok_in.shape[0]
    sw, w, sel = refs[6:9]
    per_batch = [refs[9 + 7 * i : 16 + 7 * i] for i in range(batch)]
    twt, toff, rate, tws, vec, sem = refs[9 + 7 * batch :]
    rows = tok_in.shape[1]
    heads = twt.shape[0]
    token_copies = [
        pltpu.make_async_copy(tok_in.at[i], per_batch[i][0], sem.at[i]) for i in range(batch)
    ]
    copies = [
        pltpu.make_async_copy(twt_in, twt, sem.at[batch]),
        pltpu.make_async_copy(toff_in, toff, sem.at[batch + 1]),
        pltpu.make_async_copy(rate_in, rate, sem.at[batch + 2]),
        pltpu.make_async_copy(sw_in, sw, sem.at[batch + 3]),
        pltpu.make_async_copy(w_in, w, sem.at[batch + 4]),
    ]
    for copy in copies[:3] + [token_copies[0], copies[3]] + token_copies[1:] + [copies[4]]:
        copy.start()
    sel[...] = head_select(sel.shape[1], head_width, 0)
    for copy in copies[:3]:
        copy.wait()
    tws[...] = jnp.zeros_like(tws)
    vec[...] = jnp.zeros_like(vec)
    for g in range(LANES // SLOT):
        tws[pl.ds(g * SLOT, heads), :] = twt[...]
        vec[pl.ds(0, 1), pl.ds(g * SLOT, heads)] = row(toff)
        vec[pl.ds(1, 1), pl.ds(g * SLOT, heads)] = row(rate)
    offset = vec[pl.ds(0, 1), :]
    scale = vec[pl.ds(1, 1), :] * (-LOG2E)
    r = lax.broadcasted_iota(jnp.int32, (CHUNK, CHUNK), 0)
    c = lax.broadcasted_iota(jnp.int32, (CHUNK, CHUNK), 1)
    tri = jnp.where(r >= c, 1.0, 0.0).astype(BF16)
    group = lax.broadcasted_iota(jnp.int32, (1, LANES), 1) // SLOT
    low_lane = (group & 1) == 1

    def parts(x):
        hi = x.astype(BF16).astype(F32)
        return jnp.where(low_lane, x - hi, hi).astype(BF16)

    for i in range(batch):
        tok, io_out, close_out, thr_out, cum_out, cumt_out, dtt_out = per_batch[i]
        token_copies[i].wait()
        if i == 0:
            copies[3].wait()
        x = tok[...]
        io_out[...] = mm(x, sw[...]).astype(BF16)
        z = mm_t(x, tws[...]) + offset
        dt = jnp.maximum(z, 0.0) + jnp.log1p(jnp.exp(-jnp.abs(z)))
        log_decay = dt * scale
        base = jnp.zeros((1, LANES), F32)
        lasts, bases = [], []
        for q, span in enumerate(pieces(rows)):
            part = log_decay[span]
            hi = part.astype(BF16)
            rest = part - hi.astype(F32)
            mid = rest.astype(BF16)
            low = (rest - mid.astype(F32)).astype(BF16)
            cum = mm(tri, hi) + (mm(tri, mid) + mm(tri, low))
            last = cum[CHUNK - 1 :]
            cum_out[span, :] = cum
            cumt_out[q] = cum.T[:SLOT]
            dtt_out[q] = dt[span].T[:SLOT]
            close_out[span, :] = parts(jnp.exp2(last - cum) * dt[span])
            lasts.append(last)
            bases.append(base)
            base = base + last
        zero = [jnp.zeros((1, LANES), F32)]
        table = lasts + [base] + zero * (7 - len(lasts)) + bases + zero * (8 - len(bases))
        thr_out[...] = parts(jnp.exp2(jnp.concatenate(table, axis=0)))
    copies[4].wait()


def values_kernel(owners, axis, index, batch, *refs):
    tok, io, close, thr, halo, w, sw, vkern, voff, skern, soff, sel = refs[:12]
    loads = index == batch - 1
    sem = refs[-6]
    bt, mbuf, hold, vb0, vb1 = refs[-5:]
    ends = refs[-6 - owners : -6]
    if loads:
        gate_in, gw = refs[12], refs[-7 - owners]
        copy = pltpu.make_async_copy(gate_in, gw, sem)
        copy.start()
    first = -6 - owners - loads - 4
    vc_out, mid_out, b_out, c_out = refs[first : first + 4]
    rows = tok.shape[0]
    inner = w.shape[1]
    n = sw.shape[1] // 2
    share = n // owners
    spot = lax.rem(lax.axis_index(axis), owners)
    tiles = pieces(inner, TILE)
    rim = halo[index]
    offset = row(voff)

    def project(j, buf):
        x = jnp.concatenate([rim, tok[...]], axis=0)
        buf[...] = mm(x, w[:, tiles[j]]).astype(BF16).astype(F32)

    def maps():
        mbuf[pl.ds(0, PAD), :] = mm(rim, sw[...]).astype(BF16).astype(F32)
        mbuf[pl.ds(PAD, rows), :] = io[...].astype(F32)
        y = conv_of(mbuf[...], skern[...], row(soff))
        b_out[...] = y[:, :n]
        c_out[...] = y[:, n:]
        bt[...] = y[:, :n].astype(F32).T.astype(BF16)

    def finish(j, buf):
        at = tiles[j]
        vc = conv_of(buf[...], vkern[:, at], offset[:, at])
        vc_out[:, at] = vc
        select = sel[:, at]
        through = mm(thr[...], select)
        state = None
        for q, span in enumerate(pieces(rows)):
            scaled = (vc[span].astype(F32) * mm(close[span, :], select)).astype(BF16)
            made = mm(bt[:, span], scaled)
            if q == 0:
                state = made
            else:
                mid_out[q - 1, :, at] = state.astype(BF16)
                state = state * through[q : q + 1] + made
        hold[...] = state
        for k in range(owners):
            owner = jnp.bitwise_xor(spot, k)
            part = hold[pl.ds(pl.multiple_of(owner * share, share), share), :]
            ends[k][:, index * inner + at.start : index * inner + at.stop] = part.astype(BF16)

    line = lax.broadcasted_iota(jnp.int32, (share, LANES), 0)
    count = rows // CHUNK
    mine = jnp.broadcast_to(thr[...].astype(F32)[count : count + 1], (share, LANES))
    decays = jnp.where(line == 0, mine, 0.0).astype(BF16)
    tail = batch * inner + index * LANES
    for k in range(owners):
        ends[k][:, tail : tail + LANES] = decays
    bufs = (vb0, vb1)
    for j in range(len(tiles)):
        project(j, bufs[j % 2])
        if j == 0:
            maps()
        else:
            finish(j - 1, bufs[(j - 1) % 2])
    finish(len(tiles) - 1, bufs[(len(tiles) - 1) % 2])
    if loads:
        copy.wait()


def inside_kernel(
    head_width, owners, axis, runs, tok, gw, b_rows, c_rows, vc, mid, dtt, cum, cumt, thr, sel, skip,
    *refs,
):
    part_out, grow_out, scores, gb0, gb1 = refs[-5:]
    rows, inner = vc.shape
    tiles = pieces(inner, TILE)
    spans = pieces(rows)
    r = lax.broadcasted_iota(jnp.int32, (CHUNK, CHUNK), 0)
    s = lax.broadcasted_iota(jnp.int32, (CHUNK, CHUNK), 1)
    wide = 2 * head_width
    assert wide == CHUNK
    lane = lax.broadcasted_iota(jnp.int32, (CHUNK, wide), 1)
    flat = lane[:1]

    def project(j, buf):
        buf[...] = mm(tok[...], gw[:, tiles[j]]).astype(BF16)

    def score():
        for q, span in enumerate(spans):
            scores[q] = jnp.where(r >= s, mm_t(c_rows[span, :], b_rows[span, :]), 0.0)

    def finish(j, buf):
        tile = tiles[j]
        base = mm(thr[...], sel[:, tile])
        for q, span in enumerate(spans):
            swish = silu(buf[span, :].astype(F32))
            if q > 0:
                carried = mm(c_rows[span, :], mid[q - 1, :, tile])
            for cut in pieces(TILE, wide):
                at = slice(tile.start + cut.start, tile.start + cut.stop)
                first = at.start // head_width
                block = vc[span, at]
                mixes, halves, columns = [], [], []
                for k in range(2):
                    head = first + k
                    column = jnp.broadcast_to(cum[span, head : head + 1], (CHUNK, CHUNK))
                    columns.append(column)
                    gap = jnp.minimum(column - cumt[q, head : head + 1, :], 0.0)
                    mixes.append(
                        (scores[q] * jnp.exp2(gap) * dtt[q, head : head + 1, :]).astype(BF16)
                    )
                    halves.append(
                        jnp.where((lane >= head_width) == (k == 1), block, jnp.zeros_like(block))
                    )
                mixture = mm(jnp.concatenate(mixes, axis=1), jnp.concatenate(halves, axis=0))
                gain = jnp.where(flat < head_width, skip[first], skip[first + 1])
                mixture = mixture + gain * block.astype(F32)
                rise = jnp.exp2(jnp.where(lane < head_width, columns[0], columns[1]))
                gated = swish[:, cut] * rise
                if q > 0:
                    mixture = mixture + carried[:, cut] * rise
                    gated = gated * base[8 + q : 9 + q, cut]
                grow_out[span, at] = gated.astype(BF16)
                part_out[span, at] = mixture * swish[:, cut]

    bufs = (gb0, gb1)

    def run(first, last):
        for j in range(first, last):
            project(j, bufs[j % 2])
            if j == first:
                score()
            else:
                finish(j - 1, bufs[(j - 1) % 2])
        finish(last - 1, bufs[(last - 1) % 2])

    for first, last, side in runs:
        if side is None:
            run(first, last)
        else:
            half = lax.axis_index(axis) // owners
            pl.when(half == side)(functools.partial(run, first, last))


def total_kernel(owners, axis, index, batch, *refs):
    came, sel = refs[:owners], refs[owners]
    total_out, decay_out, held, lines = refs[-4:]
    inner = sel.shape[1]
    at = slice(index * inner, (index + 1) * inner)
    tail = slice(batch * inner + index * LANES, batch * inner + (index + 1) * LANES)
    spot = lax.rem(lax.axis_index(axis), owners)
    lines[...] = jnp.zeros_like(lines)
    for k in range(owners):
        owner = jnp.bitwise_xor(spot, k)
        held[owner] = came[k][:, at]
        lines[pl.ds(owner, 1), :] = came[k][:, tail].astype(F32)[:1]
    decay_out[...] = mm(lines[...].astype(BF16), sel[...])
    state = held[0].astype(F32)
    for k in range(1, owners):
        state = state * decay_out[pl.ds(k, 1), :] + held[k].astype(F32)
    total_out[...] = state.astype(BF16)


def prefix_kernel(owners, axis, index, *refs):
    came = refs[:owners]
    decay, first = refs[owners : owners + 2]
    outs = refs[-owners - 2 : -2]
    held, made = refs[-2:]
    inner = decay.shape[1]
    at = slice(index * inner, (index + 1) * inner)
    spot = lax.rem(lax.axis_index(axis), owners)
    for k in range(owners):
        held[jnp.bitwise_xor(spot, k)] = came[k][:, at]
    state = first[...].astype(F32)
    for k in range(owners):
        made[k] = state.astype(BF16)
        if k + 1 < owners:
            state = state * decay[pl.ds(k, 1), :] + held[k].astype(F32)
    for k in range(owners):
        outs[k][...] = made[jnp.bitwise_xor(spot, k)]


def enter_kernel(owners, axis, part, grow, c_rows, *refs):
    came = refs[:owners]
    out, sq_out, state = refs[-3:]
    rows, inner = part.shape
    share = came[0].shape[0]
    spot = lax.rem(lax.axis_index(axis), owners)
    for k in range(owners):
        at = pl.multiple_of(jnp.bitwise_xor(spot, k) * share, share)
        state[pl.ds(at, share), :] = came[k][...]
    for span in pieces(rows):
        acc = jnp.zeros((CHUNK, LANES), F32)
        for at in pieces(inner, TILE):
            extra = mm(c_rows[span, :], state[:, at])
            total = part[span, at] + grow[span, at].astype(F32) * extra
            out[span, at] = total
            for cut in pieces(TILE, LANES):
                acc = acc + total[:, cut] * total[:, cut]
        sq_out[:, span] = jnp.sum(acc.T, axis=0, keepdims=True)


def norm_kernel(inner_all, count, *refs):
    squares = refs[:count]
    x, gain = refs[count : count + 2]
    out = refs[-1]
    rows = out.shape[1]
    span = pl.ds(pl.multiple_of(pl.program_id(0) * rows, rows), rows)
    total = squares[0][:, span]
    for ref in squares[1:]:
        total = total + ref[:, span]
    inverse = lax.rsqrt(total / inner_all + EPS)
    columns = jnp.broadcast_to(inverse, (LANES, rows)).T
    gains = row(gain)
    for cut in pieces(out.shape[2], LANES):
        out[0, :, cut] = (x[span, cut] * columns * gains[:, cut]).astype(BF16)


def local(
    tokens,
    gate_weight,
    value_weight,
    state_weight,
    step_weight,
    value_kernel,
    value_offset,
    state_kernel,
    state_offset,
    step_offset,
    decay_rate,
    skip_gain,
    norm_gain,
):
    b, t, d = tokens.shape
    inner = gate_weight.shape[1]
    h = step_weight.shape[1]
    n = state_weight.shape[1] // 2
    head_width = inner // h
    peers = lax.axis_size("seq")
    ranks = lax.axis_size("head")
    owners = peers // 2
    share = n // owners
    chunks = t // CHUNK
    assert h <= SLOT and owners * 2 == peers and owners & (owners - 1) == 0
    assert b == 2 and chunks < 8 and value_kernel.shape[0] == 4
    lines = max(owners, 8)

    def swap(arrays):
        return [arrays[0]] + [
            here(lax.ppermute(arrays[k], "seq", [(s, s ^ k) for s in range(peers)]))
            for k in range(1, owners)
        ]

    halo = here(
        lax.ppermute(tokens[:, t - PAD :], "seq", [(s, s + 1) for s in range(peers - 1)])
    )
    outs = pl.pallas_call(
        functools.partial(front_kernel, head_width),
        in_specs=[FAR] * 6,
        out_specs=[WHOLE] * (3 + 7 * b),
        out_shape=[
            pltpu.VMEM(state_weight.shape, BF16),
            pltpu.VMEM(value_weight.shape, BF16),
            pltpu.VMEM((LANES, inner), BF16),
        ]
        + [
            pltpu.VMEM((t, d), BF16),
            pltpu.VMEM((t, 2 * n), BF16),
            pltpu.VMEM((t, LANES), BF16),
            pltpu.VMEM((16, LANES), BF16),
            pltpu.VMEM((t, LANES), F32),
            pltpu.VMEM((chunks, SLOT, CHUNK), F32),
            pltpu.VMEM((chunks, SLOT, CHUNK), F32),
        ]
        * b,
        scratch_shapes=[
            pltpu.VMEM((h, d), BF16),
            pltpu.VMEM((h,), F32),
            pltpu.VMEM((h,), F32),
            pltpu.VMEM((LANES, d), BF16),
            pltpu.VMEM((8, LANES), F32),
            pltpu.SemaphoreType.DMA((b + 5,)),
        ],
        compiler_params=params(16),
        name="front",
        cost_estimate=cost(2 * b * t * d * (2 * n + LANES)),
    )(*map(far, (tokens, state_weight, step_weight.T, value_weight, step_offset, decay_rate)))
    sw, w, sel = outs[:3]
    fronts = [outs[3 + 7 * i : 10 + 7 * i] for i in range(b)]

    wide = b * (inner + LANES)

    def values(i, ends):
        tok, io, close, thr, _, _, _ = fronts[i]
        loads = i == b - 1
        inputs = 12 + loads
        return pl.pallas_call(
            functools.partial(values_kernel, owners, "seq", i, b),
            in_specs=[WHOLE] * 12 + [FAR] * loads + [WHOLE] * len(ends),
            out_specs=[WHOLE] * (4 + loads + owners),
            out_shape=[
                pltpu.VMEM((t, inner), BF16),
                pltpu.VMEM((chunks - 1, n, inner), BF16),
                pltpu.VMEM((t, n), BF16),
                pltpu.VMEM((t, n), BF16),
            ]
            + [pltpu.VMEM(gate_weight.shape, BF16)] * loads
            + [pltpu.VMEM((share, wide), BF16)] * owners,
            scratch_shapes=[
                pltpu.SemaphoreType.DMA,
                pltpu.VMEM((n, t), BF16),
                pltpu.VMEM((t + PAD, 2 * n), F32),
                pltpu.VMEM((n, TILE), F32),
                pltpu.VMEM((t + PAD, TILE), F32),
                pltpu.VMEM((t + PAD, TILE), F32),
            ],
            input_output_aliases={inputs + k: 4 + loads + k for k in range(len(ends))},
            compiler_params=params(16),
            name=f"values{i}",
            cost_estimate=cost(2 * t * d * inner),
        )(
            tok, io, close, thr, halo, w, sw, value_kernel, value_offset,
            state_kernel, state_offset, sel, *[far(gate_weight)] * loads, *ends,
        )

    made, ends = [], ()
    for i in range(b):
        outs = values(i, ends)
        made.append(outs[:4])
        ends = outs[-owners:]
    gw = outs[4]

    def inside(i, runs, gw, made, prior, after):
        tok, _, _, thr, cum, cumt, dtt = fronts[i]
        vc, mid, b_rows, c_rows = made[:4]
        return pl.pallas_call(
            functools.partial(inside_kernel, head_width, owners, "seq", runs),
            in_specs=[WHOLE] * 11 + [SCALARS] + [WHOLE] * (len(prior) + len(after)),
            out_specs=[WHOLE] * 2,
            out_shape=[pltpu.VMEM((t, inner), F32), pltpu.VMEM((t, inner), BF16)],
            scratch_shapes=[
                pltpu.VMEM((chunks, CHUNK, CHUNK), F32),
                pltpu.VMEM((t, TILE), BF16),
                pltpu.VMEM((t, TILE), BF16),
            ],
            input_output_aliases={12 + k: k for k in range(len(prior))},
            compiler_params=params(16),
            name=f"inside{i}",
            cost_estimate=cost(2.5 * t * d * inner),
        )(
            tok, gw, b_rows, c_rows, vc, mid, dtt, cum, cumt, thr, sel, skip_gain,
            *prior, *after,
        )

    def total(i, came, after):
        return pl.pallas_call(
            functools.partial(total_kernel, owners, "seq", i, b),
            in_specs=[WHOLE] * (owners + 1 + len(after)),
            out_specs=[WHOLE] * 2,
            out_shape=[pltpu.VMEM((share, inner), BF16), pltpu.VMEM((lines, inner), F32)],
            scratch_shapes=[
                pltpu.VMEM((owners, share, inner), BF16),
                pltpu.VMEM((lines, LANES), F32),
            ],
            compiler_params=params(16),
            name=f"total{i}",
        )(*came, sel, *after)

    def prefix(i, came, decay, first, after):
        return pl.pallas_call(
            functools.partial(prefix_kernel, owners, "seq", i),
            in_specs=[WHOLE] * (owners + 2 + len(after)),
            out_specs=[WHOLE] * owners,
            out_shape=[pltpu.VMEM((share, inner), BF16)] * owners,
            scratch_shapes=[
                pltpu.VMEM((owners, share, inner), BF16),
                pltpu.VMEM((owners, share, inner), BF16),
            ],
            compiler_params=params(16),
            name=f"prefix{i}",
        )(*came, decay, first, *after)

    def across(x):
        return here(lax.ppermute(x, "seq", [(s, s + owners) for s in range(owners)]))

    def enter(i, part, grow, c_rows, states, after):
        x, sq = pl.pallas_call(
            functools.partial(enter_kernel, owners, "seq"),
            in_specs=[WHOLE] * (3 + owners + len(after)),
            out_specs=[WHOLE] * 2,
            out_shape=[pltpu.VMEM((t, inner), F32), pltpu.VMEM((1, t), F32)],
            scratch_shapes=[pltpu.VMEM((n, inner), BF16)],
            compiler_params=params(16),
            name=f"enter{i}",
        )(part, grow, c_rows, *states, *after)
        return x, [sq] + [
            here(lax.ppermute(sq, "head", [(s, (s + k) % ranks) for s in range(ranks)]))
            for k in range(1, ranks)
        ]

    def norm(i, x, squares, into):
        rows = min(t, 256)
        return pl.pallas_call(
            functools.partial(norm_kernel, inner * ranks, ranks),
            grid=(t // rows,),
            in_specs=[WHOLE] * (ranks + 2) + [FAR] * len(into),
            out_specs=pl.BlockSpec((1, rows, inner), lambda q: (i, q, 0)),
            out_shape=jax.ShapeDtypeStruct((b, t, inner), BF16),
            input_output_aliases={ranks + 2: 0} if into else {},
            compiler_params=params(16),
            name=f"norm{i}",
        )(*squares, x, norm_gain, *into)

    came = swap(ends)
    tiles = inner // TILE
    ahead = tiles // 2 + 1
    part0, grow0 = inside(0, ((0, tiles, None),), gw, made[0], (), ())
    early = inside(1, ((0, ahead, 0),), gw, made[1], (), (grow0,))
    whole0, decay0 = total(0, came, (early[1],))
    first0 = across(whole0)
    whole1, decay1 = total(1, came, (whole0,))
    first1 = across(whole1)
    late = ((0, ahead, 1), (ahead, tiles, None))
    part1, grow1 = inside(1, late, gw, made[1], early, (whole1,))
    sent0 = prefix(0, came, decay0, first0, (grow1,))
    back0 = swap(sent0)
    sent1 = prefix(1, came, decay1, first1, (sent0[1],))
    back1 = swap(sent1)
    x0, squares0 = enter(0, part0, grow0, made[0][3], back0, (sent1[1],))
    x1, squares1 = enter(1, part1, grow1, made[1][3], back1, (squares0[0],))
    out = norm(0, x0, squares0, ())
    return norm(1, x1, squares1, (out,))


def solution(mesh):
    return jax.shard_map(
        local,
        mesh=mesh,
        in_specs=(
            P(None, "seq", None),
            P(None, "head"),
            P(None, "head"),
            P(),
            P(None, "head"),
            P(None, "head"),
            P("head"),
            P(),
            P(),
            P("head"),
            P("head"),
            P("head"),
            P("head"),
        ),
        out_specs=P(None, "seq", "head"),
        check_vma=False,
    )
```

```python
import functools
import jax
import jax.numpy as jnp
from jax import lax
from jax.experimental import pallas as pl
from jax.experimental.pallas import tpu as pltpu
from jax.sharding import PartitionSpec as P

EPS = 1e-05
LOG2E = 1.4426950408889634
PAD = 16
CHUNK = 128
TILE = 256
LANES = 128
SLOT = 32
F32 = jnp.float32
BF16 = jnp.bfloat16
WHOLE = pl.BlockSpec(memory_space=pltpu.VMEM)
FAR = pl.BlockSpec(memory_space=pltpu.HBM)
SCALARS = pl.BlockSpec(memory_space=pltpu.SMEM)


def here(x):
    return pltpu.with_memory_space_constraint(x, pltpu.VMEM)


def far(x):
    return pltpu.with_memory_space_constraint(x, pltpu.HBM)


def params(mib):
    return pltpu.CompilerParams(vmem_limit_bytes=mib << 20)


def cost(flops):
    return pl.CostEstimate(flops=int(flops), transcendentals=0, bytes_accessed=0)


def mm(a, b):
    return jnp.dot(a, b, preferred_element_type=F32)


def mm_t(a, b):
    return lax.dot_general(a, b, (((1,), (1,)), ((), ())), preferred_element_type=F32)


def silu(x):
    half = 0.5 * x
    return half + half * jnp.tanh(half)


def row(ref):
    return ref[...].reshape(1, ref.shape[0])


def pieces(total, size=CHUNK):
    return [slice(k * size, (k + 1) * size) for k in range(total // size)]


def head_select(width, head_width):
    lane = lax.broadcasted_iota(jnp.int32, (LANES, width), 0)
    col = lax.broadcasted_iota(jnp.int32, (LANES, width), 1)
    start = (lane & (SLOT - 1)) * head_width
    hit = (lane >= SLOT) & (lane < 3 * SLOT) & (col >= start) & (col < start + head_width)
    return jnp.where(hit, 1.0, 0.0).astype(BF16)


def conv_of(x, kernel, offset):
    back = pltpu.roll(x, 1, 0)
    near = offset + kernel[3:4] * x + kernel[2:3] * back
    deep = kernel[1:2] * x + kernel[0:1] * back
    return silu((near + pltpu.roll(deep, 2, 0))[PAD:]).astype(BF16)


def front_kernel(head_width, *refs):
    tok_in, sw_in, twt_in, w_in, toff_in, rate_in = refs[:6]
    batch = tok_in.shape[0]
    sw, w, sel = refs[6:9]
    per_batch = [refs[9 + 7 * i : 16 + 7 * i] for i in range(batch)]
    twt, toff, rate, tws, vec, sem = refs[9 + 7 * batch :]
    rows = tok_in.shape[1]
    heads = twt.shape[0]
    token_copies = [
        pltpu.make_async_copy(tok_in.at[i], per_batch[i][0], sem.at[i]) for i in range(batch)
    ]
    copies = [
        pltpu.make_async_copy(twt_in, twt, sem.at[batch]),
        pltpu.make_async_copy(toff_in, toff, sem.at[batch + 1]),
        pltpu.make_async_copy(rate_in, rate, sem.at[batch + 2]),
        pltpu.make_async_copy(sw_in, sw, sem.at[batch + 3]),
        pltpu.make_async_copy(w_in.at[:, pl.ds(0, w.shape[1])], w, sem.at[batch + 4]),
    ]
    for copy in copies[:3] + [token_copies[0], copies[3]] + token_copies[1:] + [copies[4]]:
        copy.start()
    sel[...] = head_select(sel.shape[1], head_width)
    tws[...] = jnp.zeros_like(tws)
    vec[...] = jnp.zeros_like(vec)
    for copy in copies[:3]:
        copy.wait()
    tws[pl.ds(0, heads), :] = twt[...]
    vec[pl.ds(0, 1), pl.ds(0, heads)] = row(toff)
    vec[pl.ds(1, 1), pl.ds(0, heads)] = row(rate)
    columns = vec[...].T[:SLOT]
    offset = columns[:, 0:1]
    scale = columns[:, 1:2] * (-LOG2E)
    r = lax.broadcasted_iota(jnp.int32, (CHUNK, CHUNK), 0)
    c = lax.broadcasted_iota(jnp.int32, (CHUNK, CHUNK), 1)
    tri = jnp.where(r <= c, 1.0, 0.0).astype(BF16)
    lane = lax.broadcasted_iota(jnp.int32, (SLOT, LANES), 1)
    blank = jnp.zeros((SLOT, LANES), F32)

    def turned(first, x):
        hi = x.astype(BF16).astype(F32)
        return jnp.concatenate([first, hi, x - hi, blank], axis=0).T

    for i in range(batch):
        tok, io_out, close_out, thr_out, cum_out, cumt_out, dtt_out = per_batch[i]
        token_copies[i].wait()
        z = mm_t(tws[...], tok[...]) + offset
        dt = jnp.maximum(z, 0.0) + jnp.log1p(jnp.exp(-jnp.abs(z)))
        if i == 0:
            copies[3].wait()
        io_out[...] = mm(tok[...], sw[...]).astype(BF16)
        log_decay = dt * scale
        base = jnp.zeros((SLOT, 1), F32)
        table = blank
        for q, span in enumerate(pieces(rows)):
            part = log_decay[:, span]
            hi = part.astype(BF16)
            rest = part - hi.astype(F32)
            mid = rest.astype(BF16)
            low = (rest - mid.astype(F32)).astype(BF16)
            cum = mm(hi, tri) + (mm(mid, tri) + mm(low, tri))
            last = cum[:, CHUNK - 1 :]
            cumt_out[q] = cum
            dtt_out[q] = dt[:, span]
            both = turned(cum, jnp.exp2(last - cum) * dt[:, span])
            cum_out[span, :] = both
            close_out[span, :] = both.astype(BF16)
            table = jnp.where(lane == q, last, table)
            table = jnp.where(lane == 8 + q, base, table)
            base = base + last
        table = jnp.where(lane == rows // CHUNK, base, table)
        thr_out[...] = turned(blank, jnp.exp2(table))[:16].astype(BF16)
    copies[4].wait()


def values_kernel(owners, axis, index, batch, *refs):
    tok, io, close, thr, halo, wa, sw, vkern, voff, skern, soff, sel, extra = refs[:13]
    sem = refs[-6]
    bt, mbuf, hold, vb0, vb1 = refs[-5:]
    ends = refs[-6 - owners : -6]
    vc_out, mid_out, b_out, c_out, big = refs[-11 - owners : -6 - owners]
    cols = wa.shape[1]
    if index == 0:
        wb = big
        copy = pltpu.make_async_copy(extra.at[:, pl.ds(cols, big.shape[1])], big, sem)
    else:
        wb = extra
        copy = pltpu.make_async_copy(refs[13], big, sem)
    copy.start()
    rows = tok.shape[0]
    inner = vc_out.shape[1]
    n = sw.shape[1] // 2
    share = n // owners
    spot = lax.rem(lax.axis_index(axis), owners)
    tiles = pieces(inner, TILE)
    rim = halo[index]
    offset = row(voff)

    def project(j, buf):
        x = jnp.concatenate([rim, tok[...]], axis=0)
        at = tiles[j]
        late = at.start >= cols
        weight = wb[:, at.start - cols : at.stop - cols] if late else wa[:, at]
        buf[...] = mm(x, weight).astype(BF16).astype(F32)

    def maps():
        mbuf[pl.ds(0, PAD), :] = mm(rim, sw[...]).astype(BF16).astype(F32)
        mbuf[pl.ds(PAD, rows), :] = io[...].astype(F32)
        y = conv_of(mbuf[...], skern[...], row(soff))
        b_out[...] = y[:, :n]
        c_out[...] = y[:, n:]
        bt[...] = y[:, :n].astype(F32).T.astype(BF16)

    def finish(j, buf):
        at = tiles[j]
        vc = conv_of(buf[...], vkern[:, at], offset[:, at])
        vc_out[:, at] = vc
        select = sel[:, at]
        through = mm(thr[...], select)
        state = None
        for q, span in enumerate(pieces(rows)):
            scaled = (vc[span].astype(F32) * mm(close[span, :], select)).astype(BF16)
            made = mm(bt[:, span], scaled)
            if q == 0:
                state = made
            else:
                mid_out[q - 1, :, at] = state.astype(BF16)
                state = state * through[q : q + 1] + made
        hold[...] = state
        for k in range(owners):
            owner = jnp.bitwise_xor(spot, k)
            part = hold[pl.ds(pl.multiple_of(owner * share, share), share), :]
            ends[k][:, index * inner + at.start : index * inner + at.stop] = part.astype(BF16)

    line = lax.broadcasted_iota(jnp.int32, (share, LANES), 0)
    count = rows // CHUNK
    mine = jnp.broadcast_to(thr[...].astype(F32)[count : count + 1], (share, LANES))
    decays = jnp.where(line == 0, mine, 0.0).astype(BF16)
    tail = batch * inner + index * LANES
    for k in range(owners):
        ends[k][:, tail : tail + LANES] = decays
    bufs = (vb0, vb1)
    for j in range(len(tiles)):
        if index == 0 and tiles[j].start == cols:
            copy.wait()
        project(j, bufs[j % 2])
        if j == 0:
            maps()
        else:
            finish(j - 1, bufs[(j - 1) % 2])
    finish(len(tiles) - 1, bufs[(len(tiles) - 1) % 2])
    if index > 0:
        copy.wait()


def inside_kernel(
    head_width, owners, axis, runs, tok, gw, b_rows, c_rows, vc, mid, dtt, cum, cumt, thr, sel, skip,
    *refs,
):
    part_out, grow_out, scores, gb0, gb1 = refs[-5:]
    rows, inner = vc.shape
    tiles = pieces(inner, TILE)
    spans = pieces(rows)
    r = lax.broadcasted_iota(jnp.int32, (CHUNK, CHUNK), 0)
    s = lax.broadcasted_iota(jnp.int32, (CHUNK, CHUNK), 1)
    wide = 2 * head_width
    assert wide == CHUNK
    lane = lax.broadcasted_iota(jnp.int32, (CHUNK, wide), 1)
    flat = lane[:1]

    def project(j, buf):
        buf[...] = mm(tok[...], gw[:, tiles[j]]).astype(BF16)

    def score():
        for q, span in enumerate(spans):
            scores[q] = jnp.where(r >= s, mm_t(c_rows[span, :], b_rows[span, :]), 0.0)

    def finish(j, buf):
        tile = tiles[j]
        base = mm(thr[...], sel[:, tile])
        for q, span in enumerate(spans):
            swish = silu(buf[span, :].astype(F32))
            if q > 0:
                carried = mm(c_rows[span, :], mid[q - 1, :, tile])
            for cut in pieces(TILE, wide):
                at = slice(tile.start + cut.start, tile.start + cut.stop)
                first = at.start // head_width
                block = vc[span, at]
                mixes, halves, columns = [], [], []
                for k in range(2):
                    head = first + k
                    column = jnp.broadcast_to(cum[span, head : head + 1], (CHUNK, CHUNK))
                    columns.append(column)
                    gap = jnp.minimum(column - cumt[q, head : head + 1, :], 0.0)
                    mixes.append(
                        (scores[q] * jnp.exp2(gap) * dtt[q, head : head + 1, :]).astype(BF16)
                    )
                    halves.append(
                        jnp.where((lane >= head_width) == (k == 1), block, jnp.zeros_like(block))
                    )
                mixture = mm(jnp.concatenate(mixes, axis=1), jnp.concatenate(halves, axis=0))
                gain = jnp.where(flat < head_width, skip[first], skip[first + 1])
                mixture = mixture + gain * block.astype(F32)
                rise = jnp.exp2(jnp.where(lane < head_width, columns[0], columns[1]))
                gated = swish[:, cut] * rise
                if q > 0:
                    mixture = mixture + carried[:, cut] * rise
                    gated = gated * base[8 + q : 9 + q, cut]
                grow_out[span, at] = gated.astype(BF16)
                part_out[span, at] = mixture * swish[:, cut]

    bufs = (gb0, gb1)

    def run(first, last):
        for j in range(first, last):
            project(j, bufs[j % 2])
            if j == first:
                score()
            else:
                finish(j - 1, bufs[(j - 1) % 2])
        finish(last - 1, bufs[(last - 1) % 2])

    for first, last, side in runs:
        if side is None:
            run(first, last)
        else:
            half = lax.axis_index(axis) // owners
            pl.when(half == side)(functools.partial(run, first, last))


def total_kernel(owners, axis, index, batch, *refs):
    came, sel = refs[:owners], refs[owners]
    total_out, decay_out, held, lines = refs[-4:]
    inner = sel.shape[1]
    at = slice(index * inner, (index + 1) * inner)
    tail = slice(batch * inner + index * LANES, batch * inner + (index + 1) * LANES)
    spot = lax.rem(lax.axis_index(axis), owners)
    lines[...] = jnp.zeros_like(lines)
    for k in range(owners):
        owner = jnp.bitwise_xor(spot, k)
        held[owner] = came[k][:, at]
        lines[pl.ds(owner, 1), :] = came[k][:, tail].astype(F32)[:1]
    decay_out[...] = mm(lines[...].astype(BF16), sel[...])
    state = held[0].astype(F32)
    for k in range(1, owners):
        state = state * decay_out[pl.ds(k, 1), :] + held[k].astype(F32)
    total_out[...] = state.astype(BF16)


def prefix_kernel(owners, axis, index, *refs):
    came = refs[:owners]
    decay, first = refs[owners : owners + 2]
    outs = refs[-owners - 2 : -2]
    held, made = refs[-2:]
    inner = decay.shape[1]
    at = slice(index * inner, (index + 1) * inner)
    spot = lax.rem(lax.axis_index(axis), owners)
    for k in range(owners):
        held[jnp.bitwise_xor(spot, k)] = came[k][:, at]
    state = first[...].astype(F32)
    for k in range(owners):
        made[k] = state.astype(BF16)
        if k + 1 < owners:
            state = state * decay[pl.ds(k, 1), :] + held[k].astype(F32)
    for k in range(owners):
        outs[k][...] = made[jnp.bitwise_xor(spot, k)]


def enter_kernel(owners, axis, part, grow, c_rows, *refs):
    came = refs[:owners]
    out, sq_out, state = refs[-3:]
    rows, inner = part.shape
    share = came[0].shape[0]
    spot = lax.rem(lax.axis_index(axis), owners)
    for k in range(owners):
        at = pl.multiple_of(jnp.bitwise_xor(spot, k) * share, share)
        state[pl.ds(at, share), :] = came[k][...]
    for span in pieces(rows):
        acc = jnp.zeros((CHUNK, LANES), F32)
        for at in pieces(inner, TILE):
            extra = mm(c_rows[span, :], state[:, at])
            total = part[span, at] + grow[span, at].astype(F32) * extra
            out[span, at] = total
            for cut in pieces(TILE, LANES):
                acc = acc + total[:, cut] * total[:, cut]
        sq_out[:, span] = jnp.sum(acc.T, axis=0, keepdims=True)


def norm_kernel(inner_all, count, *refs):
    squares = refs[:count]
    x, gain = refs[count : count + 2]
    out = refs[-1]
    rows = out.shape[1]
    span = pl.ds(pl.multiple_of(pl.program_id(0) * rows, rows), rows)
    total = squares[0][:, span]
    for ref in squares[1:]:
        total = total + ref[:, span]
    inverse = lax.rsqrt(total / inner_all + EPS)
    columns = jnp.broadcast_to(inverse, (LANES, rows)).T
    gains = row(gain)
    for cut in pieces(out.shape[2], LANES):
        out[0, :, cut] = (x[span, cut] * columns * gains[:, cut]).astype(BF16)


def local(
    tokens,
    gate_weight,
    value_weight,
    state_weight,
    step_weight,
    value_kernel,
    value_offset,
    state_kernel,
    state_offset,
    step_offset,
    decay_rate,
    skip_gain,
    norm_gain,
):
    b, t, d = tokens.shape
    inner = gate_weight.shape[1]
    h = step_weight.shape[1]
    n = state_weight.shape[1] // 2
    head_width = inner // h
    peers = lax.axis_size("seq")
    ranks = lax.axis_size("head")
    owners = peers // 2
    share = n // owners
    chunks = t // CHUNK
    assert h <= SLOT and owners * 2 == peers and owners & (owners - 1) == 0
    assert b == 2 and chunks < 8 and value_kernel.shape[0] == 4
    lines = max(owners, 8)
    early_cols = (inner // TILE + 1) // 2 * TILE

    def swap(arrays):
        return [arrays[0]] + [
            here(lax.ppermute(arrays[k], "seq", [(s, s ^ k) for s in range(peers)]))
            for k in range(1, owners)
        ]

    halo = here(
        lax.ppermute(tokens[:, t - PAD :], "seq", [(s, s + 1) for s in range(peers - 1)])
    )
    outs = pl.pallas_call(
        functools.partial(front_kernel, head_width),
        in_specs=[FAR] * 6,
        out_specs=[WHOLE] * (3 + 7 * b),
        out_shape=[
            pltpu.VMEM(state_weight.shape, BF16),
            pltpu.VMEM((d, early_cols), BF16),
            pltpu.VMEM((LANES, inner), BF16),
        ]
        + [
            pltpu.VMEM((t, d), BF16),
            pltpu.VMEM((t, 2 * n), BF16),
            pltpu.VMEM((t, LANES), BF16),
            pltpu.VMEM((16, LANES), BF16),
            pltpu.VMEM((t, LANES), F32),
            pltpu.VMEM((chunks, SLOT, CHUNK), F32),
            pltpu.VMEM((chunks, SLOT, CHUNK), F32),
        ]
        * b,
        scratch_shapes=[
            pltpu.VMEM((h, d), BF16),
            pltpu.VMEM((h,), F32),
            pltpu.VMEM((h,), F32),
            pltpu.VMEM((SLOT, d), BF16),
            pltpu.VMEM((LANES, LANES), F32),
            pltpu.SemaphoreType.DMA((b + 5,)),
        ],
        compiler_params=params(16),
        name="front",
        cost_estimate=cost(2 * b * t * d * (2 * n + LANES)),
    )(*map(far, (tokens, state_weight, step_weight.T, value_weight, step_offset, decay_rate)))
    sw, w, sel = outs[:3]
    fronts = [outs[3 + 7 * i : 10 + 7 * i] for i in range(b)]

    wide = b * (inner + LANES)

    def values(i, rest, ends):
        tok, io, close, thr, _, _, _ = fronts[i]
        big = gate_weight.shape if i else (d, inner - early_cols)
        extra = (rest, far(gate_weight)) if i else (far(value_weight),)
        return pl.pallas_call(
            functools.partial(values_kernel, owners, "seq", i, b),
            in_specs=[WHOLE] * 12 + ([WHOLE, FAR] if i else [FAR]) + [WHOLE] * len(ends),
            out_specs=[WHOLE] * (5 + owners),
            out_shape=[
                pltpu.VMEM((t, inner), BF16),
                pltpu.VMEM((chunks - 1, n, inner), BF16),
                pltpu.VMEM((t, n), BF16),
                pltpu.VMEM((t, n), BF16),
                pltpu.VMEM(big, BF16),
            ]
            + [pltpu.VMEM((share, wide), BF16)] * owners,
            scratch_shapes=[
                pltpu.SemaphoreType.DMA,
                pltpu.VMEM((n, t), BF16),
                pltpu.VMEM((t + PAD, 2 * n), F32),
                pltpu.VMEM((n, TILE), F32),
                pltpu.VMEM((t + PAD, TILE), F32),
                pltpu.VMEM((t + PAD, TILE), F32),
            ],
            input_output_aliases={12 + len(extra) + k: 5 + k for k in range(len(ends))},
            compiler_params=params(16),
            name=f"values{i}",
            cost_estimate=cost(2 * t * d * inner),
        )(
            tok, io, close, thr, halo, w, sw, value_kernel, value_offset,
            state_kernel, state_offset, sel, *extra, *ends,
        )

    made, ends, big = [], (), None
    for i in range(b):
        outs = values(i, big, ends)
        made.append(outs[:4])
        big, ends = outs[4], outs[5:]
    gw = big

    def inside(i, runs, gw, made, prior, after):
        tok, _, _, thr, cum, cumt, dtt = fronts[i]
        vc, mid, b_rows, c_rows = made[:4]
        return pl.pallas_call(
            functools.partial(inside_kernel, head_width, owners, "seq", runs),
            in_specs=[WHOLE] * 11 + [SCALARS] + [WHOLE] * (len(prior) + len(after)),
            out_specs=[WHOLE] * 2,
            out_shape=[pltpu.VMEM((t, inner), F32), pltpu.VMEM((t, inner), BF16)],
            scratch_shapes=[
                pltpu.VMEM((chunks, CHUNK, CHUNK), F32),
                pltpu.VMEM((t, TILE), BF16),
                pltpu.VMEM((t, TILE), BF16),
            ],
            input_output_aliases={12 + k: k for k in range(len(prior))},
            compiler_params=params(16),
            name=f"inside{i}",
            cost_estimate=cost(2.5 * t * d * inner),
        )(
            tok, gw, b_rows, c_rows, vc, mid, dtt, cum, cumt, thr, sel, skip_gain,
            *prior, *after,
        )

    def total(i, came, after):
        return pl.pallas_call(
            functools.partial(total_kernel, owners, "seq", i, b),
            in_specs=[WHOLE] * (owners + 1 + len(after)),
            out_specs=[WHOLE] * 2,
            out_shape=[pltpu.VMEM((share, inner), BF16), pltpu.VMEM((lines, inner), F32)],
            scratch_shapes=[
                pltpu.VMEM((owners, share, inner), BF16),
                pltpu.VMEM((lines, LANES), F32),
            ],
            compiler_params=params(16),
            name=f"total{i}",
        )(*came, sel, *after)

    def prefix(i, came, decay, first, after):
        return pl.pallas_call(
            functools.partial(prefix_kernel, owners, "seq", i),
            in_specs=[WHOLE] * (owners + 2 + len(after)),
            out_specs=[WHOLE] * owners,
            out_shape=[pltpu.VMEM((share, inner), BF16)] * owners,
            scratch_shapes=[
                pltpu.VMEM((owners, share, inner), BF16),
                pltpu.VMEM((owners, share, inner), BF16),
            ],
            compiler_params=params(16),
            name=f"prefix{i}",
        )(*came, decay, first, *after)

    def across(x):
        return here(lax.ppermute(x, "seq", [(s, s + owners) for s in range(owners)]))

    def enter(i, part, grow, c_rows, states, after):
        x, sq = pl.pallas_call(
            functools.partial(enter_kernel, owners, "seq"),
            in_specs=[WHOLE] * (3 + owners + len(after)),
            out_specs=[WHOLE] * 2,
            out_shape=[pltpu.VMEM((t, inner), F32), pltpu.VMEM((1, t), F32)],
            scratch_shapes=[pltpu.VMEM((n, inner), BF16)],
            compiler_params=params(16),
            name=f"enter{i}",
        )(part, grow, c_rows, *states, *after)
        return x, [sq] + [
            here(lax.ppermute(sq, "head", [(s, (s + k) % ranks) for s in range(ranks)]))
            for k in range(1, ranks)
        ]

    def norm(i, x, squares, into):
        rows = min(t, 256)
        return pl.pallas_call(
            functools.partial(norm_kernel, inner * ranks, ranks),
            grid=(t // rows,),
            in_specs=[WHOLE] * (ranks + 2) + [FAR] * len(into),
            out_specs=pl.BlockSpec((1, rows, inner), lambda q: (i, q, 0)),
            out_shape=jax.ShapeDtypeStruct((b, t, inner), BF16),
            input_output_aliases={ranks + 2: 0} if into else {},
            compiler_params=params(16),
            name=f"norm{i}",
        )(*squares, x, norm_gain, *into)

    came = swap(ends)
    tiles = inner // TILE
    ahead = tiles // 2 + 1
    part0, grow0 = inside(0, ((0, tiles, None),), gw, made[0], (), ())
    early = inside(1, ((0, ahead, 0),), gw, made[1], (), (grow0,))
    whole0, decay0 = total(0, came, (early[1],))
    first0 = across(whole0)
    whole1, decay1 = total(1, came, (whole0,))
    first1 = across(whole1)
    late = ((0, ahead, 1), (ahead, tiles, None))
    part1, grow1 = inside(1, late, gw, made[1], early, (whole1,))
    sent0 = prefix(0, came, decay0, first0, (grow1,))
    back0 = swap(sent0)
    sent1 = prefix(1, came, decay1, first1, (sent0[1],))
    back1 = swap(sent1)
    x0, squares0 = enter(0, part0, grow0, made[0][3], back0, (sent1[1],))
    x1, squares1 = enter(1, part1, grow1, made[1][3], back1, (squares0[0],))
    out = norm(0, x0, squares0, ())
    return norm(1, x1, squares1, (out,))


def solution(mesh):
    return jax.shard_map(
        local,
        mesh=mesh,
        in_specs=(
            P(None, "seq", None),
            P(None, "head"),
            P(None, "head"),
            P(),
            P(None, "head"),
            P(None, "head"),
            P("head"),
            P(),
            P(),
            P("head"),
            P("head"),
            P("head"),
            P("head"),
        ),
        out_specs=P(None, "seq", "head"),
        check_vma=False,
    )
```

```python
import functools
import jax
import jax.numpy as jnp
from jax import lax
from jax.experimental import pallas as pl
from jax.experimental.pallas import tpu as pltpu
from jax.sharding import PartitionSpec as P

EPS = 1e-05
LOG2E = 1.4426950408889634
PAD = 16
CHUNK = 128
TILE = 256
LANES = 128
SLOT = 32
F32 = jnp.float32
BF16 = jnp.bfloat16
WHOLE = pl.BlockSpec(memory_space=pltpu.VMEM)
FAR = pl.BlockSpec(memory_space=pltpu.HBM)
SCALARS = pl.BlockSpec(memory_space=pltpu.SMEM)


def here(x):
    return pltpu.with_memory_space_constraint(x, pltpu.VMEM)


def far(x):
    return pltpu.with_memory_space_constraint(x, pltpu.HBM)


def params(mib):
    return pltpu.CompilerParams(vmem_limit_bytes=mib << 20)


def cost(flops):
    return pl.CostEstimate(flops=int(flops), transcendentals=0, bytes_accessed=0)


def mm(a, b):
    return jnp.dot(a, b, preferred_element_type=F32)


def mm_t(a, b):
    return lax.dot_general(a, b, (((1,), (1,)), ((), ())), preferred_element_type=F32)


def silu(x):
    half = 0.5 * x
    return half + half * jnp.tanh(half)


def row(ref):
    return ref[...].reshape(1, ref.shape[0])


def pieces(total, size=CHUNK):
    return [slice(k * size, (k + 1) * size) for k in range(total // size)]


def head_select(width, head_width):
    lane = lax.broadcasted_iota(jnp.int32, (LANES, width), 0)
    col = lax.broadcasted_iota(jnp.int32, (LANES, width), 1)
    start = (lane & (SLOT - 1)) * head_width
    hit = (lane >= SLOT) & (lane < 3 * SLOT) & (col >= start) & (col < start + head_width)
    return jnp.where(hit, 1.0, 0.0).astype(BF16)


def conv_of(x, kernel, offset):
    back = pltpu.roll(x, 1, 0)
    near = offset + kernel[3:4] * x + kernel[2:3] * back
    deep = kernel[1:2] * x + kernel[0:1] * back
    return silu((near + pltpu.roll(deep, 2, 0))[PAD:])


def front_kernel(head_width, *refs):
    tok_in, sw_in, twt_in, w_in, toff_in, rate_in = refs[:6]
    batch = tok_in.shape[0]
    sw, w, sel = refs[6:9]
    per_batch = [refs[9 + 7 * i : 16 + 7 * i] for i in range(batch)]
    twt, toff, rate, tws, vec, sem = refs[9 + 7 * batch :]
    rows = tok_in.shape[1]
    heads = twt.shape[0]
    token_copies = [
        pltpu.make_async_copy(tok_in.at[i], per_batch[i][0], sem.at[i]) for i in range(batch)
    ]
    copies = [
        pltpu.make_async_copy(twt_in, twt, sem.at[batch]),
        pltpu.make_async_copy(toff_in, toff, sem.at[batch + 1]),
        pltpu.make_async_copy(rate_in, rate, sem.at[batch + 2]),
        pltpu.make_async_copy(sw_in, sw, sem.at[batch + 3]),
        pltpu.make_async_copy(w_in.at[:, pl.ds(0, w.shape[1])], w, sem.at[batch + 4]),
    ]
    for copy in copies[:3] + [token_copies[0], copies[3]] + token_copies[1:] + [copies[4]]:
        copy.start()
    sel[...] = head_select(sel.shape[1], head_width)
    tws[...] = jnp.zeros_like(tws)
    vec[...] = jnp.zeros_like(vec)
    for copy in copies[:3]:
        copy.wait()
    tws[pl.ds(0, heads), :] = twt[...]
    vec[pl.ds(0, 1), pl.ds(0, heads)] = row(toff)
    vec[pl.ds(1, 1), pl.ds(0, heads)] = row(rate)
    columns = vec[...].T[:SLOT]
    offset = columns[:, 0:1]
    scale = columns[:, 1:2] * (-LOG2E)
    r = lax.broadcasted_iota(jnp.int32, (CHUNK, CHUNK), 0)
    c = lax.broadcasted_iota(jnp.int32, (CHUNK, CHUNK), 1)
    tri = jnp.where(r <= c, 1.0, 0.0).astype(BF16)
    lane = lax.broadcasted_iota(jnp.int32, (SLOT, LANES), 1)
    blank = jnp.zeros((SLOT, LANES), F32)

    def turned(first, x):
        hi = x.astype(BF16).astype(F32)
        return jnp.concatenate([first, hi, x - hi, blank], axis=0).T

    for i in range(batch):
        tok, io_out, close_out, thr_out, cum_out, cumt_out, dtt_out = per_batch[i]
        token_copies[i].wait()
        z = mm_t(tws[...], tok[...]) + offset
        dt = jnp.maximum(z, 0.0) + jnp.log1p(jnp.exp(-jnp.abs(z)))
        if i == 0:
            copies[3].wait()
        io_out[...] = mm(tok[...], sw[...]).astype(BF16)
        log_decay = dt * scale
        base = jnp.zeros((SLOT, 1), F32)
        table = blank
        for q, span in enumerate(pieces(rows)):
            part = log_decay[:, span]
            hi = part.astype(BF16)
            rest = part - hi.astype(F32)
            mid = rest.astype(BF16)
            low = (rest - mid.astype(F32)).astype(BF16)
            cum = mm(hi, tri) + (mm(mid, tri) + mm(low, tri))
            last = cum[:, CHUNK - 1 :]
            cumt_out[q] = cum
            dtt_out[q] = dt[:, span]
            both = turned(cum, jnp.exp2(last - cum) * dt[:, span])
            cum_out[span, :] = both
            close_out[span, :] = both.astype(BF16)
            table = jnp.where(lane == q, last, table)
            table = jnp.where(lane == 8 + q, base, table)
            base = base + last
        table = jnp.where(lane == rows // CHUNK, base, table)
        thr_out[...] = turned(blank, jnp.exp2(table))[:16].astype(BF16)
    copies[4].wait()


def values_kernel(owners, axis, index, batch, *refs):
    tok, io, close, thr, halo, w, sw, vkern, voff, skern, soff, sel = refs[:12]
    loads = index == batch - 1
    sem = refs[-6]
    bt, mbuf, hold, vb0, vb1 = refs[-5:]
    ends = refs[-6 - owners : -6]
    if loads:
        gate_in, gw = refs[12], refs[-7 - owners]
        copy = pltpu.make_async_copy(gate_in, gw, sem)
        copy.start()
    first = -6 - owners - loads - 4
    vc_out, mid_out, b_out, c_out = refs[first : first + 4]
    rows = tok.shape[0]
    inner = w.shape[1]
    n = sw.shape[1] // 2
    share = n // owners
    spot = lax.rem(lax.axis_index(axis), owners)
    tiles = pieces(inner, TILE)
    rim = halo[index]
    offset = row(voff)

    def project(j, buf):
        x = jnp.concatenate([rim, tok[...]], axis=0)
        buf[...] = mm(x, w[:, tiles[j]])

    def maps():
        mbuf[pl.ds(0, PAD), :] = mm(rim, sw[...]).astype(BF16).astype(F32)
        mbuf[pl.ds(PAD, rows), :] = io[...].astype(F32)
        y = conv_of(mbuf[...], skern[...], row(soff)).astype(BF16)
        b_out[...] = y[:, :n]
        c_out[...] = y[:, n:]
        bt[...] = y[:, :n].astype(F32).T.astype(BF16)

    def finish(j, buf):
        at = tiles[j]
        vc = conv_of(buf[...], vkern[:, at], offset[:, at])
        vc_out[:, at] = vc.astype(BF16)
        select = sel[:, at]
        through = mm(thr[...], select)
        state = None
        for q, span in enumerate(pieces(rows)):
            scaled = (vc[span] * mm(close[span, :], select)).astype(BF16)
            made = mm(bt[:, span], scaled)
            if q == 0:
                state = made
            else:
                mid_out[q - 1, :, at] = state.astype(BF16)
                state = state * through[q : q + 1] + made
        hold[...] = state
        for k in range(owners):
            owner = jnp.bitwise_xor(spot, k)
            part = hold[pl.ds(pl.multiple_of(owner * share, share), share), :]
            ends[k][:, index * inner + at.start : index * inner + at.stop] = part.astype(BF16)

    line = lax.broadcasted_iota(jnp.int32, (share, LANES), 0)
    count = rows // CHUNK
    mine = jnp.broadcast_to(thr[...].astype(F32)[count : count + 1], (share, LANES))
    decays = jnp.where(line == 0, mine, 0.0).astype(BF16)
    tail = batch * inner + index * LANES
    for k in range(owners):
        ends[k][:, tail : tail + LANES] = decays
    bufs = (vb0, vb1)
    for j in range(len(tiles)):
        project(j, bufs[j % 2])
        if j == 0:
            maps()
        else:
            finish(j - 1, bufs[(j - 1) % 2])
    finish(len(tiles) - 1, bufs[(len(tiles) - 1) % 2])
    if loads:
        copy.wait()


def inside_kernel(
    head_width, owners, axis, runs, tok, gw, b_rows, c_rows, vc, mid, dtt, cum, cumt, thr, sel, skip,
    *refs,
):
    part_out, grow_out, scores, gb0, gb1 = refs[-5:]
    rows, inner = vc.shape
    tiles = pieces(inner, TILE)
    spans = pieces(rows)
    r = lax.broadcasted_iota(jnp.int32, (CHUNK, CHUNK), 0)
    s = lax.broadcasted_iota(jnp.int32, (CHUNK, CHUNK), 1)
    wide = 2 * head_width
    assert wide == CHUNK
    lane = lax.broadcasted_iota(jnp.int32, (CHUNK, wide), 1)
    flat = lane[:1]

    def project(j, buf):
        buf[...] = mm(tok[...], gw[:, tiles[j]]).astype(BF16)

    def score():
        for q, span in enumerate(spans):
            scores[q] = jnp.where(r >= s, mm_t(c_rows[span, :], b_rows[span, :]), 0.0)

    def finish(j, buf):
        tile = tiles[j]
        base = mm(thr[...], sel[:, tile])
        for q, span in enumerate(spans):
            swish = silu(buf[span, :].astype(F32))
            if q > 0:
                carried = mm(c_rows[span, :], mid[q - 1, :, tile])
            for cut in pieces(TILE, wide):
                at = slice(tile.start + cut.start, tile.start + cut.stop)
                first = at.start // head_width
                block = vc[span, at]
                mixes, halves, columns = [], [], []
                for k in range(2):
                    head = first + k
                    column = jnp.broadcast_to(cum[span, head : head + 1], (CHUNK, CHUNK))
                    columns.append(column)
                    gap = jnp.minimum(column - cumt[q, head : head + 1, :], 0.0)
                    mixes.append(
                        (scores[q] * jnp.exp2(gap) * dtt[q, head : head + 1, :]).astype(BF16)
                    )
                    halves.append(
                        jnp.where((lane >= head_width) == (k == 1), block, jnp.zeros_like(block))
                    )
                mixture = mm(jnp.concatenate(mixes, axis=1), jnp.concatenate(halves, axis=0))
                gain = jnp.where(flat < head_width, skip[first], skip[first + 1])
                mixture = mixture + gain * block.astype(F32)
                rise = jnp.exp2(jnp.where(lane < head_width, columns[0], columns[1]))
                gated = swish[:, cut] * rise
                if q > 0:
                    mixture = mixture + carried[:, cut] * rise
                    gated = gated * base[8 + q : 9 + q, cut]
                grow_out[span, at] = gated.astype(BF16)
                part_out[span, at] = mixture * swish[:, cut]

    bufs = (gb0, gb1)

    def run(first, last):
        for j in range(first, last):
            project(j, bufs[j % 2])
            if j == first:
                score()
            else:
                finish(j - 1, bufs[(j - 1) % 2])
        finish(last - 1, bufs[(last - 1) % 2])

    for first, last, side in runs:
        if side is None:
            run(first, last)
        else:
            half = lax.axis_index(axis) // owners
            pl.when(half == side)(functools.partial(run, first, last))


def total_kernel(owners, axis, index, batch, *refs):
    came, sel = refs[:owners], refs[owners]
    total_out, decay_out, held, lines = refs[-4:]
    inner = sel.shape[1]
    at = slice(index * inner, (index + 1) * inner)
    tail = slice(batch * inner + index * LANES, batch * inner + (index + 1) * LANES)
    spot = lax.rem(lax.axis_index(axis), owners)
    lines[...] = jnp.zeros_like(lines)
    for k in range(owners):
        owner = jnp.bitwise_xor(spot, k)
        held[owner] = came[k][:, at]
        lines[pl.ds(owner, 1), :] = came[k][:, tail].astype(F32)[:1]
    decay_out[...] = mm(lines[...].astype(BF16), sel[...])
    state = held[0].astype(F32)
    for k in range(1, owners):
        state = state * decay_out[pl.ds(k, 1), :] + held[k].astype(F32)
    total_out[...] = state.astype(BF16)


def prefix_kernel(owners, axis, index, *refs):
    came = refs[:owners]
    decay, first = refs[owners : owners + 2]
    outs = refs[-owners - 2 : -2]
    held, made = refs[-2:]
    inner = decay.shape[1]
    at = slice(index * inner, (index + 1) * inner)
    spot = lax.rem(lax.axis_index(axis), owners)
    for k in range(owners):
        held[jnp.bitwise_xor(spot, k)] = came[k][:, at]
    state = first[...].astype(F32)
    for k in range(owners):
        made[k] = state.astype(BF16)
        if k + 1 < owners:
            state = state * decay[pl.ds(k, 1), :] + held[k].astype(F32)
    for k in range(owners):
        outs[k][...] = made[jnp.bitwise_xor(spot, k)]


def enter_kernel(owners, axis, index, part, grow, c_rows, *refs):
    came = refs[:owners]
    out, sq_out, state = refs[-3:]
    rows, inner = part.shape
    share = came[0].shape[0]
    spot = lax.rem(lax.axis_index(axis), owners)
    if index:
        sq_out[:, : index * rows] = refs[owners][...]
    for k in range(owners):
        at = pl.multiple_of(jnp.bitwise_xor(spot, k) * share, share)
        state[pl.ds(at, share), :] = came[k][...]
    for span in pieces(rows):
        acc = jnp.zeros((CHUNK, LANES), F32)
        for at in pieces(inner, TILE):
            extra = mm(c_rows[span, :], state[:, at])
            total = part[span, at] + grow[span, at].astype(F32) * extra
            out[span, at] = total
            for cut in pieces(TILE, LANES):
                acc = acc + total[:, cut] * total[:, cut]
        at = slice(index * rows + span.start, index * rows + span.stop)
        sq_out[:, at] = jnp.sum(acc.T, axis=0, keepdims=True)


def norm_kernel(inner_all, count, *refs):
    squares, xs = refs[:count], refs[count:-2]
    gain, out = refs[-2:]
    rows = out.shape[1]
    i, q = pl.program_id(0), pl.program_id(1)
    span = pl.ds(pl.multiple_of(q * rows, rows), rows)
    at = pl.ds(pl.multiple_of((i * pl.num_programs(1) + q) * rows, rows), rows)
    total = squares[0][:, at]
    for ref in squares[1:]:
        total = total + ref[:, at]
    inverse = lax.rsqrt(total / inner_all + EPS)
    columns = jnp.broadcast_to(inverse, (LANES, rows)).T
    gains = row(gain)
    for k, x in enumerate(xs):

        @pl.when(i == k)
        def _():
            for cut in pieces(out.shape[2], LANES):
                out[0, :, cut] = (x[span, cut] * columns * gains[:, cut]).astype(BF16)


def local(
    tokens,
    gate_weight,
    value_weight,
    state_weight,
    step_weight,
    value_kernel,
    value_offset,
    state_kernel,
    state_offset,
    step_offset,
    decay_rate,
    skip_gain,
    norm_gain,
):
    b, t, d = tokens.shape
    inner = gate_weight.shape[1]
    h = step_weight.shape[1]
    n = state_weight.shape[1] // 2
    head_width = inner // h
    peers = lax.axis_size("seq")
    ranks = lax.axis_size("head")
    owners = peers // 2
    share = n // owners
    chunks = t // CHUNK
    assert h <= SLOT and owners * 2 == peers and owners & (owners - 1) == 0
    assert b == 2 and chunks < 8 and value_kernel.shape[0] == 4
    lines = max(owners, 8)

    def swap(arrays):
        return [arrays[0]] + [
            here(lax.ppermute(arrays[k], "seq", [(s, s ^ k) for s in range(peers)]))
            for k in range(1, owners)
        ]

    halo = here(
        lax.ppermute(tokens[:, t - PAD :], "seq", [(s, s + 1) for s in range(peers - 1)])
    )
    outs = pl.pallas_call(
        functools.partial(front_kernel, head_width),
        in_specs=[FAR] * 6,
        out_specs=[WHOLE] * (3 + 7 * b),
        out_shape=[
            pltpu.VMEM(state_weight.shape, BF16),
            pltpu.VMEM(value_weight.shape, BF16),
            pltpu.VMEM((LANES, inner), BF16),
        ]
        + [
            pltpu.VMEM((t, d), BF16),
            pltpu.VMEM((t, 2 * n), BF16),
            pltpu.VMEM((t, LANES), BF16),
            pltpu.VMEM((16, LANES), BF16),
            pltpu.VMEM((t, LANES), F32),
            pltpu.VMEM((chunks, SLOT, CHUNK), F32),
            pltpu.VMEM((chunks, SLOT, CHUNK), F32),
        ]
        * b,
        scratch_shapes=[
            pltpu.VMEM((h, d), BF16),
            pltpu.VMEM((h,), F32),
            pltpu.VMEM((h,), F32),
            pltpu.VMEM((SLOT, d), BF16),
            pltpu.VMEM((LANES, LANES), F32),
            pltpu.SemaphoreType.DMA((b + 5,)),
        ],
        compiler_params=params(16),
        name="front",
        cost_estimate=cost(2 * b * t * d * (2 * n + LANES)),
    )(*map(far, (tokens, state_weight, step_weight.T, value_weight, step_offset, decay_rate)))
    sw, w, sel = outs[:3]
    fronts = [outs[3 + 7 * i : 10 + 7 * i] for i in range(b)]

    wide = b * (inner + LANES)

    def values(i, ends):
        tok, io, close, thr, _, _, _ = fronts[i]
        loads = i == b - 1
        inputs = 12 + loads
        return pl.pallas_call(
            functools.partial(values_kernel, owners, "seq", i, b),
            in_specs=[WHOLE] * 12 + [FAR] * loads + [WHOLE] * len(ends),
            out_specs=[WHOLE] * (4 + loads + owners),
            out_shape=[
                pltpu.VMEM((t, inner), BF16),
                pltpu.VMEM((chunks - 1, n, inner), BF16),
                pltpu.VMEM((t, n), BF16),
                pltpu.VMEM((t, n), BF16),
            ]
            + [pltpu.VMEM(gate_weight.shape, BF16)] * loads
            + [pltpu.VMEM((share, wide), BF16)] * owners,
            scratch_shapes=[
                pltpu.SemaphoreType.DMA,
                pltpu.VMEM((n, t), BF16),
                pltpu.VMEM((t + PAD, 2 * n), F32),
                pltpu.VMEM((n, TILE), F32),
                pltpu.VMEM((t + PAD, TILE), F32),
                pltpu.VMEM((t + PAD, TILE), F32),
            ],
            input_output_aliases={inputs + k: 4 + loads + k for k in range(len(ends))},
            compiler_params=params(16),
            name=f"values{i}",
            cost_estimate=cost(2 * t * d * inner),
        )(
            tok, io, close, thr, halo, w, sw, value_kernel, value_offset,
            state_kernel, state_offset, sel, *[far(gate_weight)] * loads, *ends,
        )

    made, ends = [], ()
    for i in range(b):
        outs = values(i, ends)
        made.append(outs[:4])
        ends = outs[-owners:]
    gw = outs[4]

    def inside(i, runs, gw, made, prior, after):
        tok, _, _, thr, cum, cumt, dtt = fronts[i]
        vc, mid, b_rows, c_rows = made[:4]
        return pl.pallas_call(
            functools.partial(inside_kernel, head_width, owners, "seq", runs),
            in_specs=[WHOLE] * 11 + [SCALARS] + [WHOLE] * (len(prior) + len(after)),
            out_specs=[WHOLE] * 2,
            out_shape=[pltpu.VMEM((t, inner), F32), pltpu.VMEM((t, inner), BF16)],
            scratch_shapes=[
                pltpu.VMEM((chunks, CHUNK, CHUNK), F32),
                pltpu.VMEM((t, TILE), BF16),
                pltpu.VMEM((t, TILE), BF16),
            ],
            input_output_aliases={12 + k: k for k in range(len(prior))},
            compiler_params=params(16),
            name=f"inside{i}",
            cost_estimate=cost(2.5 * t * d * inner),
        )(
            tok, gw, b_rows, c_rows, vc, mid, dtt, cum, cumt, thr, sel, skip_gain,
            *prior, *after,
        )

    def total(i, came, after):
        return pl.pallas_call(
            functools.partial(total_kernel, owners, "seq", i, b),
            in_specs=[WHOLE] * (owners + 1 + len(after)),
            out_specs=[WHOLE] * 2,
            out_shape=[pltpu.VMEM((share, inner), BF16), pltpu.VMEM((lines, inner), F32)],
            scratch_shapes=[
                pltpu.VMEM((owners, share, inner), BF16),
                pltpu.VMEM((lines, LANES), F32),
            ],
            compiler_params=params(16),
            name=f"total{i}",
        )(*came, sel, *after)

    def prefix(i, came, decay, first, after):
        return pl.pallas_call(
            functools.partial(prefix_kernel, owners, "seq", i),
            in_specs=[WHOLE] * (owners + 2 + len(after)),
            out_specs=[WHOLE] * owners,
            out_shape=[pltpu.VMEM((share, inner), BF16)] * owners,
            scratch_shapes=[
                pltpu.VMEM((owners, share, inner), BF16),
                pltpu.VMEM((owners, share, inner), BF16),
            ],
            compiler_params=params(16),
            name=f"prefix{i}",
        )(*came, decay, first, *after)

    def across(x):
        return here(lax.ppermute(x, "seq", [(s, s + owners) for s in range(owners)]))

    def enter(i, part, grow, c_rows, states, before):
        return pl.pallas_call(
            functools.partial(enter_kernel, owners, "seq", i),
            in_specs=[WHOLE] * (3 + owners + len(before)),
            out_specs=[WHOLE] * 2,
            out_shape=[pltpu.VMEM((t, inner), F32), pltpu.VMEM((1, (i + 1) * t), F32)],
            scratch_shapes=[pltpu.VMEM((n, inner), BF16)],
            compiler_params=params(16),
            name=f"enter{i}",
        )(part, grow, c_rows, *states, *before)

    def norm(xs, squares):
        rows = min(t, 256)
        return pl.pallas_call(
            functools.partial(norm_kernel, inner * ranks, ranks),
            grid=(b, t // rows),
            in_specs=[WHOLE] * (ranks + b + 1),
            out_specs=pl.BlockSpec((1, rows, inner), lambda i, q: (i, q, 0)),
            out_shape=jax.ShapeDtypeStruct((b, t, inner), BF16),
            compiler_params=params(16),
            name="norm",
        )(*squares, *xs, norm_gain)

    came = swap(ends)
    tiles = inner // TILE
    ahead = tiles // 2 + 1
    part0, grow0 = inside(0, ((0, tiles, None),), gw, made[0], (), ())
    early = inside(1, ((0, ahead, 0),), gw, made[1], (), (grow0,))
    whole0, decay0 = total(0, came, (early[1],))
    first0 = across(whole0)
    whole1, decay1 = total(1, came, (whole0,))
    first1 = across(whole1)
    late = ((0, ahead, 1), (ahead, tiles, None))
    part1, grow1 = inside(1, late, gw, made[1], early, (whole1,))
    sent0 = prefix(0, came, decay0, first0, (grow1,))
    back0 = swap(sent0)
    sent1 = prefix(1, came, decay1, first1, (sent0[1],))
    back1 = swap(sent1)
    x0, sq0 = enter(0, part0, grow0, made[0][3], back0, (sent1[1],))
    x1, sq1 = enter(1, part1, grow1, made[1][3], back1, (sq0,))
    squares = [sq1] + [
        here(lax.ppermute(sq1, "head", [(s, (s + k) % ranks) for s in range(ranks)]))
        for k in range(1, ranks)
    ]
    return norm((x0, x1), squares)


def solution(mesh):
    return jax.shard_map(
        local,
        mesh=mesh,
        in_specs=(
            P(None, "seq", None),
            P(None, "head"),
            P(None, "head"),
            P(),
            P(None, "head"),
            P(None, "head"),
            P("head"),
            P(),
            P(),
            P("head"),
            P("head"),
            P("head"),
            P("head"),
        ),
        out_specs=P(None, "seq", "head"),
        check_vma=False,
    )
```

```python
import functools
import jax
import jax.numpy as jnp
from jax import lax
from jax.experimental import pallas as pl
from jax.experimental.pallas import tpu as pltpu
from jax.sharding import PartitionSpec as P

EPS = 1e-05
LOG2E = 1.4426950408889634
PAD = 16
CHUNK = 128
TILE = 256
LANES = 128
SLOT = 32
F32 = jnp.float32
BF16 = jnp.bfloat16
WHOLE = pl.BlockSpec(memory_space=pltpu.VMEM)
FAR = pl.BlockSpec(memory_space=pltpu.HBM)
SCALARS = pl.BlockSpec(memory_space=pltpu.SMEM)


def here(x):
    return pltpu.with_memory_space_constraint(x, pltpu.VMEM)


def far(x):
    return pltpu.with_memory_space_constraint(x, pltpu.HBM)


def params(mib):
    return pltpu.CompilerParams(vmem_limit_bytes=mib << 20)


def cost(flops):
    return pl.CostEstimate(flops=int(flops), transcendentals=0, bytes_accessed=0)


def mm(a, b):
    return jnp.dot(a, b, preferred_element_type=F32)


def mm_t(a, b):
    return lax.dot_general(a, b, (((1,), (1,)), ((), ())), preferred_element_type=F32)


def silu(x):
    half = 0.5 * x
    return half + half * jnp.tanh(half)


def row(ref):
    return ref[...].reshape(1, ref.shape[0])


def pieces(total, size=CHUNK):
    return [slice(k * size, (k + 1) * size) for k in range(total // size)]


def head_select(width, head_width):
    lane = lax.broadcasted_iota(jnp.int32, (LANES, width), 0)
    col = lax.broadcasted_iota(jnp.int32, (LANES, width), 1)
    start = (lane & (SLOT - 1)) * head_width
    hit = (lane >= SLOT) & (lane < 3 * SLOT) & (col >= start) & (col < start + head_width)
    return jnp.where(hit, 1.0, 0.0).astype(BF16)


def conv_of(x, kernel, offset):
    back = pltpu.roll(x, 1, 0)
    near = offset + kernel[3:4] * x + kernel[2:3] * back
    deep = kernel[1:2] * x + kernel[0:1] * back
    return silu((near + pltpu.roll(deep, 2, 0))[PAD:]).astype(BF16)


def front_kernel(head_width, axis, *refs):
    tok_in, sw_in, twt_in, w_in, toff_in, rate_in = refs[:6]
    batch = tok_in.shape[0]
    sw, w, sel = refs[6:9]
    per_batch = [refs[9 + 7 * i : 16 + 7 * i] for i in range(batch)]
    twt, toff, rate, tws, vec, sem = refs[9 + 7 * batch :]
    rows = tok_in.shape[1]
    heads = twt.shape[0]
    half = rows // 2
    token_copies = [
        pltpu.make_async_copy(
            tok_in.at[i, pl.ds(k * half, half)],
            per_batch[i][0].at[pl.ds(k * half, half)],
            sem.at[5 + 2 * i + k],
        )
        for i in range(batch)
        for k in range(2)
    ]
    copies = [
        pltpu.make_async_copy(twt_in, twt, sem.at[0]),
        pltpu.make_async_copy(toff_in, toff, sem.at[1]),
        pltpu.make_async_copy(rate_in, rate, sem.at[2]),
        pltpu.make_async_copy(sw_in, sw, sem.at[3]),
        pltpu.make_async_copy(w_in.at[:, pl.ds(0, w.shape[1])], w, sem.at[4]),
    ]

    @pl.when(lax.axis_index(axis) >= 0)
    def _():
        order = copies[:3] + [token_copies[0], copies[3]] + token_copies[1:] + [copies[4]]
        for copy in order:
            copy.start()

    sel[...] = head_select(sel.shape[1], head_width)
    tws[...] = jnp.zeros_like(tws)
    vec[...] = jnp.zeros_like(vec)
    for copy in copies[:3]:
        copy.wait()
    tws[pl.ds(0, heads), :] = twt[...]
    vec[pl.ds(0, 1), pl.ds(0, heads)] = row(toff)
    vec[pl.ds(1, 1), pl.ds(0, heads)] = row(rate)
    columns = vec[...].T[:SLOT]
    offset = columns[:, 0:1]
    scale = columns[:, 1:2] * (-LOG2E)
    r = lax.broadcasted_iota(jnp.int32, (CHUNK, CHUNK), 0)
    c = lax.broadcasted_iota(jnp.int32, (CHUNK, CHUNK), 1)
    tri = jnp.where(r <= c, 1.0, 0.0).astype(BF16)
    lane = lax.broadcasted_iota(jnp.int32, (SLOT, LANES), 1)
    blank = jnp.zeros((SLOT, LANES), F32)

    def turned(first, x):
        hi = x.astype(BF16).astype(F32)
        return jnp.concatenate([first, hi, x - hi, blank], axis=0).T

    for i in range(batch):
        tok, io_out, close_out, thr_out, cum_out, cumt_out, dtt_out = per_batch[i]
        parts = []
        for k in range(2):
            at = slice(k * half, (k + 1) * half)
            token_copies[2 * i + k].wait()
            parts.append(mm_t(tws[...], tok[at, :]))
            if i + k == 0:
                copies[3].wait()
            io_out[at, :] = mm(tok[at, :], sw[...]).astype(BF16)
        z = jnp.concatenate(parts, axis=1) + offset
        dt = jnp.maximum(z, 0.0) + jnp.log1p(jnp.exp(-jnp.abs(z)))
        log_decay = dt * scale
        base = jnp.zeros((SLOT, 1), F32)
        table = blank
        for q, span in enumerate(pieces(rows)):
            part = log_decay[:, span]
            hi = part.astype(BF16)
            rest = part - hi.astype(F32)
            mid = rest.astype(BF16)
            low = (rest - mid.astype(F32)).astype(BF16)
            cum = mm(hi, tri) + (mm(mid, tri) + mm(low, tri))
            last = cum[:, CHUNK - 1 :]
            cumt_out[q] = cum
            dtt_out[q] = dt[:, span]
            both = turned(cum, jnp.exp2(last - cum) * dt[:, span])
            cum_out[span, :] = both
            close_out[span, :] = both.astype(BF16)
            table = jnp.where(lane == q, last, table)
            table = jnp.where(lane == 8 + q, base, table)
            base = base + last
        table = jnp.where(lane == rows // CHUNK, base, table)
        thr_out[...] = turned(blank, jnp.exp2(table))[:16].astype(BF16)
    copies[4].wait()


def values_kernel(owners, axis, index, batch, *refs):
    tok, io, close, thr, halo, wa, sw, vkern, voff, skern, soff, sel, extra = refs[:13]
    sem = refs[-6]
    bt, mbuf, hold, vb0, vb1 = refs[-5:]
    ends = refs[-6 - owners : -6]
    vc_out, mid_out, b_out, c_out, big = refs[-11 - owners : -6 - owners]
    cols = wa.shape[1]
    if index == 0:
        wb = big
        copy = pltpu.make_async_copy(extra.at[:, pl.ds(cols, big.shape[1])], big, sem)
    else:
        wb = extra
        copy = pltpu.make_async_copy(refs[13], big, sem)
    pl.when(lax.axis_index(axis) >= 0)(copy.start)
    rows = tok.shape[0]
    inner = vc_out.shape[1]
    n = sw.shape[1] // 2
    share = n // owners
    spot = lax.rem(lax.axis_index(axis), owners)
    tiles = pieces(inner, TILE)
    rim = halo[index]
    offset = row(voff)

    def project(j, buf):
        x = jnp.concatenate([rim, tok[...]], axis=0)
        at = tiles[j]
        late = at.start >= cols
        weight = wb[:, at.start - cols : at.stop - cols] if late else wa[:, at]
        buf[...] = mm(x, weight).astype(BF16).astype(F32)

    def maps():
        mbuf[pl.ds(0, PAD), :] = mm(rim, sw[...]).astype(BF16).astype(F32)
        mbuf[pl.ds(PAD, rows), :] = io[...].astype(F32)
        y = conv_of(mbuf[...], skern[...], row(soff))
        b_out[...] = y[:, :n]
        c_out[...] = y[:, n:]
        bt[...] = y[:, :n].astype(F32).T.astype(BF16)

    def finish(j, buf):
        at = tiles[j]
        vc = conv_of(buf[...], vkern[:, at], offset[:, at])
        vc_out[:, at] = vc
        select = sel[:, at]
        through = mm(thr[...], select)
        state = None
        for q, span in enumerate(pieces(rows)):
            scaled = (vc[span].astype(F32) * mm(close[span, :], select)).astype(BF16)
            made = mm(bt[:, span], scaled)
            if q == 0:
                state = made
            else:
                mid_out[q - 1, :, at] = state.astype(BF16)
                state = state * through[q : q + 1] + made
        hold[...] = state
        for k in range(owners):
            owner = jnp.bitwise_xor(spot, k)
            part = hold[pl.ds(pl.multiple_of(owner * share, share), share), :]
            ends[k][:, index * inner + at.start : index * inner + at.stop] = part.astype(BF16)

    line = lax.broadcasted_iota(jnp.int32, (share, LANES), 0)
    count = rows // CHUNK
    mine = jnp.broadcast_to(thr[...].astype(F32)[count : count + 1], (share, LANES))
    decays = jnp.where(line == 0, mine, 0.0).astype(BF16)
    tail = batch * inner + index * LANES
    for k in range(owners):
        ends[k][:, tail : tail + LANES] = decays
    bufs = (vb0, vb1)
    for j in range(len(tiles)):
        if index == 0 and tiles[j].start == cols:
            copy.wait()
        project(j, bufs[j % 2])
        if j == 0:
            maps()
        else:
            finish(j - 1, bufs[(j - 1) % 2])
    finish(len(tiles) - 1, bufs[(len(tiles) - 1) % 2])
    if index > 0:
        copy.wait()


def inside_kernel(
    head_width, owners, axis, runs, tok, gw, b_rows, c_rows, vc, mid, dtt, cum, cumt, thr, sel, skip,
    *refs,
):
    part_out, grow_out, scores, gb0, gb1 = refs[-5:]
    rows, inner = vc.shape
    tiles = pieces(inner, TILE)
    spans = pieces(rows)
    r = lax.broadcasted_iota(jnp.int32, (CHUNK, CHUNK), 0)
    s = lax.broadcasted_iota(jnp.int32, (CHUNK, CHUNK), 1)
    wide = 2 * head_width
    assert wide == CHUNK
    lane = lax.broadcasted_iota(jnp.int32, (CHUNK, wide), 1)
    flat = lane[:1]

    def project(j, buf):
        buf[...] = mm(tok[...], gw[:, tiles[j]]).astype(BF16)

    def score():
        for q, span in enumerate(spans):
            scores[q] = jnp.where(r >= s, mm_t(c_rows[span, :], b_rows[span, :]), 0.0)

    def finish(j, buf):
        tile = tiles[j]
        base = mm(thr[...], sel[:, tile])
        for q, span in enumerate(spans):
            swish = silu(buf[span, :].astype(F32))
            if q > 0:
                carried = mm(c_rows[span, :], mid[q - 1, :, tile])
            for cut in pieces(TILE, wide):
                at = slice(tile.start + cut.start, tile.start + cut.stop)
                first = at.start // head_width
                block = vc[span, at]
                mixes, halves, columns = [], [], []
                for k in range(2):
                    head = first + k
                    column = jnp.broadcast_to(cum[span, head : head + 1], (CHUNK, CHUNK))
                    columns.append(column)
                    gap = jnp.minimum(column - cumt[q, head : head + 1, :], 0.0)
                    mixes.append(
                        (scores[q] * jnp.exp2(gap) * dtt[q, head : head + 1, :]).astype(BF16)
                    )
                    halves.append(
                        jnp.where((lane >= head_width) == (k == 1), block, jnp.zeros_like(block))
                    )
                mixture = mm(jnp.concatenate(mixes, axis=1), jnp.concatenate(halves, axis=0))
                gain = jnp.where(flat < head_width, skip[first], skip[first + 1])
                mixture = mixture + gain * block.astype(F32)
                rise = jnp.exp2(jnp.where(lane < head_width, columns[0], columns[1]))
                gated = swish[:, cut] * rise
                if q > 0:
                    mixture = mixture + carried[:, cut] * rise
                    gated = gated * base[8 + q : 9 + q, cut]
                grow_out[span, at] = gated.astype(BF16)
                part_out[span, at] = mixture * swish[:, cut]

    bufs = (gb0, gb1)

    def run(first, last):
        for j in range(first, last):
            project(j, bufs[j % 2])
            if j == first:
                score()
            else:
                finish(j - 1, bufs[(j - 1) % 2])
        finish(last - 1, bufs[(last - 1) % 2])

    for first, last, side in runs:
        if side is None:
            run(first, last)
        else:
            half = lax.axis_index(axis) // owners
            pl.when(half == side)(functools.partial(run, first, last))


def total_kernel(owners, axis, index, batch, *refs):
    came, sel = refs[:owners], refs[owners]
    total_out, decay_out, held, lines = refs[-4:]
    inner = sel.shape[1]
    at = slice(index * inner, (index + 1) * inner)
    tail = slice(batch * inner + index * LANES, batch * inner + (index + 1) * LANES)
    spot = lax.rem(lax.axis_index(axis), owners)
    lines[...] = jnp.zeros_like(lines)
    for k in range(owners):
        owner = jnp.bitwise_xor(spot, k)
        held[owner] = came[k][:, at]
        lines[pl.ds(owner, 1), :] = came[k][:, tail].astype(F32)[:1]
    decay_out[...] = mm(lines[...].astype(BF16), sel[...])
    state = held[0].astype(F32)
    for k in range(1, owners):
        state = state * decay_out[pl.ds(k, 1), :] + held[k].astype(F32)
    total_out[...] = state.astype(BF16)


def prefix_kernel(owners, axis, index, *refs):
    came = refs[:owners]
    decay, first = refs[owners : owners + 2]
    outs = refs[-owners - 2 : -2]
    held, made = refs[-2:]
    inner = decay.shape[1]
    at = slice(index * inner, (index + 1) * inner)
    spot = lax.rem(lax.axis_index(axis), owners)
    for k in range(owners):
        held[jnp.bitwise_xor(spot, k)] = came[k][:, at]
    state = first[...].astype(F32)
    for k in range(owners):
        made[k] = state.astype(BF16)
        if k + 1 < owners:
            state = state * decay[pl.ds(k, 1), :] + held[k].astype(F32)
    for k in range(owners):
        outs[k][...] = made[jnp.bitwise_xor(spot, k)]


def enter_kernel(owners, axis, part, grow, c_rows, *refs):
    came = refs[:owners]
    out, sq_out, state = refs[-3:]
    rows, inner = part.shape
    share = came[0].shape[0]
    spot = lax.rem(lax.axis_index(axis), owners)
    for k in range(owners):
        at = pl.multiple_of(jnp.bitwise_xor(spot, k) * share, share)
        state[pl.ds(at, share), :] = came[k][...]
    for span in pieces(rows):
        acc = jnp.zeros((CHUNK, LANES), F32)
        for at in pieces(inner, TILE):
            extra = mm(c_rows[span, :], state[:, at])
            total = part[span, at] + grow[span, at].astype(F32) * extra
            out[span, at] = total
            for cut in pieces(TILE, LANES):
                acc = acc + total[:, cut] * total[:, cut]
        sq_out[:, span] = jnp.sum(acc.T, axis=0, keepdims=True)


def norm_kernel(inner_all, count, *refs):
    squares = refs[:count]
    x, gain = refs[count : count + 2]
    out = refs[-1]
    rows = out.shape[1]
    span = pl.ds(pl.multiple_of(pl.program_id(0) * rows, rows), rows)
    total = squares[0][:, span]
    for ref in squares[1:]:
        total = total + ref[:, span]
    inverse = lax.rsqrt(total / inner_all + EPS)
    columns = jnp.broadcast_to(inverse, (LANES, rows)).T
    gains = row(gain)
    for cut in pieces(out.shape[2], LANES):
        out[0, :, cut] = (x[span, cut] * columns * gains[:, cut]).astype(BF16)


def local(
    tokens,
    gate_weight,
    value_weight,
    state_weight,
    step_weight,
    value_kernel,
    value_offset,
    state_kernel,
    state_offset,
    step_offset,
    decay_rate,
    skip_gain,
    norm_gain,
):
    b, t, d = tokens.shape
    inner = gate_weight.shape[1]
    h = step_weight.shape[1]
    n = state_weight.shape[1] // 2
    head_width = inner // h
    peers = lax.axis_size("seq")
    ranks = lax.axis_size("head")
    owners = peers // 2
    share = n // owners
    chunks = t // CHUNK
    assert h <= SLOT and owners * 2 == peers and owners & (owners - 1) == 0
    assert b == 2 and chunks < 8 and value_kernel.shape[0] == 4
    lines = max(owners, 8)
    early_cols = (inner // TILE + 1) // 2 * TILE

    def swap(arrays):
        return [arrays[0]] + [
            here(lax.ppermute(arrays[k], "seq", [(s, s ^ k) for s in range(peers)]))
            for k in range(1, owners)
        ]

    halo = here(
        lax.ppermute(tokens[:, t - PAD :], "seq", [(s, s + 1) for s in range(peers - 1)])
    )
    outs = pl.pallas_call(
        functools.partial(front_kernel, head_width, "seq"),
        in_specs=[FAR] * 6,
        out_specs=[WHOLE] * (3 + 7 * b),
        out_shape=[
            pltpu.VMEM(state_weight.shape, BF16),
            pltpu.VMEM((d, early_cols), BF16),
            pltpu.VMEM((LANES, inner), BF16),
        ]
        + [
            pltpu.VMEM((t, d), BF16),
            pltpu.VMEM((t, 2 * n), BF16),
            pltpu.VMEM((t, LANES), BF16),
            pltpu.VMEM((16, LANES), BF16),
            pltpu.VMEM((t, LANES), F32),
            pltpu.VMEM((chunks, SLOT, CHUNK), F32),
            pltpu.VMEM((chunks, SLOT, CHUNK), F32),
        ]
        * b,
        scratch_shapes=[
            pltpu.VMEM((h, d), BF16),
            pltpu.VMEM((h,), F32),
            pltpu.VMEM((h,), F32),
            pltpu.VMEM((SLOT, d), BF16),
            pltpu.VMEM((LANES, LANES), F32),
            pltpu.SemaphoreType.DMA((2 * b + 5,)),
        ],
        compiler_params=params(16),
        name="front",
        cost_estimate=cost(2 * b * t * d * (2 * n + LANES)),
    )(*map(far, (tokens, state_weight, step_weight.T, value_weight, step_offset, decay_rate)))
    sw, w, sel = outs[:3]
    fronts = [outs[3 + 7 * i : 10 + 7 * i] for i in range(b)]

    wide = b * (inner + LANES)

    def values(i, rest, ends):
        tok, io, close, thr, _, _, _ = fronts[i]
        big = gate_weight.shape if i else (d, inner - early_cols)
        extra = (rest, far(gate_weight)) if i else (far(value_weight),)
        return pl.pallas_call(
            functools.partial(values_kernel, owners, "seq", i, b),
            in_specs=[WHOLE] * 12 + ([WHOLE, FAR] if i else [FAR]) + [WHOLE] * len(ends),
            out_specs=[WHOLE] * (5 + owners),
            out_shape=[
                pltpu.VMEM((t, inner), BF16),
                pltpu.VMEM((chunks - 1, n, inner), BF16),
                pltpu.VMEM((t, n), BF16),
                pltpu.VMEM((t, n), BF16),
                pltpu.VMEM(big, BF16),
            ]
            + [pltpu.VMEM((share, wide), BF16)] * owners,
            scratch_shapes=[
                pltpu.SemaphoreType.DMA,
                pltpu.VMEM((n, t), BF16),
                pltpu.VMEM((t + PAD, 2 * n), F32),
                pltpu.VMEM((n, TILE), F32),
                pltpu.VMEM((t + PAD, TILE), F32),
                pltpu.VMEM((t + PAD, TILE), F32),
            ],
            input_output_aliases={12 + len(extra) + k: 5 + k for k in range(len(ends))},
            compiler_params=params(16),
            name=f"values{i}",
            cost_estimate=cost(2 * t * d * inner),
        )(
            tok, io, close, thr, halo, w, sw, value_kernel, value_offset,
            state_kernel, state_offset, sel, *extra, *ends,
        )

    made, ends, big = [], (), None
    for i in range(b):
        outs = values(i, big, ends)
        made.append(outs[:4])
        big, ends = outs[4], outs[5:]
    gw = big

    def inside(i, runs, gw, made, prior, after):
        tok, _, _, thr, cum, cumt, dtt = fronts[i]
        vc, mid, b_rows, c_rows = made[:4]
        return pl.pallas_call(
            functools.partial(inside_kernel, head_width, owners, "seq", runs),
            in_specs=[WHOLE] * 11 + [SCALARS] + [WHOLE] * (len(prior) + len(after)),
            out_specs=[WHOLE] * 2,
            out_shape=[pltpu.VMEM((t, inner), F32), pltpu.VMEM((t, inner), BF16)],
            scratch_shapes=[
                pltpu.VMEM((chunks, CHUNK, CHUNK), F32),
                pltpu.VMEM((t, TILE), BF16),
                pltpu.VMEM((t, TILE), BF16),
            ],
            input_output_aliases={12 + k: k for k in range(len(prior))},
            compiler_params=params(16),
            name=f"inside{i}",
            cost_estimate=cost(2.5 * t * d * inner),
        )(
            tok, gw, b_rows, c_rows, vc, mid, dtt, cum, cumt, thr, sel, skip_gain,
            *prior, *after,
        )

    def total(i, came, after):
        return pl.pallas_call(
            functools.partial(total_kernel, owners, "seq", i, b),
            in_specs=[WHOLE] * (owners + 1 + len(after)),
            out_specs=[WHOLE] * 2,
            out_shape=[pltpu.VMEM((share, inner), BF16), pltpu.VMEM((lines, inner), F32)],
            scratch_shapes=[
                pltpu.VMEM((owners, share, inner), BF16),
                pltpu.VMEM((lines, LANES), F32),
            ],
            compiler_params=params(16),
            name=f"total{i}",
        )(*came, sel, *after)

    def prefix(i, came, decay, first, after):
        return pl.pallas_call(
            functools.partial(prefix_kernel, owners, "seq", i),
            in_specs=[WHOLE] * (owners + 2 + len(after)),
            out_specs=[WHOLE] * owners,
            out_shape=[pltpu.VMEM((share, inner), BF16)] * owners,
            scratch_shapes=[
                pltpu.VMEM((owners, share, inner), BF16),
                pltpu.VMEM((owners, share, inner), BF16),
            ],
            compiler_params=params(16),
            name=f"prefix{i}",
        )(*came, decay, first, *after)

    def across(x):
        return here(lax.ppermute(x, "seq", [(s, s + owners) for s in range(owners)]))

    def enter(i, part, grow, c_rows, states, after):
        x, sq = pl.pallas_call(
            functools.partial(enter_kernel, owners, "seq"),
            in_specs=[WHOLE] * (3 + owners + len(after)),
            out_specs=[WHOLE] * 2,
            out_shape=[pltpu.VMEM((t, inner), F32), pltpu.VMEM((1, t), F32)],
            scratch_shapes=[pltpu.VMEM((n, inner), BF16)],
            compiler_params=params(16),
            name=f"enter{i}",
        )(part, grow, c_rows, *states, *after)
        return x, [sq] + [
            here(lax.ppermute(sq, "head", [(s, (s + k) % ranks) for s in range(ranks)]))
            for k in range(1, ranks)
        ]

    def norm(i, x, squares, into):
        rows = min(t, 256)
        return pl.pallas_call(
            functools.partial(norm_kernel, inner * ranks, ranks),
            grid=(t // rows,),
            in_specs=[WHOLE] * (ranks + 2) + [FAR] * len(into),
            out_specs=pl.BlockSpec((1, rows, inner), lambda q: (i, q, 0)),
            out_shape=jax.ShapeDtypeStruct((b, t, inner), BF16),
            input_output_aliases={ranks + 2: 0} if into else {},
            compiler_params=params(16),
            name=f"norm{i}",
        )(*squares, x, norm_gain, *into)

    came = swap(ends)
    tiles = inner // TILE
    ahead = tiles // 2 + 1
    part0, grow0 = inside(0, ((0, tiles, None),), gw, made[0], (), ())
    early = inside(1, ((0, ahead, 0),), gw, made[1], (), (grow0,))
    whole0, decay0 = total(0, came, (early[1],))
    first0 = across(whole0)
    whole1, decay1 = total(1, came, (whole0,))
    first1 = across(whole1)
    late = ((0, ahead, 1), (ahead, tiles, None))
    part1, grow1 = inside(1, late, gw, made[1], early, (whole1,))
    sent0 = prefix(0, came, decay0, first0, (grow1,))
    back0 = swap(sent0)
    sent1 = prefix(1, came, decay1, first1, (sent0[1],))
    back1 = swap(sent1)
    x0, squares0 = enter(0, part0, grow0, made[0][3], back0, (sent1[1],))
    x1, squares1 = enter(1, part1, grow1, made[1][3], back1, (squares0[0],))
    out = norm(0, x0, squares0, ())
    return norm(1, x1, squares1, (out,))


def solution(mesh):
    return jax.shard_map(
        local,
        mesh=mesh,
        in_specs=(
            P(None, "seq", None),
            P(None, "head"),
            P(None, "head"),
            P(),
            P(None, "head"),
            P(None, "head"),
            P("head"),
            P(),
            P(),
            P("head"),
            P("head"),
            P("head"),
            P("head"),
        ),
        out_specs=P(None, "seq", "head"),
        check_vma=False,
    )
```

```python
import functools
import jax
import jax.numpy as jnp
from jax import lax
from jax.experimental import pallas as pl
from jax.experimental.pallas import tpu as pltpu
from jax.sharding import PartitionSpec as P

EPS = 1e-05
LOG2E = 1.4426950408889634
PAD = 16
CHUNK = 128
TILE = 256
LANES = 128
SLOT = 32
F32 = jnp.float32
BF16 = jnp.bfloat16
WHOLE = pl.BlockSpec(memory_space=pltpu.VMEM)
FAR = pl.BlockSpec(memory_space=pltpu.HBM)
SCALARS = pl.BlockSpec(memory_space=pltpu.SMEM)


def here(x):
    return pltpu.with_memory_space_constraint(x, pltpu.VMEM)


def far(x):
    return pltpu.with_memory_space_constraint(x, pltpu.HBM)


def params(mib):
    return pltpu.CompilerParams(vmem_limit_bytes=mib << 20)


def cost(flops):
    return pl.CostEstimate(flops=int(flops), transcendentals=0, bytes_accessed=0)


def mm(a, b):
    return jnp.dot(a, b, preferred_element_type=F32)


def mm_t(a, b):
    return lax.dot_general(a, b, (((1,), (1,)), ((), ())), preferred_element_type=F32)


def silu(x):
    half = 0.5 * x
    return half + half * jnp.tanh(half)


def row(ref):
    return ref[...].reshape(1, ref.shape[0])


def pieces(total, size=CHUNK):
    return [slice(k * size, (k + 1) * size) for k in range(total // size)]


def head_select(width, head_width, group):
    lane = lax.broadcasted_iota(jnp.int32, (LANES, width), 0) - 2 * SLOT * group
    col = lax.broadcasted_iota(jnp.int32, (LANES, width), 1)
    start = (lane & (SLOT - 1)) * head_width
    hit = (lane >= 0) & (lane < 2 * SLOT) & (col >= start) & (col < start + head_width)
    return jnp.where(hit, 1.0, 0.0).astype(BF16)


def conv_of(x, kernel, offset):
    back = pltpu.roll(x, 1, 0)
    near = offset + kernel[3:4] * x + kernel[2:3] * back
    deep = kernel[1:2] * x + kernel[0:1] * back
    return silu((near + pltpu.roll(deep, 2, 0))[PAD:]).astype(BF16)


def front_kernel(head_width, *refs):
    tok_in, sw_in, twt_in, w_in, toff_in, rate_in = refs[:6]
    batch = tok_in.shape[0]
    sw, w, sel = refs[6:9]
    per_batch = [refs[9 + 7 * i : 16 + 7 * i] for i in range(batch)]
    twt, toff, rate, tws, vec, sem = refs[9 + 7 * batch :]
    rows = tok_in.shape[1]
    heads = twt.shape[0]
    token_copies = [
        pltpu.make_async_copy(tok_in.at[i], per_batch[i][0], sem.at[i]) for i in range(batch)
    ]
    copies = [
        pltpu.make_async_copy(twt_in, twt, sem.at[batch]),
        pltpu.make_async_copy(toff_in, toff, sem.at[batch + 1]),
        pltpu.make_async_copy(rate_in, rate, sem.at[batch + 2]),
        pltpu.make_async_copy(sw_in, sw, sem.at[batch + 3]),
        pltpu.make_async_copy(w_in, w, sem.at[batch + 4]),
    ]
    for copy in copies[:3] + [token_copies[0], copies[3]] + token_copies[1:] + [copies[4]]:
        copy.start()
    sel[...] = head_select(sel.shape[1], head_width, 0)
    for copy in copies[:3]:
        copy.wait()
    tws[...] = jnp.zeros_like(tws)
    vec[...] = jnp.zeros_like(vec)
    for g in range(LANES // SLOT):
        tws[pl.ds(g * SLOT, heads), :] = twt[...]
        vec[pl.ds(0, 1), pl.ds(g * SLOT, heads)] = row(toff)
        vec[pl.ds(1, 1), pl.ds(g * SLOT, heads)] = row(rate)
    offset = vec[pl.ds(0, 1), :]
    scale = vec[pl.ds(1, 1), :] * (-LOG2E)
    r = lax.broadcasted_iota(jnp.int32, (CHUNK, CHUNK), 0)
    c = lax.broadcasted_iota(jnp.int32, (CHUNK, CHUNK), 1)
    tri = jnp.where(r >= c, 1.0, 0.0).astype(BF16)
    group = lax.broadcasted_iota(jnp.int32, (1, LANES), 1) // SLOT
    low_lane = (group & 1) == 1

    def parts(x):
        hi = x.astype(BF16).astype(F32)
        return jnp.where(low_lane, x - hi, hi).astype(BF16)

    for i in range(batch):
        tok, io_out, close_out, thr_out, cum_out, cumt_out, dtt_out = per_batch[i]
        token_copies[i].wait()
        if i == 0:
            copies[3].wait()
        x = tok[...]
        io_out[...] = mm(x, sw[...]).astype(BF16)
        z = mm_t(x, tws[...]) + offset
        dt = jnp.maximum(z, 0.0) + jnp.log1p(jnp.exp(-jnp.abs(z)))
        log_decay = dt * scale
        base = jnp.zeros((1, LANES), F32)
        lasts, bases = [], []
        for q, span in enumerate(pieces(rows)):
            part = log_decay[span]
            hi = part.astype(BF16)
            rest = part - hi.astype(F32)
            mid = rest.astype(BF16)
            low = (rest - mid.astype(F32)).astype(BF16)
            cum = mm(tri, hi) + (mm(tri, mid) + mm(tri, low))
            last = cum[CHUNK - 1 :]
            cum_out[span, :] = cum
            cumt_out[q] = cum.T[:SLOT]
            dtt_out[q] = dt[span].T[:SLOT]
            close_out[span, :] = parts(jnp.exp2(last - cum) * dt[span])
            lasts.append(last)
            bases.append(base)
            base = base + last
        zero = [jnp.zeros((1, LANES), F32)]
        table = lasts + [base] + zero * (7 - len(lasts)) + bases + zero * (8 - len(bases))
        thr_out[...] = parts(jnp.exp2(jnp.concatenate(table, axis=0)))
    copies[4].wait()


def values_kernel(owners, axis, index, batch, *refs):
    tok, io, close, thr, halo, w, sw, vkern, voff, skern, soff, sel = refs[:12]
    loads = index == batch - 1
    sem = refs[-6]
    bt, mbuf, hold, vb0, vb1 = refs[-5:]
    ends = refs[-6 - owners : -6]
    if loads:
        gate_in, gw = refs[12], refs[-7 - owners]
        copy = pltpu.make_async_copy(gate_in, gw, sem)
        copy.start()
    first = -6 - owners - loads - 4
    vc_out, mid_out, b_out, c_out = refs[first : first + 4]
    rows = tok.shape[0]
    inner = w.shape[1]
    n = sw.shape[1] // 2
    share = n // owners
    spot = lax.rem(lax.axis_index(axis), owners)
    tiles = pieces(inner, TILE)
    rim = halo[index]
    offset = row(voff)

    def project(j, buf):
        x = jnp.concatenate([rim, tok[...]], axis=0)
        buf[...] = mm(x, w[:, tiles[j]]).astype(BF16).astype(F32)

    def maps():
        mbuf[pl.ds(0, PAD), :] = mm(rim, sw[...]).astype(BF16).astype(F32)
        mbuf[pl.ds(PAD, rows), :] = io[...].astype(F32)
        y = conv_of(mbuf[...], skern[...], row(soff))
        b_out[...] = y[:, :n]
        c_out[...] = y[:, n:]
        bt[...] = y[:, :n].astype(F32).T.astype(BF16)

    def finish(j, buf):
        at = tiles[j]
        vc = conv_of(buf[...], vkern[:, at], offset[:, at])
        vc_out[:, at] = vc
        select = sel[:, at]
        through = mm(thr[...], select)
        state = None
        for q, span in enumerate(pieces(rows)):
            scaled = (vc[span].astype(F32) * mm(close[span, :], select)).astype(BF16)
            made = mm(bt[:, span], scaled)
            if q == 0:
                state = made
            else:
                mid_out[q - 1, :, at] = state.astype(BF16)
                state = state * through[q : q + 1] + made
        hold[...] = state
        for k in range(owners):
            owner = jnp.bitwise_xor(spot, k)
            part = hold[pl.ds(pl.multiple_of(owner * share, share), share), :]
            ends[k][:, index * inner + at.start : index * inner + at.stop] = part.astype(BF16)

    line = lax.broadcasted_iota(jnp.int32, (share, LANES), 0)
    count = rows // CHUNK
    mine = jnp.broadcast_to(thr[...].astype(F32)[count : count + 1], (share, LANES))
    decays = jnp.where(line == 0, mine, 0.0).astype(BF16)
    tail = batch * inner + index * LANES
    for k in range(owners):
        ends[k][:, tail : tail + LANES] = decays
    bufs = (vb0, vb1)
    for j in range(len(tiles)):
        project(j, bufs[j % 2])
        if j == 0:
            maps()
        else:
            finish(j - 1, bufs[(j - 1) % 2])
    finish(len(tiles) - 1, bufs[(len(tiles) - 1) % 2])
    if loads:
        copy.wait()


def inside_kernel(
    head_width, owners, axis, runs, tok, gw, b_rows, c_rows, vc, mid, dtt, cum, cumt, thr, sel, skip,
    *refs,
):
    part_out, grow_out, scores, gb0, gb1 = refs[-5:]
    rows, inner = vc.shape
    tiles = pieces(inner, TILE)
    spans = pieces(rows)
    r = lax.broadcasted_iota(jnp.int32, (CHUNK, CHUNK), 0)
    s = lax.broadcasted_iota(jnp.int32, (CHUNK, CHUNK), 1)
    wide = 2 * head_width
    assert wide == CHUNK
    lane = lax.broadcasted_iota(jnp.int32, (CHUNK, wide), 1)
    flat = lane[:1]

    def project(j, buf):
        buf[...] = mm(tok[...], gw[:, tiles[j]]).astype(BF16)

    def score():
        for q, span in enumerate(spans):
            scores[q] = jnp.where(r >= s, mm_t(c_rows[span, :], b_rows[span, :]), 0.0)

    def finish(j, buf):
        tile = tiles[j]
        base = mm(thr[...], sel[:, tile])
        for q, span in enumerate(spans):
            swish = silu(buf[span, :].astype(F32))
            if q > 0:
                carried = mm(c_rows[span, :], mid[q - 1, :, tile])
            for cut in pieces(TILE, wide):
                at = slice(tile.start + cut.start, tile.start + cut.stop)
                first = at.start // head_width
                block = vc[span, at]
                mixes, halves, columns = [], [], []
                for k in range(2):
                    head = first + k
                    column = jnp.broadcast_to(cum[span, head : head + 1], (CHUNK, CHUNK))
                    columns.append(column)
                    gap = jnp.minimum(column - cumt[q, head : head + 1, :], 0.0)
                    mixes.append(
                        (scores[q] * jnp.exp2(gap) * dtt[q, head : head + 1, :]).astype(BF16)
                    )
                    halves.append(
                        jnp.where((lane >= head_width) == (k == 1), block, jnp.zeros_like(block))
                    )
                mixture = mm(jnp.concatenate(mixes, axis=1), jnp.concatenate(halves, axis=0))
                gain = jnp.where(flat < head_width, skip[first], skip[first + 1])
                mixture = mixture + gain * block.astype(F32)
                rise = jnp.exp2(jnp.where(lane < head_width, columns[0], columns[1]))
                gated = swish[:, cut] * rise
                if q > 0:
                    mixture = mixture + carried[:, cut] * rise
                    gated = gated * base[8 + q : 9 + q, cut]
                grow_out[span, at] = gated.astype(BF16)
                part_out[span, at] = mixture * swish[:, cut]

    bufs = (gb0, gb1)

    def run(first, last):
        for j in range(first, last):
            project(j, bufs[j % 2])
            if j == first:
                score()
            else:
                finish(j - 1, bufs[(j - 1) % 2])
        finish(last - 1, bufs[(last - 1) % 2])

    for first, last, side in runs:
        if side is None:
            run(first, last)
        else:
            half = lax.axis_index(axis) // owners
            pl.when(half == side)(functools.partial(run, first, last))


def total_kernel(owners, axis, index, batch, *refs):
    came, sel = refs[:owners], refs[owners]
    total_out, decay_out, held, lines = refs[-4:]
    inner = sel.shape[1]
    at = slice(index * inner, (index + 1) * inner)
    tail = slice(batch * inner + index * LANES, batch * inner + (index + 1) * LANES)
    spot = lax.rem(lax.axis_index(axis), owners)
    lines[...] = jnp.zeros_like(lines)
    for k in range(owners):
        owner = jnp.bitwise_xor(spot, k)
        held[owner] = came[k][:, at]
        lines[pl.ds(owner, 1), :] = came[k][:, tail].astype(F32)[:1]
    decay_out[...] = mm(lines[...].astype(BF16), sel[...])
    state = held[0].astype(F32)
    for k in range(1, owners):
        state = state * decay_out[pl.ds(k, 1), :] + held[k].astype(F32)
    total_out[...] = state.astype(BF16)


def prefix_kernel(owners, axis, index, *refs):
    came = refs[:owners]
    decay, first = refs[owners : owners + 2]
    outs = refs[-owners - 2 : -2]
    held, made = refs[-2:]
    inner = decay.shape[1]
    at = slice(index * inner, (index + 1) * inner)
    spot = lax.rem(lax.axis_index(axis), owners)
    for k in range(owners):
        held[jnp.bitwise_xor(spot, k)] = came[k][:, at]
    state = first[...].astype(F32)
    for k in range(owners):
        made[k] = state.astype(BF16)
        if k + 1 < owners:
            state = state * decay[pl.ds(k, 1), :] + held[k].astype(F32)
    for k in range(owners):
        outs[k][...] = made[jnp.bitwise_xor(spot, k)]


def enter_kernel(owners, axis, part, grow, c_rows, *refs):
    came = refs[:owners]
    out, sq_out, state = refs[-3:]
    rows, inner = part.shape
    share = came[0].shape[0]
    spot = lax.rem(lax.axis_index(axis), owners)
    for k in range(owners):
        at = pl.multiple_of(jnp.bitwise_xor(spot, k) * share, share)
        state[pl.ds(at, share), :] = came[k][...]
    for span in pieces(rows):
        acc = jnp.zeros((CHUNK, LANES), F32)
        for at in pieces(inner, TILE):
            extra = mm(c_rows[span, :], state[:, at])
            total = part[span, at] + grow[span, at].astype(F32) * extra
            out[span, at] = total
            for cut in pieces(TILE, LANES):
                acc = acc + total[:, cut] * total[:, cut]
        sq_out[:, span] = jnp.sum(acc.T, axis=0, keepdims=True)


def norm_kernel(inner_all, count, *refs):
    squares = refs[:count]
    x, gain = refs[count : count + 2]
    out = refs[-1]
    rows = out.shape[1]
    span = pl.ds(pl.multiple_of(pl.program_id(0) * rows, rows), rows)
    total = squares[0][:, span]
    for ref in squares[1:]:
        total = total + ref[:, span]
    inverse = lax.rsqrt(total / inner_all + EPS)
    columns = jnp.broadcast_to(inverse, (LANES, rows)).T
    gains = row(gain)
    for cut in pieces(out.shape[2], LANES):
        out[0, :, cut] = (x[span, cut] * columns * gains[:, cut]).astype(BF16)


def local(
    tokens,
    gate_weight,
    value_weight,
    state_weight,
    step_weight,
    value_kernel,
    value_offset,
    state_kernel,
    state_offset,
    step_offset,
    decay_rate,
    skip_gain,
    norm_gain,
):
    b, t, d = tokens.shape
    inner = gate_weight.shape[1]
    h = step_weight.shape[1]
    n = state_weight.shape[1] // 2
    head_width = inner // h
    peers = lax.axis_size("seq")
    ranks = lax.axis_size("head")
    owners = peers // 2
    share = n // owners
    chunks = t // CHUNK
    assert h <= SLOT and owners * 2 == peers and owners & (owners - 1) == 0
    assert b == 2 and chunks < 8 and value_kernel.shape[0] == 4
    lines = max(owners, 8)

    def swap(arrays):
        return [arrays[0]] + [
            here(lax.ppermute(arrays[k], "seq", [(s, s ^ k) for s in range(peers)]))
            for k in range(1, owners)
        ]

    halo = here(
        lax.ppermute(tokens[:, t - PAD :], "seq", [(s, s + 1) for s in range(peers - 1)])
    )
    outs = pl.pallas_call(
        functools.partial(front_kernel, head_width),
        in_specs=[FAR] * 6,
        out_specs=[WHOLE] * (3 + 7 * b),
        out_shape=[
            pltpu.VMEM(state_weight.shape, BF16),
            pltpu.VMEM(value_weight.shape, BF16),
            pltpu.VMEM((LANES, inner), BF16),
        ]
        + [
            pltpu.VMEM((t, d), BF16),
            pltpu.VMEM((t, 2 * n), BF16),
            pltpu.VMEM((t, LANES), BF16),
            pltpu.VMEM((16, LANES), BF16),
            pltpu.VMEM((t, LANES), F32),
            pltpu.VMEM((chunks, SLOT, CHUNK), F32),
            pltpu.VMEM((chunks, SLOT, CHUNK), F32),
        ]
        * b,
        scratch_shapes=[
            pltpu.VMEM((h, d), BF16),
            pltpu.VMEM((h,), F32),
            pltpu.VMEM((h,), F32),
            pltpu.VMEM((LANES, d), BF16),
            pltpu.VMEM((8, LANES), F32),
            pltpu.SemaphoreType.DMA((b + 5,)),
        ],
        compiler_params=params(16),
        name="front",
        cost_estimate=cost(2 * b * t * d * (2 * n + LANES)),
    )(*map(far, (tokens, state_weight, step_weight.T, value_weight, step_offset, decay_rate)))
    sw, w, sel = outs[:3]
    fronts = [outs[3 + 7 * i : 10 + 7 * i] for i in range(b)]

    wide = b * (inner + LANES)

    def values(i, ends):
        tok, io, close, thr, _, _, _ = fronts[i]
        loads = i == b - 1
        inputs = 12 + loads
        return pl.pallas_call(
            functools.partial(values_kernel, owners, "seq", i, b),
            in_specs=[WHOLE] * 12 + [FAR] * loads + [WHOLE] * len(ends),
            out_specs=[WHOLE] * (4 + loads + owners),
            out_shape=[
                pltpu.VMEM((t, inner), BF16),
                pltpu.VMEM((chunks - 1, n, inner), BF16),
                pltpu.VMEM((t, n), BF16),
                pltpu.VMEM((t, n), BF16),
            ]
            + [pltpu.VMEM(gate_weight.shape, BF16)] * loads
            + [pltpu.VMEM((share, wide), BF16)] * owners,
            scratch_shapes=[
                pltpu.SemaphoreType.DMA,
                pltpu.VMEM((n, t), BF16),
                pltpu.VMEM((t + PAD, 2 * n), F32),
                pltpu.VMEM((n, TILE), F32),
                pltpu.VMEM((t + PAD, TILE), F32),
                pltpu.VMEM((t + PAD, TILE), F32),
            ],
            input_output_aliases={inputs + k: 4 + loads + k for k in range(len(ends))},
            compiler_params=params(16),
            name=f"values{i}",
            cost_estimate=cost(2 * t * d * inner),
        )(
            tok, io, close, thr, halo, w, sw, value_kernel, value_offset,
            state_kernel, state_offset, sel, *[far(gate_weight)] * loads, *ends,
        )

    made, ends = [], ()
    for i in range(b):
        outs = values(i, ends)
        made.append(outs[:4])
        ends = outs[-owners:]
    gw = outs[4]

    def inside(i, runs, gw, made, prior, after):
        tok, _, _, thr, cum, cumt, dtt = fronts[i]
        vc, mid, b_rows, c_rows = made[:4]
        return pl.pallas_call(
            functools.partial(inside_kernel, head_width, owners, "seq", runs),
            in_specs=[WHOLE] * 11 + [SCALARS] + [WHOLE] * (len(prior) + len(after)),
            out_specs=[WHOLE] * 2,
            out_shape=[pltpu.VMEM((t, inner), F32), pltpu.VMEM((t, inner), BF16)],
            scratch_shapes=[
                pltpu.VMEM((chunks, CHUNK, CHUNK), F32),
                pltpu.VMEM((t, TILE), BF16),
                pltpu.VMEM((t, TILE), BF16),
            ],
            input_output_aliases={12 + k: k for k in range(len(prior))},
            compiler_params=params(16),
            name=f"inside{i}",
            cost_estimate=cost(2.5 * t * d * inner),
        )(
            tok, gw, b_rows, c_rows, vc, mid, dtt, cum, cumt, thr, sel, skip_gain,
            *prior, *after,
        )

    def total(i, came, after):
        return pl.pallas_call(
            functools.partial(total_kernel, owners, "seq", i, b),
            in_specs=[WHOLE] * (owners + 1 + len(after)),
            out_specs=[WHOLE] * 2,
            out_shape=[pltpu.VMEM((share, inner), BF16), pltpu.VMEM((lines, inner), F32)],
            scratch_shapes=[
                pltpu.VMEM((owners, share, inner), BF16),
                pltpu.VMEM((lines, LANES), F32),
            ],
            compiler_params=params(16),
            name=f"total{i}",
        )(*came, sel, *after)

    def prefix(i, came, decay, first, after):
        return pl.pallas_call(
            functools.partial(prefix_kernel, owners, "seq", i),
            in_specs=[WHOLE] * (owners + 2 + len(after)),
            out_specs=[WHOLE] * owners,
            out_shape=[pltpu.VMEM((share, inner), BF16)] * owners,
            scratch_shapes=[
                pltpu.VMEM((owners, share, inner), BF16),
                pltpu.VMEM((owners, share, inner), BF16),
            ],
            compiler_params=params(16),
            name=f"prefix{i}",
        )(*came, decay, first, *after)

    def across(x):
        return here(lax.ppermute(x, "seq", [(s, s + owners) for s in range(owners)]))

    def enter(i, part, grow, c_rows, states, after):
        x, sq = pl.pallas_call(
            functools.partial(enter_kernel, owners, "seq"),
            in_specs=[WHOLE] * (3 + owners + len(after)),
            out_specs=[WHOLE] * 2,
            out_shape=[pltpu.VMEM((t, inner), F32), pltpu.VMEM((1, t), F32)],
            scratch_shapes=[pltpu.VMEM((n, inner), BF16)],
            compiler_params=params(16),
            name=f"enter{i}",
        )(part, grow, c_rows, *states, *after)
        return x, [sq] + [
            here(lax.ppermute(sq, "head", [(s, (s + k) % ranks) for s in range(ranks)]))
            for k in range(1, ranks)
        ]

    def norm(i, x, squares, into):
        rows = min(t, 256)
        return pl.pallas_call(
            functools.partial(norm_kernel, inner * ranks, ranks),
            grid=(t // rows,),
            in_specs=[WHOLE] * (ranks + 2) + [FAR] * len(into),
            out_specs=pl.BlockSpec((1, rows, inner), lambda q: (i, q, 0)),
            out_shape=jax.ShapeDtypeStruct((b, t, inner), BF16),
            input_output_aliases={ranks + 2: 0} if into else {},
            compiler_params=params(16),
            name=f"norm{i}",
        )(*squares, x, norm_gain, *into)

    came = swap(ends)
    tiles = inner // TILE
    ahead = tiles - 1
    part0, grow0 = inside(0, ((0, tiles, None),), gw, made[0], (), ())
    early = inside(1, ((0, ahead, 0), (0, 1, 1)), gw, made[1], (), (grow0,))
    whole0, decay0 = total(0, came, (early[1],))
    first0 = across(whole0)
    whole1, decay1 = total(1, came, (whole0,))
    first1 = across(whole1)
    late = ((1, tiles, 1), (ahead, tiles, 0))
    part1, grow1 = inside(1, late, gw, made[1], early, (whole1,))
    sent0 = prefix(0, came, decay0, first0, (grow1,))
    back0 = swap(sent0)
    sent1 = prefix(1, came, decay1, first1, (sent0[1],))
    back1 = swap(sent1)
    x0, squares0 = enter(0, part0, grow0, made[0][3], back0, (sent1[1],))
    x1, squares1 = enter(1, part1, grow1, made[1][3], back1, (squares0[0],))
    out = norm(0, x0, squares0, ())
    return norm(1, x1, squares1, (out,))


def solution(mesh):
    return jax.shard_map(
        local,
        mesh=mesh,
        in_specs=(
            P(None, "seq", None),
            P(None, "head"),
            P(None, "head"),
            P(),
            P(None, "head"),
            P(None, "head"),
            P("head"),
            P(),
            P(),
            P("head"),
            P("head"),
            P("head"),
            P("head"),
        ),
        out_specs=P(None, "seq", "head"),
        check_vma=False,
    )
```

```python
import functools
import jax
import jax.numpy as jnp
from jax import lax
from jax.experimental import pallas as pl
from jax.experimental.pallas import tpu as pltpu
from jax.sharding import PartitionSpec as P

EPS = 1e-05
LOG2E = 1.4426950408889634
PAD = 16
CHUNK = 128
TILE = 256
LANES = 128
SLOT = 32
F32 = jnp.float32
BF16 = jnp.bfloat16
WHOLE = pl.BlockSpec(memory_space=pltpu.VMEM)
FAR = pl.BlockSpec(memory_space=pltpu.HBM)
SCALARS = pl.BlockSpec(memory_space=pltpu.SMEM)


def here(x):
    return pltpu.with_memory_space_constraint(x, pltpu.VMEM)


def far(x):
    return pltpu.with_memory_space_constraint(x, pltpu.HBM)


def params(mib):
    return pltpu.CompilerParams(vmem_limit_bytes=mib << 20)


def cost(flops):
    return pl.CostEstimate(flops=int(flops), transcendentals=0, bytes_accessed=0)


def mm(a, b):
    return jnp.dot(a, b, preferred_element_type=F32)


def mm_t(a, b):
    return lax.dot_general(a, b, (((1,), (1,)), ((), ())), preferred_element_type=F32)


def silu(x):
    half = 0.5 * x
    return half + half * jnp.tanh(half)


def row(ref):
    return ref[...].reshape(1, ref.shape[0])


def pieces(total, size=CHUNK):
    return [slice(k * size, (k + 1) * size) for k in range(total // size)]


def head_select(width, head_width, group):
    lane = lax.broadcasted_iota(jnp.int32, (LANES, width), 0) - 2 * SLOT * group
    col = lax.broadcasted_iota(jnp.int32, (LANES, width), 1)
    start = (lane & (SLOT - 1)) * head_width
    hit = (lane >= 0) & (lane < 2 * SLOT) & (col >= start) & (col < start + head_width)
    return jnp.where(hit, 1.0, 0.0).astype(BF16)


def conv_of(x, kernel, offset):
    back = pltpu.roll(x, 1, 0)
    near = offset + kernel[3:4] * x + kernel[2:3] * back
    deep = kernel[1:2] * x + kernel[0:1] * back
    return silu((near + pltpu.roll(deep, 2, 0))[PAD:]).astype(BF16)


def front_kernel(head_width, *refs):
    tok_in, sw_in, twt_in, w_in, toff_in, rate_in = refs[:6]
    batch = tok_in.shape[0]
    sw, w, sel = refs[6:9]
    per_batch = [refs[9 + 7 * i : 16 + 7 * i] for i in range(batch)]
    twt, toff, rate, tws, vec, sem = refs[9 + 7 * batch :]
    rows = tok_in.shape[1]
    heads = twt.shape[0]
    token_copies = [
        pltpu.make_async_copy(tok_in.at[i], per_batch[i][0], sem.at[i]) for i in range(batch)
    ]
    copies = [
        pltpu.make_async_copy(twt_in, twt, sem.at[batch]),
        pltpu.make_async_copy(toff_in, toff, sem.at[batch + 1]),
        pltpu.make_async_copy(rate_in, rate, sem.at[batch + 2]),
        pltpu.make_async_copy(sw_in, sw, sem.at[batch + 3]),
        pltpu.make_async_copy(w_in, w, sem.at[batch + 4]),
    ]
    for copy in copies[:3] + [token_copies[0], copies[3]] + token_copies[1:] + [copies[4]]:
        copy.start()
    sel[...] = head_select(sel.shape[1], head_width, 0)
    for copy in copies[:3]:
        copy.wait()
    tws[...] = jnp.zeros_like(tws)
    vec[...] = jnp.zeros_like(vec)
    for g in range(LANES // SLOT):
        tws[pl.ds(g * SLOT, heads), :] = twt[...]
        vec[pl.ds(0, 1), pl.ds(g * SLOT, heads)] = row(toff)
        vec[pl.ds(1, 1), pl.ds(g * SLOT, heads)] = row(rate)
    offset = vec[pl.ds(0, 1), :]
    scale = vec[pl.ds(1, 1), :] * (-LOG2E)
    r = lax.broadcasted_iota(jnp.int32, (CHUNK, CHUNK), 0)
    c = lax.broadcasted_iota(jnp.int32, (CHUNK, CHUNK), 1)
    tri = jnp.where(r >= c, 1.0, 0.0).astype(BF16)
    group = lax.broadcasted_iota(jnp.int32, (1, LANES), 1) // SLOT
    low_lane = (group & 1) == 1

    def parts(x):
        hi = x.astype(BF16).astype(F32)
        return jnp.where(low_lane, x - hi, hi).astype(BF16)

    for i in range(batch):
        tok, io_out, close_out, thr_out, cum_out, cumt_out, dtt_out = per_batch[i]
        token_copies[i].wait()
        if i == 0:
            copies[3].wait()
        x = tok[...]
        io_out[...] = mm(x, sw[...]).astype(BF16)
        z = mm_t(x, tws[...]) + offset
        dt = jnp.maximum(z, 0.0) + jnp.log1p(jnp.exp(-jnp.abs(z)))
        log_decay = dt * scale
        base = jnp.zeros((1, LANES), F32)
        lasts, bases = [], []
        for q, span in enumerate(pieces(rows)):
            part = log_decay[span]
            hi = part.astype(BF16)
            rest = part - hi.astype(F32)
            mid = rest.astype(BF16)
            low = (rest - mid.astype(F32)).astype(BF16)
            cum = mm(tri, hi) + (mm(tri, mid) + mm(tri, low))
            last = cum[CHUNK - 1 :]
            cum_out[span, :] = cum
            cumt_out[q] = cum.T[:SLOT]
            dtt_out[q] = dt[span].T[:SLOT]
            close_out[span, :] = parts(jnp.exp2(last - cum) * dt[span])
            lasts.append(last)
            bases.append(base)
            base = base + last
        zero = [jnp.zeros((1, LANES), F32)]
        table = lasts + [base] + zero * (7 - len(lasts)) + bases + zero * (8 - len(bases))
        thr_out[...] = parts(jnp.exp2(jnp.concatenate(table, axis=0)))
    copies[4].wait()


def values_kernel(owners, axis, index, batch, *refs):
    tok, io, close, thr, halo, w, sw, vkern, voff, skern, soff, sel = refs[:12]
    loads = index == batch - 1
    sem = refs[-6]
    bt, mbuf, hold, vb0, vb1 = refs[-5:]
    ends = refs[-6 - owners : -6]
    if loads:
        gate_in, gw = refs[12], refs[-7 - owners]
        copy = pltpu.make_async_copy(gate_in, gw, sem)
        copy.start()
    first = -6 - owners - loads - 4
    vc_out, mid_out, b_out, c_out = refs[first : first + 4]
    rows = tok.shape[0]
    inner = w.shape[1]
    n = sw.shape[1] // 2
    share = n // owners
    spot = lax.rem(lax.axis_index(axis), owners)
    tiles = pieces(inner, TILE)
    rim = halo[index]
    offset = row(voff)

    def project(j, buf):
        x = jnp.concatenate([rim, tok[...]], axis=0)
        buf[...] = mm(x, w[:, tiles[j]]).astype(BF16).astype(F32)

    def maps():
        mbuf[pl.ds(0, PAD), :] = mm(rim, sw[...]).astype(BF16).astype(F32)
        mbuf[pl.ds(PAD, rows), :] = io[...].astype(F32)
        y = conv_of(mbuf[...], skern[...], row(soff))
        b_out[...] = y[:, :n]
        c_out[...] = y[:, n:]
        bt[...] = y[:, :n].astype(F32).T.astype(BF16)

    def finish(j, buf):
        at = tiles[j]
        vc = conv_of(buf[...], vkern[:, at], offset[:, at])
        vc_out[:, at] = vc
        select = sel[:, at]
        through = mm(thr[...], select)
        state = None
        for q, span in enumerate(pieces(rows)):
            scaled = (vc[span].astype(F32) * mm(close[span, :], select)).astype(BF16)
            made = mm(bt[:, span], scaled)
            if q == 0:
                state = made
            else:
                mid_out[q - 1, :, at] = state.astype(BF16)
                state = state * through[q : q + 1] + made
        hold[...] = state
        for k in range(owners):
            owner = jnp.bitwise_xor(spot, k)
            part = hold[pl.ds(pl.multiple_of(owner * share, share), share), :]
            ends[k][:, index * inner + at.start : index * inner + at.stop] = part.astype(BF16)

    line = lax.broadcasted_iota(jnp.int32, (share, LANES), 0)
    count = rows // CHUNK
    mine = jnp.broadcast_to(thr[...].astype(F32)[count : count + 1], (share, LANES))
    decays = jnp.where(line == 0, mine, 0.0).astype(BF16)
    tail = batch * inner + index * LANES
    for k in range(owners):
        ends[k][:, tail : tail + LANES] = decays
    bufs = (vb0, vb1)
    for j in range(len(tiles)):
        project(j, bufs[j % 2])
        if j == 0:
            maps()
        else:
            finish(j - 1, bufs[(j - 1) % 2])
    finish(len(tiles) - 1, bufs[(len(tiles) - 1) % 2])
    if loads:
        copy.wait()


def inside_kernel(
    head_width, owners, axis, runs, tok, gw, b_rows, c_rows, vc, mid, dtt, cum, cumt, thr, sel, skip,
    *refs,
):
    part_out, grow_out, scores, gb0, gb1 = refs[-5:]
    rows, inner = vc.shape
    tiles = pieces(inner, TILE)
    spans = pieces(rows)
    r = lax.broadcasted_iota(jnp.int32, (CHUNK, CHUNK), 0)
    s = lax.broadcasted_iota(jnp.int32, (CHUNK, CHUNK), 1)
    wide = 2 * head_width
    assert wide == CHUNK
    lane = lax.broadcasted_iota(jnp.int32, (CHUNK, wide), 1)
    flat = lane[:1]

    def project(j, buf):
        buf[...] = mm(tok[...], gw[:, tiles[j]]).astype(BF16)

    def score():
        for q, span in enumerate(spans):
            scores[q] = jnp.where(r >= s, mm_t(c_rows[span, :], b_rows[span, :]), 0.0)

    def finish(j, buf):
        tile = tiles[j]
        base = mm(thr[...], sel[:, tile])
        for q, span in enumerate(spans):
            swish = silu(buf[span, :].astype(F32))
            if q > 0:
                carried = mm(c_rows[span, :], mid[q - 1, :, tile])
            for cut in pieces(TILE, wide):
                at = slice(tile.start + cut.start, tile.start + cut.stop)
                first = at.start // head_width
                block = vc[span, at]
                mixes, halves, columns = [], [], []
                for k in range(2):
                    head = first + k
                    column = jnp.broadcast_to(cum[span, head : head + 1], (CHUNK, CHUNK))
                    columns.append(column)
                    gap = jnp.minimum(column - cumt[q, head : head + 1, :], 0.0)
                    mixes.append(
                        (scores[q] * jnp.exp2(gap) * dtt[q, head : head + 1, :]).astype(BF16)
                    )
                    halves.append(
                        jnp.where((lane >= head_width) == (k == 1), block, jnp.zeros_like(block))
                    )
                mixture = mm(jnp.concatenate(mixes, axis=1), jnp.concatenate(halves, axis=0))
                gain = jnp.where(flat < head_width, skip[first], skip[first + 1])
                mixture = mixture + gain * block.astype(F32)
                rise = jnp.exp2(jnp.where(lane < head_width, columns[0], columns[1]))
                gated = swish[:, cut] * rise
                if q > 0:
                    mixture = mixture + carried[:, cut] * rise
                    gated = gated * base[8 + q : 9 + q, cut]
                grow_out[span, at] = gated.astype(BF16)
                part_out[span, at] = mixture * swish[:, cut]

    bufs = (gb0, gb1)

    def run(first, last):
        for j in range(first, last):
            project(j, bufs[j % 2])
            if j == first:
                score()
            else:
                finish(j - 1, bufs[(j - 1) % 2])
        finish(last - 1, bufs[(last - 1) % 2])

    for first, last, side in runs:
        if side is None:
            run(first, last)
        else:
            half = lax.axis_index(axis) // owners
            pl.when(half == side)(functools.partial(run, first, last))


def total_kernel(owners, axis, index, batch, *refs):
    came, sel = refs[:owners], refs[owners]
    total_out, decay_out, held, lines = refs[-4:]
    inner = sel.shape[1]
    at = slice(index * inner, (index + 1) * inner)
    tail = slice(batch * inner + index * LANES, batch * inner + (index + 1) * LANES)
    spot = lax.rem(lax.axis_index(axis), owners)
    lines[...] = jnp.zeros_like(lines)
    for k in range(owners):
        owner = jnp.bitwise_xor(spot, k)
        held[owner] = came[k][:, at]
        lines[pl.ds(owner, 1), :] = came[k][:, tail].astype(F32)[:1]
    decay_out[...] = mm(lines[...].astype(BF16), sel[...])
    state = held[0].astype(F32)
    for k in range(1, owners):
        state = state * decay_out[pl.ds(k, 1), :] + held[k].astype(F32)
    total_out[...] = state.astype(BF16)


def prefix_kernel(owners, axis, index, *refs):
    came = refs[:owners]
    decay, first = refs[owners : owners + 2]
    outs = refs[-owners - 2 : -2]
    held, made = refs[-2:]
    inner = decay.shape[1]
    at = slice(index * inner, (index + 1) * inner)
    spot = lax.rem(lax.axis_index(axis), owners)
    for k in range(owners):
        held[jnp.bitwise_xor(spot, k)] = came[k][:, at]
    state = first[...].astype(F32)
    for k in range(owners):
        made[k] = state.astype(BF16)
        if k + 1 < owners:
            state = state * decay[pl.ds(k, 1), :] + held[k].astype(F32)
    for k in range(owners):
        outs[k][...] = made[jnp.bitwise_xor(spot, k)]


def enter_kernel(owners, axis, part, grow, c_rows, *refs):
    came = refs[:owners]
    out, sq_out, state = refs[-3:]
    rows, inner = part.shape
    share = came[0].shape[0]
    spot = lax.rem(lax.axis_index(axis), owners)
    for k in range(owners):
        at = pl.multiple_of(jnp.bitwise_xor(spot, k) * share, share)
        state[pl.ds(at, share), :] = came[k][...]
    for span in pieces(rows):
        acc = jnp.zeros((CHUNK, LANES), F32)
        for at in pieces(inner, TILE):
            extra = mm(c_rows[span, :], state[:, at])
            total = part[span, at] + grow[span, at].astype(F32) * extra
            out[span, at] = total
            for cut in pieces(TILE, LANES):
                acc = acc + total[:, cut] * total[:, cut]
        sq_out[:, span] = jnp.sum(acc.T, axis=0, keepdims=True)


def norm_kernel(inner_all, count, *refs):
    squares = refs[:count]
    x, gain = refs[count : count + 2]
    out = refs[-1]
    rows = out.shape[1]
    span = pl.ds(pl.multiple_of(pl.program_id(0) * rows, rows), rows)
    total = squares[0][:, span]
    for ref in squares[1:]:
        total = total + ref[:, span]
    inverse = lax.rsqrt(total / inner_all + EPS)
    columns = jnp.broadcast_to(inverse, (LANES, rows)).T
    gains = row(gain)
    for cut in pieces(out.shape[2], LANES):
        out[0, :, cut] = (x[span, cut] * columns * gains[:, cut]).astype(BF16)


def local(
    tokens,
    gate_weight,
    value_weight,
    state_weight,
    step_weight,
    value_kernel,
    value_offset,
    state_kernel,
    state_offset,
    step_offset,
    decay_rate,
    skip_gain,
    norm_gain,
):
    b, t, d = tokens.shape
    inner = gate_weight.shape[1]
    h = step_weight.shape[1]
    n = state_weight.shape[1] // 2
    head_width = inner // h
    peers = lax.axis_size("seq")
    ranks = lax.axis_size("head")
    owners = peers // 2
    share = n // owners
    chunks = t // CHUNK
    assert h <= SLOT and owners * 2 == peers and owners & (owners - 1) == 0
    assert b == 2 and chunks < 8 and value_kernel.shape[0] == 4
    lines = max(owners, 8)

    def swap(arrays):
        return [arrays[0]] + [
            here(lax.ppermute(arrays[k], "seq", [(s, s ^ k) for s in range(peers)]))
            for k in range(1, owners)
        ]

    halo = here(
        lax.ppermute(tokens[:, t - PAD :], "seq", [(s, s + 1) for s in range(peers - 1)])
    )
    outs = pl.pallas_call(
        functools.partial(front_kernel, head_width),
        in_specs=[FAR] * 6,
        out_specs=[WHOLE] * (3 + 7 * b),
        out_shape=[
            pltpu.VMEM(state_weight.shape, BF16),
            pltpu.VMEM(value_weight.shape, BF16),
            pltpu.VMEM((LANES, inner), BF16),
        ]
        + [
            pltpu.VMEM((t, d), BF16),
            pltpu.VMEM((t, 2 * n), BF16),
            pltpu.VMEM((t, LANES), BF16),
            pltpu.VMEM((16, LANES), BF16),
            pltpu.VMEM((t, LANES), F32),
            pltpu.VMEM((chunks, SLOT, CHUNK), F32),
            pltpu.VMEM((chunks, SLOT, CHUNK), F32),
        ]
        * b,
        scratch_shapes=[
            pltpu.VMEM((h, d), BF16),
            pltpu.VMEM((h,), F32),
            pltpu.VMEM((h,), F32),
            pltpu.VMEM((LANES, d), BF16),
            pltpu.VMEM((8, LANES), F32),
            pltpu.SemaphoreType.DMA((b + 5,)),
        ],
        compiler_params=params(16),
        name="front",
        cost_estimate=cost(2 * b * t * d * (2 * n + LANES)),
    )(*map(far, (tokens, state_weight, step_weight.T, value_weight, step_offset, decay_rate)))
    sw, w, sel = outs[:3]
    fronts = [outs[3 + 7 * i : 10 + 7 * i] for i in range(b)]

    wide = b * (inner + LANES)

    def values(i, ends):
        tok, io, close, thr, _, _, _ = fronts[i]
        loads = i == b - 1
        inputs = 12 + loads
        return pl.pallas_call(
            functools.partial(values_kernel, owners, "seq", i, b),
            in_specs=[WHOLE] * 12 + [FAR] * loads + [WHOLE] * len(ends),
            out_specs=[WHOLE] * (4 + loads + owners),
            out_shape=[
                pltpu.VMEM((t, inner), BF16),
                pltpu.VMEM((chunks - 1, n, inner), BF16),
                pltpu.VMEM((t, n), BF16),
                pltpu.VMEM((t, n), BF16),
            ]
            + [pltpu.VMEM(gate_weight.shape, BF16)] * loads
            + [pltpu.VMEM((share, wide), BF16)] * owners,
            scratch_shapes=[
                pltpu.SemaphoreType.DMA,
                pltpu.VMEM((n, t), BF16),
                pltpu.VMEM((t + PAD, 2 * n), F32),
                pltpu.VMEM((n, TILE), F32),
                pltpu.VMEM((t + PAD, TILE), F32),
                pltpu.VMEM((t + PAD, TILE), F32),
            ],
            input_output_aliases={inputs + k: 4 + loads + k for k in range(len(ends))},
            compiler_params=params(16),
            name=f"values{i}",
            cost_estimate=cost(2 * t * d * inner),
        )(
            tok, io, close, thr, halo, w, sw, value_kernel, value_offset,
            state_kernel, state_offset, sel, *[far(gate_weight)] * loads, *ends,
        )

    made, ends = [], ()
    for i in range(b):
        outs = values(i, ends)
        made.append(outs[:4])
        ends = outs[-owners:]
    gw = outs[4]

    def inside(i, runs, gw, made, prior, after):
        tok, _, _, thr, cum, cumt, dtt = fronts[i]
        vc, mid, b_rows, c_rows = made[:4]
        return pl.pallas_call(
            functools.partial(inside_kernel, head_width, owners, "seq", runs),
            in_specs=[WHOLE] * 11 + [SCALARS] + [WHOLE] * (len(prior) + len(after)),
            out_specs=[WHOLE] * 2,
            out_shape=[pltpu.VMEM((t, inner), F32), pltpu.VMEM((t, inner), BF16)],
            scratch_shapes=[
                pltpu.VMEM((chunks, CHUNK, CHUNK), F32),
                pltpu.VMEM((t, TILE), BF16),
                pltpu.VMEM((t, TILE), BF16),
            ],
            input_output_aliases={12 + k: k for k in range(len(prior))},
            compiler_params=params(16),
            name=f"inside{i}",
            cost_estimate=cost(2.5 * t * d * inner),
        )(
            tok, gw, b_rows, c_rows, vc, mid, dtt, cum, cumt, thr, sel, skip_gain,
            *prior, *after,
        )

    def total(i, came, after):
        return pl.pallas_call(
            functools.partial(total_kernel, owners, "seq", i, b),
            in_specs=[WHOLE] * (owners + 1 + len(after)),
            out_specs=[WHOLE] * 2,
            out_shape=[pltpu.VMEM((share, inner), BF16), pltpu.VMEM((lines, inner), F32)],
            scratch_shapes=[
                pltpu.VMEM((owners, share, inner), BF16),
                pltpu.VMEM((lines, LANES), F32),
            ],
            compiler_params=params(16),
            name=f"total{i}",
        )(*came, sel, *after)

    def prefix(i, came, decay, first, after):
        return pl.pallas_call(
            functools.partial(prefix_kernel, owners, "seq", i),
            in_specs=[WHOLE] * (owners + 2 + len(after)),
            out_specs=[WHOLE] * owners,
            out_shape=[pltpu.VMEM((share, inner), BF16)] * owners,
            scratch_shapes=[
                pltpu.VMEM((owners, share, inner), BF16),
                pltpu.VMEM((owners, share, inner), BF16),
            ],
            compiler_params=params(16),
            name=f"prefix{i}",
        )(*came, decay, first, *after)

    def across(x):
        return here(lax.ppermute(x, "seq", [(s, s + owners) for s in range(owners)]))

    def enter(i, part, grow, c_rows, states, after):
        x, sq = pl.pallas_call(
            functools.partial(enter_kernel, owners, "seq"),
            in_specs=[WHOLE] * (3 + owners + len(after)),
            out_specs=[WHOLE] * 2,
            out_shape=[pltpu.VMEM((t, inner), F32), pltpu.VMEM((1, t), F32)],
            scratch_shapes=[pltpu.VMEM((n, inner), BF16)],
            compiler_params=params(16),
            name=f"enter{i}",
        )(part, grow, c_rows, *states, *after)
        return x, [sq] + [
            here(lax.ppermute(sq, "head", [(s, (s + k) % ranks) for s in range(ranks)]))
            for k in range(1, ranks)
        ]

    def norm(i, x, squares, into):
        rows = min(t, 256)
        return pl.pallas_call(
            functools.partial(norm_kernel, inner * ranks, ranks),
            grid=(t // rows,),
            in_specs=[WHOLE] * (ranks + 2) + [FAR] * len(into),
            out_specs=pl.BlockSpec((1, rows, inner), lambda q: (i, q, 0)),
            out_shape=jax.ShapeDtypeStruct((b, t, inner), BF16),
            input_output_aliases={ranks + 2: 0} if into else {},
            compiler_params=params(16),
            name=f"norm{i}",
        )(*squares, x, norm_gain, *into)

    came = swap(ends)
    tiles = inner // TILE
    ahead = tiles - 1
    part0, grow0 = inside(0, ((0, tiles, None),), gw, made[0], (), ())
    early = inside(1, ((0, ahead, 0), (0, 1, 1)), gw, made[1], (), (grow0,))
    whole0, decay0 = total(0, came, (early[1],))
    first0 = across(whole0)
    middle = (1 + tiles) // 2
    mixed = inside(1, ((1, middle, 1), (ahead, tiles, 0)), gw, made[1], early, (whole0,))
    whole1, decay1 = total(1, came, (mixed[1],))
    first1 = across(whole1)
    part1, grow1 = inside(1, ((middle, tiles, 1),), gw, made[1], mixed, (whole1,))
    sent0 = prefix(0, came, decay0, first0, (grow1,))
    back0 = swap(sent0)
    sent1 = prefix(1, came, decay1, first1, (sent0[1],))
    back1 = swap(sent1)
    x0, squares0 = enter(0, part0, grow0, made[0][3], back0, (sent1[1],))
    x1, squares1 = enter(1, part1, grow1, made[1][3], back1, (squares0[0],))
    out = norm(0, x0, squares0, ())
    return norm(1, x1, squares1, (out,))


def solution(mesh):
    return jax.shard_map(
        local,
        mesh=mesh,
        in_specs=(
            P(None, "seq", None),
            P(None, "head"),
            P(None, "head"),
            P(),
            P(None, "head"),
            P(None, "head"),
            P("head"),
            P(),
            P(),
            P("head"),
            P("head"),
            P("head"),
            P("head"),
        ),
        out_specs=P(None, "seq", "head"),
        check_vma=False,
    )
```

```python
import functools
import jax
import jax.numpy as jnp
from jax import lax
from jax.experimental import pallas as pl
from jax.experimental.pallas import tpu as pltpu
from jax.sharding import PartitionSpec as P

EPS = 1e-05
LOG2E = 1.4426950408889634
PAD = 16
CHUNK = 128
TILE = 256
LANES = 128
SLOT = 32
F32 = jnp.float32
BF16 = jnp.bfloat16
WHOLE = pl.BlockSpec(memory_space=pltpu.VMEM)
FAR = pl.BlockSpec(memory_space=pltpu.HBM)
SCALARS = pl.BlockSpec(memory_space=pltpu.SMEM)


def here(x):
    return pltpu.with_memory_space_constraint(x, pltpu.VMEM)


def far(x):
    return pltpu.with_memory_space_constraint(x, pltpu.HBM)


def params(mib):
    return pltpu.CompilerParams(vmem_limit_bytes=mib << 20)


def cost(flops):
    return pl.CostEstimate(flops=int(flops), transcendentals=0, bytes_accessed=0)


def mm(a, b):
    return jnp.dot(a, b, preferred_element_type=F32)


def mm_t(a, b):
    return lax.dot_general(a, b, (((1,), (1,)), ((), ())), preferred_element_type=F32)


def silu(x):
    half = 0.5 * x
    return half + half * jnp.tanh(half)


def row(ref):
    return ref[...].reshape(1, ref.shape[0])


def pieces(total, size=CHUNK):
    return [slice(k * size, (k + 1) * size) for k in range(total // size)]


def head_select(width, head_width, group):
    lane = lax.broadcasted_iota(jnp.int32, (LANES, width), 0) - 2 * SLOT * group
    col = lax.broadcasted_iota(jnp.int32, (LANES, width), 1)
    start = (lane & (SLOT - 1)) * head_width
    hit = (lane >= 0) & (lane < 2 * SLOT) & (col >= start) & (col < start + head_width)
    return jnp.where(hit, 1.0, 0.0).astype(BF16)


def conv_of(x, kernel, offset):
    back = pltpu.roll(x, 1, 0)
    near = offset + kernel[3:4] * x + kernel[2:3] * back
    deep = kernel[1:2] * x + kernel[0:1] * back
    return silu((near + pltpu.roll(deep, 2, 0))[PAD:]).astype(BF16)


def front_kernel(head_width, *refs):
    tok_in, sw_in, twt_in, w_in, toff_in, rate_in = refs[:6]
    batch = tok_in.shape[0]
    sw, w, sel = refs[6:9]
    per_batch = [refs[9 + 7 * i : 16 + 7 * i] for i in range(batch)]
    twt, toff, rate, tws, vec, sem = refs[9 + 7 * batch :]
    rows = tok_in.shape[1]
    heads = twt.shape[0]
    token_copies = [
        pltpu.make_async_copy(tok_in.at[i], per_batch[i][0], sem.at[i]) for i in range(batch)
    ]
    copies = [
        pltpu.make_async_copy(twt_in, twt, sem.at[batch]),
        pltpu.make_async_copy(toff_in, toff, sem.at[batch + 1]),
        pltpu.make_async_copy(rate_in, rate, sem.at[batch + 2]),
        pltpu.make_async_copy(sw_in, sw, sem.at[batch + 3]),
        pltpu.make_async_copy(w_in, w, sem.at[batch + 4]),
    ]
    for copy in copies[:3] + [token_copies[0], copies[3]] + token_copies[1:] + [copies[4]]:
        copy.start()
    sel[...] = head_select(sel.shape[1], head_width, 0)
    for copy in copies[:3]:
        copy.wait()
    tws[...] = jnp.zeros_like(tws)
    vec[...] = jnp.zeros_like(vec)
    for g in range(LANES // SLOT):
        tws[pl.ds(g * SLOT, heads), :] = twt[...]
        vec[pl.ds(0, 1), pl.ds(g * SLOT, heads)] = row(toff)
        vec[pl.ds(1, 1), pl.ds(g * SLOT, heads)] = row(rate)
    offset = vec[pl.ds(0, 1), :]
    scale = vec[pl.ds(1, 1), :] * (-LOG2E)
    r = lax.broadcasted_iota(jnp.int32, (CHUNK, CHUNK), 0)
    c = lax.broadcasted_iota(jnp.int32, (CHUNK, CHUNK), 1)
    tri = jnp.where(r >= c, 1.0, 0.0).astype(BF16)
    group = lax.broadcasted_iota(jnp.int32, (1, LANES), 1) // SLOT
    low_lane = (group & 1) == 1

    def parts(x):
        hi = x.astype(BF16).astype(F32)
        return jnp.where(low_lane, x - hi, hi).astype(BF16)

    for i in range(batch):
        tok, io_out, close_out, thr_out, cum_out, cumt_out, dtt_out = per_batch[i]
        token_copies[i].wait()
        if i == 0:
            copies[3].wait()
        x = tok[...]
        io_out[...] = mm(x, sw[...]).astype(BF16)
        z = mm_t(x, tws[...]) + offset
        dt = jnp.maximum(z, 0.0) + jnp.log1p(jnp.exp(-jnp.abs(z)))
        log_decay = dt * scale
        base = jnp.zeros((1, LANES), F32)
        lasts, bases = [], []
        for q, span in enumerate(pieces(rows)):
            part = log_decay[span]
            hi = part.astype(BF16)
            rest = part - hi.astype(F32)
            mid = rest.astype(BF16)
            low = (rest - mid.astype(F32)).astype(BF16)
            cum = mm(tri, hi) + (mm(tri, mid) + mm(tri, low))
            last = cum[CHUNK - 1 :]
            cum_out[span, :] = cum
            cumt_out[q] = cum.T[:SLOT]
            dtt_out[q] = dt[span].T[:SLOT]
            close_out[span, :] = parts(jnp.exp2(last - cum) * dt[span])
            lasts.append(last)
            bases.append(base)
            base = base + last
        zero = [jnp.zeros((1, LANES), F32)]
        table = lasts + [base] + zero * (7 - len(lasts)) + bases + zero * (8 - len(bases))
        thr_out[...] = parts(jnp.exp2(jnp.concatenate(table, axis=0)))
    copies[4].wait()


def values_kernel(owners, axis, index, batch, *refs):
    tok, io, close, thr, halo, w, sw, vkern, voff, skern, soff, sel = refs[:12]
    loads = index == batch - 1
    sem = refs[-6]
    bt, mbuf, hold, vb0, vb1 = refs[-5:]
    ends = refs[-6 - owners : -6]
    if loads:
        gate_in, gw = refs[12], refs[-7 - owners]
        copy = pltpu.make_async_copy(gate_in, gw, sem)
        copy.start()
    first = -6 - owners - loads - 4
    vc_out, mid_out, b_out, c_out = refs[first : first + 4]
    rows = tok.shape[0]
    inner = w.shape[1]
    n = sw.shape[1] // 2
    share = n // owners
    spot = lax.rem(lax.axis_index(axis), owners)
    tiles = pieces(inner, TILE)
    rim = halo[index]
    offset = row(voff)

    def project(j, buf):
        x = jnp.concatenate([rim, tok[...]], axis=0)
        buf[...] = mm(x, w[:, tiles[j]]).astype(BF16).astype(F32)

    def maps():
        mbuf[pl.ds(0, PAD), :] = mm(rim, sw[...]).astype(BF16).astype(F32)
        mbuf[pl.ds(PAD, rows), :] = io[...].astype(F32)
        y = conv_of(mbuf[...], skern[...], row(soff))
        b_out[...] = y[:, :n]
        c_out[...] = y[:, n:]
        bt[...] = y[:, :n].astype(F32).T.astype(BF16)

    def finish(j, buf):
        at = tiles[j]
        vc = conv_of(buf[...], vkern[:, at], offset[:, at])
        vc_out[:, at] = vc
        select = sel[:, at]
        through = mm(thr[...], select)
        state = None
        for q, span in enumerate(pieces(rows)):
            scaled = (vc[span].astype(F32) * mm(close[span, :], select)).astype(BF16)
            made = mm(bt[:, span], scaled)
            if q == 0:
                state = made
            else:
                mid_out[q - 1, :, at] = state.astype(BF16)
                state = state * through[q : q + 1] + made
        hold[...] = state
        for k in range(owners):
            owner = jnp.bitwise_xor(spot, k)
            part = hold[pl.ds(pl.multiple_of(owner * share, share), share), :]
            ends[k][:, index * inner + at.start : index * inner + at.stop] = part.astype(BF16)

    line = lax.broadcasted_iota(jnp.int32, (share, LANES), 0)
    count = rows // CHUNK
    mine = jnp.broadcast_to(thr[...].astype(F32)[count : count + 1], (share, LANES))
    decays = jnp.where(line == 0, mine, 0.0).astype(BF16)
    tail = batch * inner + index * LANES
    for k in range(owners):
        ends[k][:, tail : tail + LANES] = decays
    bufs = (vb0, vb1)
    for j in range(len(tiles)):
        project(j, bufs[j % 2])
        if j == 0:
            maps()
        else:
            finish(j - 1, bufs[(j - 1) % 2])
    finish(len(tiles) - 1, bufs[(len(tiles) - 1) % 2])
    if loads:
        copy.wait()


def inside_kernel(
    head_width, owners, axis, runs, tok, gw, b_rows, c_rows, vc, mid, dtt, cum, cumt, thr, sel, skip,
    *refs,
):
    part_out, grow_out, scores, gb0, gb1 = refs[-5:]
    rows, inner = vc.shape
    tiles = pieces(inner, TILE)
    spans = pieces(rows)
    r = lax.broadcasted_iota(jnp.int32, (CHUNK, CHUNK), 0)
    s = lax.broadcasted_iota(jnp.int32, (CHUNK, CHUNK), 1)
    wide = 2 * head_width
    assert wide == CHUNK
    lane = lax.broadcasted_iota(jnp.int32, (CHUNK, wide), 1)
    flat = lane[:1]

    def project(j, buf):
        buf[...] = mm(tok[...], gw[:, tiles[j]]).astype(BF16)

    def score():
        for q, span in enumerate(spans):
            scores[q] = jnp.where(r >= s, mm_t(c_rows[span, :], b_rows[span, :]), 0.0)

    def finish(j, buf):
        tile = tiles[j]
        base = mm(thr[...], sel[:, tile])
        for q, span in enumerate(spans):
            swish = silu(buf[span, :].astype(F32))
            if q > 0:
                carried = mm(c_rows[span, :], mid[q - 1, :, tile])
            for cut in pieces(TILE, wide):
                at = slice(tile.start + cut.start, tile.start + cut.stop)
                first = at.start // head_width
                block = vc[span, at]
                mixes, halves, columns = [], [], []
                for k in range(2):
                    head = first + k
                    column = jnp.broadcast_to(cum[span, head : head + 1], (CHUNK, CHUNK))
                    columns.append(column)
                    gap = jnp.minimum(column - cumt[q, head : head + 1, :], 0.0)
                    mixes.append(
                        (scores[q] * jnp.exp2(gap) * dtt[q, head : head + 1, :]).astype(BF16)
                    )
                    halves.append(
                        jnp.where((lane >= head_width) == (k == 1), block, jnp.zeros_like(block))
                    )
                mixture = mm(jnp.concatenate(mixes, axis=1), jnp.concatenate(halves, axis=0))
                gain = jnp.where(flat < head_width, skip[first], skip[first + 1])
                mixture = mixture + gain * block.astype(F32)
                rise = jnp.exp2(jnp.where(lane < head_width, columns[0], columns[1]))
                gated = swish[:, cut] * rise
                if q > 0:
                    mixture = mixture + carried[:, cut] * rise
                    gated = gated * base[8 + q : 9 + q, cut]
                grow_out[span, at] = gated.astype(BF16)
                part_out[span, at] = mixture * swish[:, cut]

    bufs = (gb0, gb1)

    def run(first, last):
        for j in range(first, last):
            project(j, bufs[j % 2])
            if j == first:
                score()
            else:
                finish(j - 1, bufs[(j - 1) % 2])
        finish(last - 1, bufs[(last - 1) % 2])

    for first, last, side in runs:
        if side is None:
            run(first, last)
        else:
            half = lax.axis_index(axis) // owners
            pl.when(half == side)(functools.partial(run, first, last))


def total_kernel(owners, axis, index, batch, *refs):
    came, sel = refs[:owners], refs[owners]
    total_out, decay_out, held, lines = refs[-4:]
    inner = sel.shape[1]
    at = slice(index * inner, (index + 1) * inner)
    tail = slice(batch * inner + index * LANES, batch * inner + (index + 1) * LANES)
    spot = lax.rem(lax.axis_index(axis), owners)
    lines[...] = jnp.zeros_like(lines)
    for k in range(owners):
        owner = jnp.bitwise_xor(spot, k)
        held[owner] = came[k][:, at]
        lines[pl.ds(owner, 1), :] = came[k][:, tail].astype(F32)[:1]
    decay_out[...] = mm(lines[...].astype(BF16), sel[...])
    state = held[0].astype(F32)
    for k in range(1, owners):
        state = state * decay_out[pl.ds(k, 1), :] + held[k].astype(F32)
    total_out[...] = state.astype(BF16)


def prefix_kernel(owners, axis, index, *refs):
    came = refs[:owners]
    decay, first = refs[owners : owners + 2]
    outs = refs[-owners - 2 : -2]
    held, made = refs[-2:]
    inner = decay.shape[1]
    at = slice(index * inner, (index + 1) * inner)
    spot = lax.rem(lax.axis_index(axis), owners)
    for k in range(owners):
        held[jnp.bitwise_xor(spot, k)] = came[k][:, at]
    state = first[...].astype(F32)
    for k in range(owners):
        made[k] = state.astype(BF16)
        if k + 1 < owners:
            state = state * decay[pl.ds(k, 1), :] + held[k].astype(F32)
    for k in range(owners):
        outs[k][...] = made[jnp.bitwise_xor(spot, k)]


def enter_kernel(owners, axis, part, grow, c_rows, *refs):
    came = refs[:owners]
    out, sq_out, state = refs[-3:]
    rows, inner = part.shape
    share = came[0].shape[0]
    spot = lax.rem(lax.axis_index(axis), owners)
    for k in range(owners):
        at = pl.multiple_of(jnp.bitwise_xor(spot, k) * share, share)
        state[pl.ds(at, share), :] = came[k][...]
    for span in pieces(rows):
        acc = jnp.zeros((CHUNK, LANES), F32)
        for at in pieces(inner, TILE):
            extra = mm(c_rows[span, :], state[:, at])
            total = part[span, at] + grow[span, at].astype(F32) * extra
            out[span, at] = total
            for cut in pieces(TILE, LANES):
                acc = acc + total[:, cut] * total[:, cut]
        sq_out[:, span] = jnp.sum(acc.T, axis=0, keepdims=True)


def norm_kernel(inner_all, count, *refs):
    squares = refs[:count]
    x, gain = refs[count : count + 2]
    out = refs[-1]
    rows = out.shape[1]
    span = pl.ds(pl.multiple_of(pl.program_id(0) * rows, rows), rows)
    total = squares[0][:, span]
    for ref in squares[1:]:
        total = total + ref[:, span]
    inverse = lax.rsqrt(total / inner_all + EPS)
    columns = jnp.broadcast_to(inverse, (LANES, rows)).T
    gains = row(gain)
    for cut in pieces(out.shape[2], LANES):
        out[0, :, cut] = (x[span, cut] * columns * gains[:, cut]).astype(BF16)


def local(
    tokens,
    gate_weight,
    value_weight,
    state_weight,
    step_weight,
    value_kernel,
    value_offset,
    state_kernel,
    state_offset,
    step_offset,
    decay_rate,
    skip_gain,
    norm_gain,
):
    b, t, d = tokens.shape
    inner = gate_weight.shape[1]
    h = step_weight.shape[1]
    n = state_weight.shape[1] // 2
    head_width = inner // h
    peers = lax.axis_size("seq")
    ranks = lax.axis_size("head")
    owners = peers // 2
    share = n // owners
    chunks = t // CHUNK
    assert h <= SLOT and owners * 2 == peers and owners & (owners - 1) == 0
    assert b == 2 and chunks < 8 and value_kernel.shape[0] == 4
    lines = max(owners, 8)

    def swap(arrays):
        return [arrays[0]] + [
            here(lax.ppermute(arrays[k], "seq", [(s, s ^ k) for s in range(peers)]))
            for k in range(1, owners)
        ]

    halo = here(
        lax.ppermute(tokens[:, t - PAD :], "seq", [(s, s + 1) for s in range(peers - 1)])
    )
    outs = pl.pallas_call(
        functools.partial(front_kernel, head_width),
        in_specs=[FAR] * 6,
        out_specs=[WHOLE] * (3 + 7 * b),
        out_shape=[
            pltpu.VMEM(state_weight.shape, BF16),
            pltpu.VMEM(value_weight.shape, BF16),
            pltpu.VMEM((LANES, inner), BF16),
        ]
        + [
            pltpu.VMEM((t, d), BF16),
            pltpu.VMEM((t, 2 * n), BF16),
            pltpu.VMEM((t, LANES), BF16),
            pltpu.VMEM((16, LANES), BF16),
            pltpu.VMEM((t, LANES), F32),
            pltpu.VMEM((chunks, SLOT, CHUNK), F32),
            pltpu.VMEM((chunks, SLOT, CHUNK), F32),
        ]
        * b,
        scratch_shapes=[
            pltpu.VMEM((h, d), BF16),
            pltpu.VMEM((h,), F32),
            pltpu.VMEM((h,), F32),
            pltpu.VMEM((LANES, d), BF16),
            pltpu.VMEM((8, LANES), F32),
            pltpu.SemaphoreType.DMA((b + 5,)),
        ],
        compiler_params=params(16),
        name="front",
        cost_estimate=cost(2 * b * t * d * (2 * n + LANES)),
    )(*map(far, (tokens, state_weight, step_weight.T, value_weight, step_offset, decay_rate)))
    sw, w, sel = outs[:3]
    fronts = [outs[3 + 7 * i : 10 + 7 * i] for i in range(b)]

    wide = b * (inner + LANES)

    def values(i, ends):
        tok, io, close, thr, _, _, _ = fronts[i]
        loads = i == b - 1
        inputs = 12 + loads
        return pl.pallas_call(
            functools.partial(values_kernel, owners, "seq", i, b),
            in_specs=[WHOLE] * 12 + [FAR] * loads + [WHOLE] * len(ends),
            out_specs=[WHOLE] * (4 + loads + owners),
            out_shape=[
                pltpu.VMEM((t, inner), BF16),
                pltpu.VMEM((chunks - 1, n, inner), BF16),
                pltpu.VMEM((t, n), BF16),
                pltpu.VMEM((t, n), BF16),
            ]
            + [pltpu.VMEM(gate_weight.shape, BF16)] * loads
            + [pltpu.VMEM((share, wide), BF16)] * owners,
            scratch_shapes=[
                pltpu.SemaphoreType.DMA,
                pltpu.VMEM((n, t), BF16),
                pltpu.VMEM((t + PAD, 2 * n), F32),
                pltpu.VMEM((n, TILE), F32),
                pltpu.VMEM((t + PAD, TILE), F32),
                pltpu.VMEM((t + PAD, TILE), F32),
            ],
            input_output_aliases={inputs + k: 4 + loads + k for k in range(len(ends))},
            compiler_params=params(16),
            name=f"values{i}",
            cost_estimate=cost(2 * t * d * inner),
        )(
            tok, io, close, thr, halo, w, sw, value_kernel, value_offset,
            state_kernel, state_offset, sel, *[far(gate_weight)] * loads, *ends,
        )

    made, ends = [], ()
    for i in range(b):
        outs = values(i, ends)
        made.append(outs[:4])
        ends = outs[-owners:]
    gw = outs[4]

    def inside(i, runs, gw, made, prior, after):
        tok, _, _, thr, cum, cumt, dtt = fronts[i]
        vc, mid, b_rows, c_rows = made[:4]
        return pl.pallas_call(
            functools.partial(inside_kernel, head_width, owners, "seq", runs),
            in_specs=[WHOLE] * 11 + [SCALARS] + [WHOLE] * (len(prior) + len(after)),
            out_specs=[WHOLE] * 2,
            out_shape=[pltpu.VMEM((t, inner), F32), pltpu.VMEM((t, inner), BF16)],
            scratch_shapes=[
                pltpu.VMEM((chunks, CHUNK, CHUNK), F32),
                pltpu.VMEM((t, TILE), BF16),
                pltpu.VMEM((t, TILE), BF16),
            ],
            input_output_aliases={12 + k: k for k in range(len(prior))},
            compiler_params=params(16),
            name=f"inside{i}",
            cost_estimate=cost(2.5 * t * d * inner),
        )(
            tok, gw, b_rows, c_rows, vc, mid, dtt, cum, cumt, thr, sel, skip_gain,
            *prior, *after,
        )

    def total(i, came, after):
        return pl.pallas_call(
            functools.partial(total_kernel, owners, "seq", i, b),
            in_specs=[WHOLE] * (owners + 1 + len(after)),
            out_specs=[WHOLE] * 2,
            out_shape=[pltpu.VMEM((share, inner), BF16), pltpu.VMEM((lines, inner), F32)],
            scratch_shapes=[
                pltpu.VMEM((owners, share, inner), BF16),
                pltpu.VMEM((lines, LANES), F32),
            ],
            compiler_params=params(16),
            name=f"total{i}",
        )(*came, sel, *after)

    def prefix(i, came, decay, first, after):
        return pl.pallas_call(
            functools.partial(prefix_kernel, owners, "seq", i),
            in_specs=[WHOLE] * (owners + 2 + len(after)),
            out_specs=[WHOLE] * owners,
            out_shape=[pltpu.VMEM((share, inner), BF16)] * owners,
            scratch_shapes=[
                pltpu.VMEM((owners, share, inner), BF16),
                pltpu.VMEM((owners, share, inner), BF16),
            ],
            compiler_params=params(16),
            name=f"prefix{i}",
        )(*came, decay, first, *after)

    def across(x):
        return here(lax.ppermute(x, "seq", [(s, s + owners) for s in range(owners)]))

    def enter(i, part, grow, c_rows, states, after):
        x, sq = pl.pallas_call(
            functools.partial(enter_kernel, owners, "seq"),
            in_specs=[WHOLE] * (3 + owners + len(after)),
            out_specs=[WHOLE] * 2,
            out_shape=[pltpu.VMEM((t, inner), F32), pltpu.VMEM((1, t), F32)],
            scratch_shapes=[pltpu.VMEM((n, inner), BF16)],
            compiler_params=params(16),
            name=f"enter{i}",
        )(part, grow, c_rows, *states, *after)
        return x, [sq] + [
            here(lax.ppermute(sq, "head", [(s, (s + k) % ranks) for s in range(ranks)]))
            for k in range(1, ranks)
        ]

    def norm(i, x, squares, into):
        rows = min(t, 256)
        return pl.pallas_call(
            functools.partial(norm_kernel, inner * ranks, ranks),
            grid=(t // rows,),
            in_specs=[WHOLE] * (ranks + 2) + [FAR] * len(into),
            out_specs=pl.BlockSpec((1, rows, inner), lambda q: (i, q, 0)),
            out_shape=jax.ShapeDtypeStruct((b, t, inner), BF16),
            input_output_aliases={ranks + 2: 0} if into else {},
            compiler_params=params(16),
            name=f"norm{i}",
        )(*squares, x, norm_gain, *into)

    came = swap(ends)
    tiles = inner // TILE
    ahead = tiles - 1
    part0, grow0 = inside(0, ((0, tiles, None),), gw, made[0], (), ())
    early = inside(1, ((0, ahead, 0), (0, 1, 1)), gw, made[1], (), (grow0,))
    whole0, decay0 = total(0, came, (early[1],))
    first0 = across(whole0)
    middle = 2
    mixed = inside(1, ((1, middle, 1), (ahead, tiles, 0)), gw, made[1], early, (whole0,))
    whole1, decay1 = total(1, came, (mixed[1],))
    first1 = across(whole1)
    part1, grow1 = inside(1, ((middle, tiles, 1),), gw, made[1], mixed, (whole1,))
    sent0 = prefix(0, came, decay0, first0, (grow1,))
    back0 = swap(sent0)
    sent1 = prefix(1, came, decay1, first1, (sent0[1],))
    back1 = swap(sent1)
    x0, squares0 = enter(0, part0, grow0, made[0][3], back0, (sent1[1],))
    x1, squares1 = enter(1, part1, grow1, made[1][3], back1, (squares0[0],))
    out = norm(0, x0, squares0, ())
    return norm(1, x1, squares1, (out,))


def solution(mesh):
    return jax.shard_map(
        local,
        mesh=mesh,
        in_specs=(
            P(None, "seq", None),
            P(None, "head"),
            P(None, "head"),
            P(),
            P(None, "head"),
            P(None, "head"),
            P("head"),
            P(),
            P(),
            P("head"),
            P("head"),
            P("head"),
            P("head"),
        ),
        out_specs=P(None, "seq", "head"),
        check_vma=False,
    )
```

```python
import functools
import jax
import jax.numpy as jnp
from jax import lax
from jax.experimental import pallas as pl
from jax.experimental.pallas import tpu as pltpu
from jax.sharding import PartitionSpec as P

EPS = 1e-05
LOG2E = 1.4426950408889634
PAD = 16
CHUNK = 128
TILE = 256
LANES = 128
SLOT = 32
F32 = jnp.float32
BF16 = jnp.bfloat16
WHOLE = pl.BlockSpec(memory_space=pltpu.VMEM)
FAR = pl.BlockSpec(memory_space=pltpu.HBM)
SCALARS = pl.BlockSpec(memory_space=pltpu.SMEM)


def here(x):
    return pltpu.with_memory_space_constraint(x, pltpu.VMEM)


def far(x):
    return pltpu.with_memory_space_constraint(x, pltpu.HBM)


def params(mib):
    return pltpu.CompilerParams(vmem_limit_bytes=mib << 20)


def cost(flops):
    return pl.CostEstimate(flops=int(flops), transcendentals=0, bytes_accessed=0)


def mm(a, b):
    return jnp.dot(a, b, preferred_element_type=F32)


def mm_t(a, b):
    return lax.dot_general(a, b, (((1,), (1,)), ((), ())), preferred_element_type=F32)


def silu(x):
    half = 0.5 * x
    return half + half * jnp.tanh(half)


def row(ref):
    return ref[...].reshape(1, ref.shape[0])


def pieces(total, size=CHUNK):
    return [slice(k * size, (k + 1) * size) for k in range(total // size)]


def head_select(width, head_width, group):
    lane = lax.broadcasted_iota(jnp.int32, (LANES, width), 0) - 2 * SLOT * group
    col = lax.broadcasted_iota(jnp.int32, (LANES, width), 1)
    start = (lane & (SLOT - 1)) * head_width
    hit = (lane >= 0) & (lane < 2 * SLOT) & (col >= start) & (col < start + head_width)
    return jnp.where(hit, 1.0, 0.0).astype(BF16)


def conv_of(x, kernel, offset):
    back = pltpu.roll(x, 1, 0)
    near = offset + kernel[3:4] * x + kernel[2:3] * back
    deep = kernel[1:2] * x + kernel[0:1] * back
    return silu((near + pltpu.roll(deep, 2, 0))[PAD:]).astype(BF16)


def front_kernel(head_width, *refs):
    tok_in, sw_in, twt_in, w_in, toff_in, rate_in = refs[:6]
    batch = tok_in.shape[0]
    sw, w, sel = refs[6:9]
    per_batch = [refs[9 + 7 * i : 16 + 7 * i] for i in range(batch)]
    twt, toff, rate, tws, vec, sem = refs[9 + 7 * batch :]
    rows = tok_in.shape[1]
    heads = twt.shape[0]
    token_copies = [
        pltpu.make_async_copy(tok_in.at[i], per_batch[i][0], sem.at[i]) for i in range(batch)
    ]
    copies = [
        pltpu.make_async_copy(twt_in, twt, sem.at[batch]),
        pltpu.make_async_copy(toff_in, toff, sem.at[batch + 1]),
        pltpu.make_async_copy(rate_in, rate, sem.at[batch + 2]),
        pltpu.make_async_copy(sw_in, sw, sem.at[batch + 3]),
        pltpu.make_async_copy(w_in, w, sem.at[batch + 4]),
    ]
    for copy in copies[:3] + [token_copies[0], copies[3]] + token_copies[1:] + [copies[4]]:
        copy.start()
    sel[...] = head_select(sel.shape[1], head_width, 0)
    for copy in copies[:3]:
        copy.wait()
    tws[...] = jnp.zeros_like(tws)
    vec[...] = jnp.zeros_like(vec)
    for g in range(LANES // SLOT):
        tws[pl.ds(g * SLOT, heads), :] = twt[...]
        vec[pl.ds(0, 1), pl.ds(g * SLOT, heads)] = row(toff)
        vec[pl.ds(1, 1), pl.ds(g * SLOT, heads)] = row(rate)
    offset = vec[pl.ds(0, 1), :]
    scale = vec[pl.ds(1, 1), :] * (-LOG2E)
    r = lax.broadcasted_iota(jnp.int32, (CHUNK, CHUNK), 0)
    c = lax.broadcasted_iota(jnp.int32, (CHUNK, CHUNK), 1)
    tri = jnp.where(r >= c, 1.0, 0.0).astype(BF16)
    group = lax.broadcasted_iota(jnp.int32, (1, LANES), 1) // SLOT
    low_lane = (group & 1) == 1

    def parts(x):
        hi = x.astype(BF16).astype(F32)
        return jnp.where(low_lane, x - hi, hi).astype(BF16)

    for i in range(batch):
        tok, io_out, close_out, thr_out, cum_out, cumt_out, dtt_out = per_batch[i]
        token_copies[i].wait()
        if i == 0:
            copies[3].wait()
        x = tok[...]
        io_out[...] = mm(x, sw[...]).astype(BF16)
        z = mm_t(x, tws[...]) + offset
        dt = jnp.maximum(z, 0.0) + jnp.log1p(jnp.exp(-jnp.abs(z)))
        log_decay = dt * scale
        base = jnp.zeros((1, LANES), F32)
        lasts, bases = [], []
        for q, span in enumerate(pieces(rows)):
            part = log_decay[span]
            hi = part.astype(BF16)
            rest = part - hi.astype(F32)
            mid = rest.astype(BF16)
            low = (rest - mid.astype(F32)).astype(BF16)
            cum = mm(tri, hi) + (mm(tri, mid) + mm(tri, low))
            last = cum[CHUNK - 1 :]
            cum_out[span, :] = cum
            cumt_out[q] = cum.T[:SLOT]
            dtt_out[q] = dt[span].T[:SLOT]
            close_out[span, :] = parts(jnp.exp2(last - cum) * dt[span])
            lasts.append(last)
            bases.append(base)
            base = base + last
        zero = [jnp.zeros((1, LANES), F32)]
        table = lasts + [base] + zero * (7 - len(lasts)) + bases + zero * (8 - len(bases))
        thr_out[...] = parts(jnp.exp2(jnp.concatenate(table, axis=0)))
    copies[4].wait()


def values_kernel(owners, axis, index, batch, *refs):
    tok, io, close, thr, halo, w, sw, vkern, voff, skern, soff, sel = refs[:12]
    loads = index == batch - 1
    sem = refs[-6]
    bt, mbuf, hold, vb0, vb1 = refs[-5:]
    ends = refs[-6 - owners : -6]
    if loads:
        gate_in, gw = refs[12], refs[-7 - owners]
        copy = pltpu.make_async_copy(gate_in, gw, sem)
        copy.start()
    first = -6 - owners - loads - 4
    vc_out, mid_out, b_out, c_out = refs[first : first + 4]
    rows = tok.shape[0]
    inner = w.shape[1]
    n = sw.shape[1] // 2
    share = n // owners
    spot = lax.rem(lax.axis_index(axis), owners)
    tiles = pieces(inner, TILE)
    rim = halo[index]
    offset = row(voff)

    def project(j, buf):
        x = jnp.concatenate([rim, tok[...]], axis=0)
        buf[...] = mm(x, w[:, tiles[j]]).astype(BF16).astype(F32)

    def maps():
        mbuf[pl.ds(0, PAD), :] = mm(rim, sw[...]).astype(BF16).astype(F32)
        mbuf[pl.ds(PAD, rows), :] = io[...].astype(F32)
        y = conv_of(mbuf[...], skern[...], row(soff))
        b_out[...] = y[:, :n]
        c_out[...] = y[:, n:]
        bt[...] = y[:, :n].astype(F32).T.astype(BF16)

    def finish(j, buf):
        at = tiles[j]
        vc = conv_of(buf[...], vkern[:, at], offset[:, at])
        vc_out[:, at] = vc
        select = sel[:, at]
        through = mm(thr[...], select)
        state = None
        for q, span in enumerate(pieces(rows)):
            scaled = (vc[span].astype(F32) * mm(close[span, :], select)).astype(BF16)
            made = mm(bt[:, span], scaled)
            if q == 0:
                state = made
            else:
                mid_out[q - 1, :, at] = state.astype(BF16)
                state = state * through[q : q + 1] + made
        hold[...] = state
        for k in range(owners):
            owner = jnp.bitwise_xor(spot, k)
            part = hold[pl.ds(pl.multiple_of(owner * share, share), share), :]
            ends[k][:, index * inner + at.start : index * inner + at.stop] = part.astype(BF16)

    line = lax.broadcasted_iota(jnp.int32, (share, LANES), 0)
    count = rows // CHUNK
    mine = jnp.broadcast_to(thr[...].astype(F32)[count : count + 1], (share, LANES))
    decays = jnp.where(line == 0, mine, 0.0).astype(BF16)
    tail = batch * inner + index * LANES
    for k in range(owners):
        ends[k][:, tail : tail + LANES] = decays
    bufs = (vb0, vb1)
    for j in range(len(tiles)):
        project(j, bufs[j % 2])
        if j == 0:
            maps()
        else:
            finish(j - 1, bufs[(j - 1) % 2])
    finish(len(tiles) - 1, bufs[(len(tiles) - 1) % 2])
    if loads:
        copy.wait()


def inside_kernel(
    head_width, owners, axis, runs, tok, gw, b_rows, c_rows, vc, mid, dtt, cum, cumt, thr, sel, skip,
    *refs,
):
    part_out, grow_out, scores, gb0, gb1 = refs[-5:]
    rows, inner = vc.shape
    tiles = pieces(inner, TILE)
    spans = pieces(rows)
    r = lax.broadcasted_iota(jnp.int32, (CHUNK, CHUNK), 0)
    s = lax.broadcasted_iota(jnp.int32, (CHUNK, CHUNK), 1)
    wide = 2 * head_width
    assert wide == CHUNK
    lane = lax.broadcasted_iota(jnp.int32, (CHUNK, wide), 1)
    flat = lane[:1]

    def project(j, buf):
        buf[...] = mm(tok[...], gw[:, tiles[j]]).astype(BF16)

    def score():
        for q, span in enumerate(spans):
            scores[q] = jnp.where(r >= s, mm_t(c_rows[span, :], b_rows[span, :]), 0.0)

    def finish(j, buf):
        tile = tiles[j]
        base = mm(thr[...], sel[:, tile])
        for q, span in enumerate(spans):
            swish = silu(buf[span, :].astype(F32))
            if q > 0:
                carried = mm(c_rows[span, :], mid[q - 1, :, tile])
            for cut in pieces(TILE, wide):
                at = slice(tile.start + cut.start, tile.start + cut.stop)
                first = at.start // head_width
                block = vc[span, at]
                mixes, halves, columns = [], [], []
                for k in range(2):
                    head = first + k
                    column = jnp.broadcast_to(cum[span, head : head + 1], (CHUNK, CHUNK))
                    columns.append(column)
                    gap = jnp.minimum(column - cumt[q, head : head + 1, :], 0.0)
                    mixes.append(
                        (scores[q] * jnp.exp2(gap) * dtt[q, head : head + 1, :]).astype(BF16)
                    )
                    halves.append(
                        jnp.where((lane >= head_width) == (k == 1), block, jnp.zeros_like(block))
                    )
                mixture = mm(jnp.concatenate(mixes, axis=1), jnp.concatenate(halves, axis=0))
                gain = jnp.where(flat < head_width, skip[first], skip[first + 1])
                mixture = mixture + gain * block.astype(F32)
                rise = jnp.exp2(jnp.where(lane < head_width, columns[0], columns[1]))
                gated = swish[:, cut] * rise
                if q > 0:
                    mixture = mixture + carried[:, cut] * rise
                    gated = gated * base[8 + q : 9 + q, cut]
                grow_out[span, at] = gated.astype(BF16)
                part_out[span, at] = mixture * swish[:, cut]

    bufs = (gb0, gb1)

    def run(first, last):
        for j in range(first, last):
            project(j, bufs[j % 2])
            if j == first:
                score()
            else:
                finish(j - 1, bufs[(j - 1) % 2])
        finish(last - 1, bufs[(last - 1) % 2])

    for first, last, side in runs:
        if side is None:
            run(first, last)
        else:
            half = lax.axis_index(axis) // owners
            pl.when(half == side)(functools.partial(run, first, last))


def total_kernel(owners, axis, index, batch, *refs):
    came, sel = refs[:owners], refs[owners]
    total_out, decay_out, held, lines = refs[-4:]
    inner = sel.shape[1]
    at = slice(index * inner, (index + 1) * inner)
    tail = slice(batch * inner + index * LANES, batch * inner + (index + 1) * LANES)
    spot = lax.rem(lax.axis_index(axis), owners)
    lines[...] = jnp.zeros_like(lines)
    for k in range(owners):
        owner = jnp.bitwise_xor(spot, k)
        held[owner] = came[k][:, at]
        lines[pl.ds(owner, 1), :] = came[k][:, tail].astype(F32)[:1]
    decay_out[...] = mm(lines[...].astype(BF16), sel[...])
    state = held[0].astype(F32)
    for k in range(1, owners):
        state = state * decay_out[pl.ds(k, 1), :] + held[k].astype(F32)
    total_out[...] = state.astype(BF16)


def prefix_kernel(owners, axis, index, *refs):
    came = refs[:owners]
    decay, first = refs[owners : owners + 2]
    outs = refs[-owners - 2 : -2]
    held, made = refs[-2:]
    inner = decay.shape[1]
    at = slice(index * inner, (index + 1) * inner)
    spot = lax.rem(lax.axis_index(axis), owners)
    for k in range(owners):
        held[jnp.bitwise_xor(spot, k)] = came[k][:, at]
    state = first[...].astype(F32)
    for k in range(owners):
        made[k] = state.astype(BF16)
        if k + 1 < owners:
            state = state * decay[pl.ds(k, 1), :] + held[k].astype(F32)
    for k in range(owners):
        outs[k][...] = made[jnp.bitwise_xor(spot, k)]


def enter_kernel(owners, axis, part, grow, c_rows, *refs):
    came = refs[:owners]
    out, sq_out, state = refs[-3:]
    rows, inner = part.shape
    share = came[0].shape[0]
    spot = lax.rem(lax.axis_index(axis), owners)
    for k in range(owners):
        at = pl.multiple_of(jnp.bitwise_xor(spot, k) * share, share)
        state[pl.ds(at, share), :] = came[k][...]
    for span in pieces(rows):
        acc = jnp.zeros((CHUNK, LANES), F32)
        for at in pieces(inner, TILE):
            extra = mm(c_rows[span, :], state[:, at])
            total = part[span, at] + grow[span, at].astype(F32) * extra
            out[span, at] = total
            for cut in pieces(TILE, LANES):
                acc = acc + total[:, cut] * total[:, cut]
        sq_out[:, span] = jnp.sum(acc.T, axis=0, keepdims=True)


def norm_kernel(inner_all, count, *refs):
    squares = refs[:count]
    x, gain = refs[count : count + 2]
    out = refs[-1]
    rows = out.shape[1]
    span = pl.ds(pl.multiple_of(pl.program_id(0) * rows, rows), rows)
    total = squares[0][:, span]
    for ref in squares[1:]:
        total = total + ref[:, span]
    inverse = lax.rsqrt(total / inner_all + EPS)
    columns = jnp.broadcast_to(inverse, (LANES, rows)).T
    gains = row(gain)
    for cut in pieces(out.shape[2], LANES):
        out[0, :, cut] = (x[span, cut] * columns * gains[:, cut]).astype(BF16)


def local(
    tokens,
    gate_weight,
    value_weight,
    state_weight,
    step_weight,
    value_kernel,
    value_offset,
    state_kernel,
    state_offset,
    step_offset,
    decay_rate,
    skip_gain,
    norm_gain,
):
    b, t, d = tokens.shape
    inner = gate_weight.shape[1]
    h = step_weight.shape[1]
    n = state_weight.shape[1] // 2
    head_width = inner // h
    peers = lax.axis_size("seq")
    ranks = lax.axis_size("head")
    owners = peers // 2
    share = n // owners
    chunks = t // CHUNK
    assert h <= SLOT and owners * 2 == peers and owners & (owners - 1) == 0
    assert b == 2 and chunks < 8 and value_kernel.shape[0] == 4
    lines = max(owners, 8)

    def swap(arrays):
        return [arrays[0]] + [
            here(lax.ppermute(arrays[k], "seq", [(s, s ^ k) for s in range(peers)]))
            for k in range(1, owners)
        ]

    halo = here(
        lax.ppermute(tokens[:, t - PAD :], "seq", [(s, s + 1) for s in range(peers - 1)])
    )
    outs = pl.pallas_call(
        functools.partial(front_kernel, head_width),
        in_specs=[FAR] * 6,
        out_specs=[WHOLE] * (3 + 7 * b),
        out_shape=[
            pltpu.VMEM(state_weight.shape, BF16),
            pltpu.VMEM(value_weight.shape, BF16),
            pltpu.VMEM((LANES, inner), BF16),
        ]
        + [
            pltpu.VMEM((t, d), BF16),
            pltpu.VMEM((t, 2 * n), BF16),
            pltpu.VMEM((t, LANES), BF16),
            pltpu.VMEM((16, LANES), BF16),
            pltpu.VMEM((t, LANES), F32),
            pltpu.VMEM((chunks, SLOT, CHUNK), F32),
            pltpu.VMEM((chunks, SLOT, CHUNK), F32),
        ]
        * b,
        scratch_shapes=[
            pltpu.VMEM((h, d), BF16),
            pltpu.VMEM((h,), F32),
            pltpu.VMEM((h,), F32),
            pltpu.VMEM((LANES, d), BF16),
            pltpu.VMEM((8, LANES), F32),
            pltpu.SemaphoreType.DMA((b + 5,)),
        ],
        compiler_params=params(16),
        name="front",
        cost_estimate=cost(2 * b * t * d * (2 * n + LANES)),
    )(*map(far, (tokens, state_weight, step_weight.T, value_weight, step_offset, decay_rate)))
    sw, w, sel = outs[:3]
    fronts = [outs[3 + 7 * i : 10 + 7 * i] for i in range(b)]

    wide = b * (inner + LANES)

    def values(i, ends):
        tok, io, close, thr, _, _, _ = fronts[i]
        loads = i == b - 1
        inputs = 12 + loads
        return pl.pallas_call(
            functools.partial(values_kernel, owners, "seq", i, b),
            in_specs=[WHOLE] * 12 + [FAR] * loads + [WHOLE] * len(ends),
            out_specs=[WHOLE] * (4 + loads + owners),
            out_shape=[
                pltpu.VMEM((t, inner), BF16),
                pltpu.VMEM((chunks - 1, n, inner), BF16),
                pltpu.VMEM((t, n), BF16),
                pltpu.VMEM((t, n), BF16),
            ]
            + [pltpu.VMEM(gate_weight.shape, BF16)] * loads
            + [pltpu.VMEM((share, wide), BF16)] * owners,
            scratch_shapes=[
                pltpu.SemaphoreType.DMA,
                pltpu.VMEM((n, t), BF16),
                pltpu.VMEM((t + PAD, 2 * n), F32),
                pltpu.VMEM((n, TILE), F32),
                pltpu.VMEM((t + PAD, TILE), F32),
                pltpu.VMEM((t + PAD, TILE), F32),
            ],
            input_output_aliases={inputs + k: 4 + loads + k for k in range(len(ends))},
            compiler_params=params(16),
            name=f"values{i}",
            cost_estimate=cost(2 * t * d * inner),
        )(
            tok, io, close, thr, halo, w, sw, value_kernel, value_offset,
            state_kernel, state_offset, sel, *[far(gate_weight)] * loads, *ends,
        )

    made, ends = [], ()
    for i in range(b):
        outs = values(i, ends)
        made.append(outs[:4])
        ends = outs[-owners:]
    gw = outs[4]

    def inside(i, runs, gw, made, prior, after):
        tok, _, _, thr, cum, cumt, dtt = fronts[i]
        vc, mid, b_rows, c_rows = made[:4]
        return pl.pallas_call(
            functools.partial(inside_kernel, head_width, owners, "seq", runs),
            in_specs=[WHOLE] * 11 + [SCALARS] + [WHOLE] * (len(prior) + len(after)),
            out_specs=[WHOLE] * 2,
            out_shape=[pltpu.VMEM((t, inner), F32), pltpu.VMEM((t, inner), BF16)],
            scratch_shapes=[
                pltpu.VMEM((chunks, CHUNK, CHUNK), F32),
                pltpu.VMEM((t, TILE), BF16),
                pltpu.VMEM((t, TILE), BF16),
            ],
            input_output_aliases={12 + k: k for k in range(len(prior))},
            compiler_params=params(16),
            name=f"inside{i}",
            cost_estimate=cost(2.5 * t * d * inner),
        )(
            tok, gw, b_rows, c_rows, vc, mid, dtt, cum, cumt, thr, sel, skip_gain,
            *prior, *after,
        )

    def total(i, came, after):
        return pl.pallas_call(
            functools.partial(total_kernel, owners, "seq", i, b),
            in_specs=[WHOLE] * (owners + 1 + len(after)),
            out_specs=[WHOLE] * 2,
            out_shape=[pltpu.VMEM((share, inner), BF16), pltpu.VMEM((lines, inner), F32)],
            scratch_shapes=[
                pltpu.VMEM((owners, share, inner), BF16),
                pltpu.VMEM((lines, LANES), F32),
            ],
            compiler_params=params(16),
            name=f"total{i}",
        )(*came, sel, *after)

    def prefix(i, came, decay, first, after):
        return pl.pallas_call(
            functools.partial(prefix_kernel, owners, "seq", i),
            in_specs=[WHOLE] * (owners + 2 + len(after)),
            out_specs=[WHOLE] * owners,
            out_shape=[pltpu.VMEM((share, inner), BF16)] * owners,
            scratch_shapes=[
                pltpu.VMEM((owners, share, inner), BF16),
                pltpu.VMEM((owners, share, inner), BF16),
            ],
            compiler_params=params(16),
            name=f"prefix{i}",
        )(*came, decay, first, *after)

    def across(x):
        return here(lax.ppermute(x, "seq", [(s, s + owners) for s in range(owners)]))

    def enter(i, part, grow, c_rows, states, after):
        x, sq = pl.pallas_call(
            functools.partial(enter_kernel, owners, "seq"),
            in_specs=[WHOLE] * (3 + owners + len(after)),
            out_specs=[WHOLE] * 2,
            out_shape=[pltpu.VMEM((t, inner), F32), pltpu.VMEM((1, t), F32)],
            scratch_shapes=[pltpu.VMEM((n, inner), BF16)],
            compiler_params=params(16),
            name=f"enter{i}",
        )(part, grow, c_rows, *states, *after)
        return x, [sq] + [
            here(lax.ppermute(sq, "head", [(s, (s + k) % ranks) for s in range(ranks)]))
            for k in range(1, ranks)
        ]

    def norm(i, x, squares, into):
        rows = min(t, CHUNK)
        return pl.pallas_call(
            functools.partial(norm_kernel, inner * ranks, ranks),
            grid=(t // rows,),
            in_specs=[WHOLE] * (ranks + 2) + [FAR] * len(into),
            out_specs=pl.BlockSpec((1, rows, inner), lambda q: (i, q, 0)),
            out_shape=jax.ShapeDtypeStruct((b, t, inner), BF16),
            input_output_aliases={ranks + 2: 0} if into else {},
            compiler_params=params(16),
            name=f"norm{i}",
        )(*squares, x, norm_gain, *into)

    came = swap(ends)
    tiles = inner // TILE
    ahead = tiles - 1
    part0, grow0 = inside(0, ((0, tiles, None),), gw, made[0], (), ())
    early = inside(1, ((0, ahead, 0), (0, 1, 1)), gw, made[1], (), (grow0,))
    whole0, decay0 = total(0, came, (early[1],))
    first0 = across(whole0)
    whole1, decay1 = total(1, came, (whole0,))
    first1 = across(whole1)
    late = ((1, tiles, 1), (ahead, tiles, 0))
    part1, grow1 = inside(1, late, gw, made[1], early, (whole1,))
    sent0 = prefix(0, came, decay0, first0, (grow1,))
    back0 = swap(sent0)
    sent1 = prefix(1, came, decay1, first1, (sent0[1],))
    back1 = swap(sent1)
    x0, squares0 = enter(0, part0, grow0, made[0][3], back0, (sent1[1],))
    x1, squares1 = enter(1, part1, grow1, made[1][3], back1, (squares0[0],))
    out = norm(0, x0, squares0, ())
    return norm(1, x1, squares1, (out,))


def solution(mesh):
    return jax.shard_map(
        local,
        mesh=mesh,
        in_specs=(
            P(None, "seq", None),
            P(None, "head"),
            P(None, "head"),
            P(),
            P(None, "head"),
            P(None, "head"),
            P("head"),
            P(),
            P(),
            P("head"),
            P("head"),
            P("head"),
            P("head"),
        ),
        out_specs=P(None, "seq", "head"),
        check_vma=False,
    )
```
